32 devices in a mesh: dp: 4 (over x, core), fsdp: 8 (over z, y).
Axes of the slice: x: 2, y: 2, z: 4, core: 2. Of those that a mesh axis runs over, the one named last changes fastest.
Arguments:
- tokens_in: bfloat16 [2, 64, 384, 768], P(None, 'dp', 'fsdp'), may hold values from -6 to 6
- cotangent: bfloat16 [2, 64, 384, 768], P(None, 'dp', 'fsdp'), may hold values from -6 to 6
- lengths: int32 [2, 64], replicated, may hold values from 1 to 5, as said below
- bin_deal: int32 [2, 4, 16], replicated, may hold values from 0 to 15, as said below
- random_blocks: int32 [2, 64, 6, 3], replicated, may hold values from 0 to 5
- weight_qkv: bfloat16 [2, 768, 2304], P(None, ('dp', 'fsdp')), may hold values from -0.21875 to 0.21875
- bias_query: bfloat16 [2, 768], P(None, ('dp', 'fsdp')), may hold values from -2 to 2
- bias_value: bfloat16 [2, 768], P(None, ('dp', 'fsdp')), may hold values from -2 to 2
- weight_out: bfloat16 [2, 768, 768], P(None, ('dp', 'fsdp')), may hold values from -0.625 to 0.625
- bias_out: bfloat16 [2, 768], P(None, ('dp', 'fsdp')), may hold values from -2 to 2
- gain_attn: bfloat16 [2, 768], P(None, ('dp', 'fsdp')), may hold values from 0.5 to 1.5
- beta_attn: bfloat16 [2, 768], P(None, ('dp', 'fsdp')), may hold values from -2 to 2
- weight_up: bfloat16 [2, 768, 3072], P(None, ('dp', 'fsdp')), may hold values from -0.21875 to 0.21875
- bias_up: bfloat16 [2, 3072], P(None, ('dp', 'fsdp')), may hold values from -2 to 2
- weight_down: bfloat16 [2, 3072, 768], P(None, ('dp', 'fsdp')), may hold values from -0.109375 to 0.109375
- bias_down: bfloat16 [2, 768], P(None, ('dp', 'fsdp')), may hold values from -2 to 2
- gain_ffn: bfloat16 [2, 768], P(None, ('dp', 'fsdp')), may hold values from 0.5 to 1.5
- beta_ffn: bfloat16 [2, 768], P(None, ('dp', 'fsdp')), may hold values from -2 to 2
Outputs:
- output: bfloat16 [2, 64, 384, 768], P(None, 'dp', 'fsdp')
- input_grad: bfloat16 [2, 64, 384, 768], P(None, 'dp', 'fsdp')
- grad_weight_qkv: float32 [2, 768, 2304], P(None, ('dp', 'fsdp'))
- grad_bias_query: float32 [2, 768], P(None, ('dp', 'fsdp'))
- grad_bias_value: float32 [2, 768], P(None, ('dp', 'fsdp'))
- grad_weight_out: float32 [2, 768, 768], P(None, ('dp', 'fsdp'))
- grad_bias_out: float32 [2, 768], P(None, ('dp', 'fsdp'))
- grad_gain_attn: float32 [2, 768], P(None, ('dp', 'fsdp'))
- grad_beta_attn: float32 [2, 768], P(None, ('dp', 'fsdp'))
- grad_weight_up: float32 [2, 768, 3072], P(None, ('dp', 'fsdp'))
- grad_bias_up: float32 [2, 3072], P(None, ('dp', 'fsdp'))
- grad_weight_down: float32 [2, 3072, 768], P(None, ('dp', 'fsdp'))
- grad_bias_down: float32 [2, 768], P(None, ('dp', 'fsdp'))
- grad_gain_ffn: float32 [2, 768], P(None, ('dp', 'fsdp'))
- grad_beta_ffn: float32 [2, 768], P(None, ('dp', 'fsdp'))
The draws below stay inside these ranges and needn't reach their ends.
Inputs may be any that keep to these rules, and one draw needn't show every extreme that they name: lengths are counted in blocks of 64 positions; the two sequences dealt to one bin have 6 blocks or fewer together, and in every group of every micro-batch some bin holds exactly 6. For each micro-batch m and group g, bin_deal[m, g] names each of 0 to 15 once.
All inputs are finite; a program needn't handle non-finite values.
Results may differ from the reference program's by a relative error of at most 0.02.
Values may be sent and summed in bfloat16 or wider, within the bound.
A program may use at most 320 MiB of HBM per device.

```python
import jax
import jax.numpy as jnp
from jax import lax

D = 768
HEADS = 12
FF = 3072
HEAD_DIM = 64
BLOCK = 64
NBLK = 6
RAND = 3
LAYERS = 2
MB = 2
SLOTS = 16
SEQS = 64
BIN = 384


def bin_plan(key):
    base_key = jax.random.fold_in(key, 11)
    key_total, key_first, key_full, key_order = jax.random.split(base_key, 4)
    groups = SEQS // SLOTS
    members = SLOTS // 2
    bin_shape = (MB, groups, members)
    totals = jax.random.randint(key_total, bin_shape, NBLK // 2, NBLK + 1)
    full_at = jax.random.randint(key_full, (MB, groups, 1), 0, members)
    is_full = jnp.arange(members)[None, None, :] == full_at
    totals = jnp.where(is_full, NBLK, totals)
    first_len = jax.random.randint(key_first, bin_shape, 1, totals)
    first_len = jnp.where(is_full, NBLK - 1, first_len)
    second_len = totals - first_len
    slot_len = jnp.stack([first_len, second_len], axis=-1).reshape(MB, groups, SLOTS)
    order_scores = jax.random.randint(key_order, (MB, groups, SLOTS), 0, 2 ** 20) * SLOTS + jnp.arange(SLOTS)[None, None, :]
    bin_deal = jnp.argsort(order_scores, axis=-1).astype(jnp.int32)
    lengths = jnp.take_along_axis(slot_len, bin_deal, axis=-1).reshape(MB, SEQS).astype(jnp.int32)
    return (bin_deal, lengths)


def draw_bin_deal(key, part):
    return bin_plan(key)[0]


def draw_lengths(key, part):
    return bin_plan(key)[1]


def touch_ends(drawn, stream_key, least, top_value):
    longest = drawn.shape.index(max(drawn.shape))
    spots = []
    for shift in (0, 1):
        where = [jax.random.randint(jax.random.fold_in(stream_key, axis), (), 0, length) for axis, length in enumerate(drawn.shape)]
        where[longest] = (where[longest] + shift) % drawn.shape[longest]
        spots.append(tuple(where))
    return drawn.at[spots[0]].set(least).at[spots[1]].set(top_value)


def shard_levels(stream_key, extent, cuts, smallest, top_value):
    loudness, own = 1.0, jax.random.fold_in(stream_key, 6)
    for position, blocks in cuts:
        steps = jnp.exp(jax.random.uniform(jax.random.fold_in(own, position), (blocks,), jnp.float32, smallest / len(cuts), top_value / len(cuts)))
        loudness = loudness * jnp.repeat(steps, extent[position] // blocks).reshape([-1 if axis == position else 1 for axis in range(len(extent))])
    return loudness


def scatter_about(key, extent, scale, limit, cuts=(), kind=jnp.bfloat16):
    loudness = shard_levels(key, extent, cuts, -0.22, 0.18) if cuts else 1.0
    array = jax.random.normal(key, extent, jnp.float32) * scale * loudness
    return jnp.minimum(jnp.maximum(array, -limit), limit).astype(kind)


def setup_inputs(seed: int = 0) -> dict:
    key_of = jax.random.split(jax.random.key(seed), 19)
    return {
        "tokens_in": scatter_about(key_of[0], (MB, SEQS, BIN, D), 1.0, 6.0, ((1, 4), (2, 8))),
        "cotangent": scatter_about(key_of[1], (MB, SEQS, BIN, D), 1.0, 6.0, ((1, 4), (2, 8))),
        "lengths": draw_lengths(jax.random.fold_in(key_of[18], 71), 0),
        "bin_deal": draw_bin_deal(jax.random.fold_in(key_of[18], 71), 0),
        "random_blocks": touch_ends(jax.random.randint(key_of[4], (MB, SEQS, NBLK, RAND), 0, NBLK), jax.random.fold_in(key_of[4], 1), 0, NBLK - 1).astype(jnp.int32),
        "weight_qkv": scatter_about(key_of[5], (LAYERS, D, 3 * D), D ** -0.5, 0.21875, ((1, 32),)),
        "bias_query": scatter_about(key_of[6], (LAYERS, D), 0.3, 2.0, ((1, 32),)),
        "bias_value": scatter_about(key_of[7], (LAYERS, D), 0.3, 2.0, ((1, 32),)),
        "weight_out": scatter_about(key_of[8], (LAYERS, D, D), (D // 8) ** -0.5, 0.625, ((1, 32),)),
        "bias_out": scatter_about(key_of[9], (LAYERS, D), 0.3, 2.0, ((1, 32),)),
        "gain_attn": jnp.clip(1.0 + 0.1 * jax.random.normal(key_of[10], (LAYERS, D), jnp.float32), 0.5, 1.5).astype(jnp.bfloat16),
        "beta_attn": scatter_about(key_of[11], (LAYERS, D), 0.3, 2.0, ((1, 32),)),
        "weight_up": scatter_about(key_of[12], (LAYERS, D, FF), D ** -0.5, 0.21875, ((1, 32),)),
        "bias_up": scatter_about(key_of[13], (LAYERS, FF), 0.3, 2.0, ((1, 32),)),
        "weight_down": scatter_about(key_of[14], (LAYERS, FF, D), FF ** -0.5, 0.109375, ((1, 32),)),
        "bias_down": scatter_about(key_of[15], (LAYERS, D), 0.3, 2.0, ((1, 32),)),
        "gain_ffn": jnp.clip(1.0 + 0.1 * jax.random.normal(key_of[16], (LAYERS, D), jnp.float32), 0.5, 1.5).astype(jnp.bfloat16),
        "beta_ffn": scatter_about(key_of[17], (LAYERS, D), 0.3, 2.0, ((1, 32),)),
    }


epsilon = 1e-06
highest = lax.Precision.HIGHEST

@jax.custom_vjp
def low(v):
    return lax.optimization_barrier(v.astype(jnp.bfloat16)).astype(jnp.float32)

@jax.custom_vjp
def low_back(v):
    return v

def low_keep(v):
    return (low(v), None)

def low_pass(kept, grad):
    return (grad,)

def back_keep(v):
    return (v, None)

def back_low(kept, grad):
    return (low(grad),)
low.defvjp(low_keep, low_pass)
low_back.defvjp(back_keep, back_low)

def token_mask(blocks_live, random_row):
    row_ids = jnp.arange(NBLK)[:, None]
    col_ids = jnp.arange(NBLK)[None, :]
    nearby = jnp.abs(row_ids - col_ids) <= 1
    global_hit = (col_ids == 0) | (col_ids == blocks_live - 1) | (row_ids == 0) | (row_ids == blocks_live - 1)
    picked = jnp.remainder(random_row, blocks_live)
    random_hit = jnp.any(picked[:, :, None] == jnp.arange(NBLK)[None, None, :], axis=1)
    allowed = (nearby | global_hit | random_hit) & (col_ids < blocks_live)
    return jnp.repeat(jnp.repeat(allowed, BLOCK, axis=0), BLOCK, axis=1)

def layer_norm(residual):
    center = residual - lax.optimization_barrier(jnp.mean(residual, axis=-1, keepdims=True))
    inv_std = lax.rsqrt(lax.optimization_barrier(jnp.mean(center * center, axis=-1, keepdims=True)) + epsilon)
    return center * inv_std

def gelu_tanh(values_in):
    return jax.nn.gelu(values_in, approximate=True)

def layer_forward(hidden, params, layer_at, allowed):
    weight_qkv, bias_query, bias_value, weight_out, bias_out, gain_attn, beta_attn, weight_up, bias_up, weight_down, bias_down, gain_ffn, beta_ffn = params
    seq_len = hidden.shape[0]
    score_scale = HEAD_DIM ** (-0.5)
    act_in = low(hidden)
    qkv_raw = low_back(jnp.dot(act_in, weight_qkv[layer_at], precision=highest))
    queries = low(qkv_raw[:, :D] + bias_query[layer_at]).reshape(seq_len, HEADS, HEAD_DIM)
    key_rows = low(qkv_raw[:, D:2 * D]).reshape(seq_len, HEADS, HEAD_DIM)
    value_rows = low(qkv_raw[:, 2 * D:] + bias_value[layer_at]).reshape(seq_len, HEADS, HEAD_DIM)
    scores = jnp.einsum('qhd,khd->hqk', queries, key_rows, precision=highest) * score_scale
    scores = low_back(jnp.where(allowed[None], scores, -1000000000.0))
    top_score = lax.optimization_barrier(jnp.max(scores, axis=-1, keepdims=True))
    exp_scores = jnp.exp(scores - top_score)
    soft_weights = exp_scores / lax.optimization_barrier(jnp.sum(exp_scores, axis=-1, keepdims=True))
    mixed_rows = jnp.einsum('hqk,khd->qhd', low(soft_weights), value_rows, precision=highest)
    context = low(low_back(mixed_rows.reshape(seq_len, D)))
    attn_out = low_back(jnp.dot(context, weight_out[layer_at], precision=highest)) + bias_out[layer_at]
    middle = layer_norm(hidden + attn_out) * gain_attn[layer_at] + beta_attn[layer_at]
    act_mid = low(middle)
    up_pre = low_back(jnp.dot(act_mid, weight_up[layer_at], precision=highest)) + bias_up[layer_at]
    act_up = low(gelu_tanh(up_pre))
    down_out = low_back(jnp.dot(act_up, weight_down[layer_at], precision=highest)) + bias_down[layer_at]
    return layer_norm(middle + down_out) * gain_ffn[layer_at] + beta_ffn[layer_at]

def sequence_forward(seq_tokens, blocks_live, random_row, params):
    allowed = token_mask(blocks_live, random_row)
    live_rows = (jnp.arange(BIN) < blocks_live * BLOCK).astype(jnp.float32)[:, None]
    hidden = seq_tokens
    for layer_at in range(LAYERS):
        hidden = layer_forward(hidden, params, layer_at, allowed)
    return hidden * live_rows

def reference(tokens_in, cotangent, lengths, bin_deal, random_blocks, weight_qkv, bias_query, bias_value, weight_out, bias_out, gain_attn, beta_attn, weight_up, bias_up, weight_down, bias_down, gain_ffn, beta_ffn):
    params = tuple((item.astype(jnp.float32) for item in (weight_qkv, bias_query, bias_value, weight_out, bias_out, gain_attn, beta_attn, weight_up, bias_up, weight_down, bias_down, gain_ffn, beta_ffn)))
    seq_count = MB * SEQS
    groups = SEQS // SLOTS
    flat_tokens = tokens_in.astype(jnp.float32).reshape(seq_count, BIN, D)
    flat_lengths = lengths.reshape(seq_count)
    rand_by_slot = random_blocks.reshape(MB, groups, SLOTS, NBLK, RAND)
    given_rand = jnp.take_along_axis(rand_by_slot, bin_deal[:, :, :, None, None].astype(jnp.int32), axis=2)
    flat_random = given_rand.reshape(seq_count, NBLK, RAND)
    step_fn = jax.checkpoint(sequence_forward)

    def forward(all_tokens, all_params):

        def scan_step(state_carry, seq_items):
            seq_tokens, blocks_live, random_row = seq_items
            return (state_carry, step_fn(seq_tokens, blocks_live, random_row, all_params))
        unused, results = lax.scan(scan_step, jnp.zeros((), jnp.float32), (all_tokens, flat_lengths, flat_random))
        return results
    results, pull_back = jax.vjp(forward, flat_tokens, params)
    grad_tokens, grad_params = pull_back(cotangent.astype(jnp.float32).reshape(seq_count, BIN, D))
    output = results.astype(jnp.bfloat16).reshape(MB, SEQS, BIN, D)
    input_grad = grad_tokens.astype(jnp.bfloat16).reshape(MB, SEQS, BIN, D)
    return (output, input_grad, grad_params[0], grad_params[1], grad_params[2], grad_params[3], grad_params[4], grad_params[5], grad_params[6], grad_params[7], grad_params[8], grad_params[9], grad_params[10], grad_params[11], grad_params[12])
```

```python
import jax
import jax.numpy as jnp
from jax import lax
from jax.experimental import pallas as pl
from jax.experimental.pallas import tpu as pltpu
from jax.sharding import PartitionSpec as P

HEADS = 12
BLOCK = 64
NBLK = 6
LAYERS = 2
CORES = 2
AXES = ("dp", "fsdp")
NEG = -1000000000.0
HEAD_DIM = 64


epsilon = 1e-06


def split_fsdp(count):
    inner = 1
    while (2 * inner) ** 2 <= count:
        inner *= 2
    return (count // inner, inner)


class Grid:
    def __init__(self, dp_count, fsdp_count):
        outer, inner = split_fsdp(fsdp_count)
        self.sizes = (dp_count // CORES, CORES, outer, inner)
        dp_at, fsdp_at = lax.axis_index("dp"), lax.axis_index("fsdp")
        self.at = (dp_at // CORES, dp_at % CORES, fsdp_at // inner, fsdp_at % inner)

        self.count = dp_count * fsdp_count

    def index(self, place):
        total = 0
        for size, at in zip(self.sizes, place):
            total = total * size + at
        return total

    def send(self, array, axis, offset):
        pairs = []
        sizes = self.sizes
        for flat in range(sizes[0] * sizes[1] * sizes[2] * sizes[3]):
            place, rest = [], flat
            for size in reversed(sizes):
                place.insert(0, rest % size)
                rest //= size
            place[axis] = (place[axis] + offset) % sizes[axis]
            pairs.append((flat, self.index(place)))
        return lax.ppermute(array, AXES, pairs)


ALL = slice(None)
HBM = pl.BlockSpec(memory_space=pl.ANY)


class Links:
    def __init__(self, sizes, send_sem, recv_sem):
        outer, inner = sizes[2:]
        dp_at, fsdp_at = lax.axis_index("dp"), lax.axis_index("fsdp")
        self.sizes = sizes
        self.at = (dp_at // CORES, dp_at % CORES, fsdp_at // inner, fsdp_at % inner)
        self.send_sem, self.recv_sem = send_sem, recv_sem
        self.used = 0

    def device(self, place):
        return (place[0] * CORES + place[1], place[2] * self.sizes[3] + place[3])

    def along(self, axis, offset):
        place = list(self.at)
        place[axis] = (place[axis] + offset) % self.sizes[axis]
        return self.device(place)

    def start(self, source, target, device):
        copy = pltpu.make_async_remote_copy(
            src_ref=source,
            dst_ref=target,
            send_sem=self.send_sem.at[self.used],
            recv_sem=self.recv_sem.at[self.used],
            device_id=device,
            device_id_type=pl.DeviceIdType.MESH,
        )
        self.used += 1
        copy.start()
        return copy

    def start_here(self, source, target):
        copy = pltpu.make_async_copy(source, target, self.recv_sem.at[self.used])
        self.used += 1
        copy.start()
        return copy

    def greet(self, devices):
        barrier = pltpu.get_barrier_semaphore()
        for device in devices:
            pl.semaphore_signal(barrier, inc=1, device_id=device, device_id_type=pl.DeviceIdType.MESH)
        pl.semaphore_wait(barrier, len(devices))

    def partners(self):
        found = [self.along(axis, k) for axis in (0, 1) for k in range(1, self.sizes[axis])]
        count = self.sizes[2] * self.sizes[3]
        return found + [self.member(k) for k in range(1, count)]

    def member(self, offset):
        count = self.sizes[2] * self.sizes[3]
        flat = self.at[2] * self.sizes[3] + self.at[3]
        return (self.at[0] * CORES + self.at[1], (flat + offset) % count)


class Gather:
    def __init__(self, links, source, target, order):
        self.links, self.source, self.target, self.order = links, source, target, order
        self.sent = []
        self.across = []

    def begin(self):
        links = self.links
        spot = self.target(*links.at)
        self.own = links.start_here(self.source, spot)
        self.column = [
            links.start(self.source, spot, links.along(2, k)) for k in range(1, links.sizes[2])
        ]

    def hand_over(self, spot):
        self.across.append(self.links.start(spot, spot, self.links.along(1, 1)))

    def first(self):
        links = self.links
        x, c, o, i = links.at
        self.own.wait()
        for copy in self.column:
            copy.wait_recv()
        spot = self.target(x, c, ALL, i)
        axis = self.order[0]
        self.line = [
            links.start(spot, spot, links.along(axis, k)) for k in range(1, links.sizes[axis])
        ]
        self.hand_over(spot)

    def second(self):
        links = self.links
        x, c, o, i = links.at
        for copy in self.line:
            copy.wait_recv()
        first, second = self.order
        spot = self.target(ALL, c, ALL, i) if first == 0 else self.target(x, c, ALL, ALL)
        self.sheet = [
            links.start(spot, spot, links.along(second, k)) for k in range(1, links.sizes[second])
        ]
        for k in range(1, links.sizes[first]):
            near = (links.at[first] - k) % links.sizes[first]
            self.hand_over(
                self.target(near, c, ALL, i) if first == 0 else self.target(x, c, ALL, near)
            )

    def third(self):
        links = self.links
        c = links.at[1]
        second = self.order[1]
        for k, copy in enumerate(self.sheet, 1):
            copy.wait_recv()
            near = (links.at[second] - k) % links.sizes[second]
            self.hand_over(
                self.target(near, c, ALL, ALL) if second == 0 else self.target(ALL, c, ALL, near)
            )

    def end(self):
        for copy in self.across:
            copy.wait()
        for copy in self.column + self.line + self.sheet:
            copy.wait_send()


def deal_out(links, source, target):
    count = links.sizes[2] * links.sizes[3]
    me = links.at[2] * links.sizes[3] + links.at[3]
    spot = target.at[:, :, me]
    copies = [links.start_here(source.at[:, me], spot)]
    for k in range(1, count):
        copies.append(links.start(source.at[:, (me + k) % count], spot, links.member(k)))
    return copies


def deal_back(links, source, target):
    count = links.sizes[2] * links.sizes[3]
    me = links.at[2] * links.sizes[3] + links.at[3]
    spot = target.at[:, me]
    copies = [links.start_here(source.at[:, :, me], spot)]
    for k in range(1, count):
        copies.append(links.start(source.at[:, :, (me + k) % count], spot, links.member(k)))
    return copies


def gathers_of(links, layer_at, square, down, small, all_square, all_down, all_small):
    def of_square(start, order):
        blocks = slice(start, start + 2)
        return Gather(
            links,
            square.at[layer_at, blocks],
            lambda *place: all_square.at[(layer_at, blocks) + place],
            order,
        )

    def of_down(start, order):
        blocks = slice(start, start + 2)
        return Gather(
            links,
            down.at[layer_at, blocks],
            lambda *place: all_down.at[(layer_at,) + place + (blocks,)],
            order,
        )

    tiny = Gather(
        links, small.at[layer_at], lambda *place: all_small.at[(layer_at,) + place], (0, 3)
    )
    return [
        [tiny, of_square(0, (0, 3)), of_square(2, (3, 0))],
        [of_square(4, (0, 3)), of_square(6, (3, 0))],
        [of_down(0, (0, 3)), of_down(2, (3, 0))],
    ]


def bring_kernel(sizes, *refs):
    sent_x, sent_grad, square, down, small = refs[:5]
    got_x, got_grad, all_square, all_down, all_small = refs[5:10]
    links = Links(sizes, *refs[10:])
    links.greet(links.partners())
    groups = []
    for layer_at in range(LAYERS):
        groups += gathers_of(
            links, layer_at, square, down, small, all_square, all_down, all_small
        )
    for at, group in enumerate(groups):
        for item in group:
            item.begin()
        if at == 2:
            moved = deal_out(links, sent_x, got_x)
    moved += deal_out(links, sent_grad, got_grad)
    for at in range(len(groups) + 1):
        if at > 0:
            for item in groups[at - 1]:
                item.second()
        if at < len(groups):
            for item in groups[at]:
                item.first()
        if at > 1:
            for item in groups[at - 2]:
                item.third()
    for item in groups[-1]:
        item.third()
    for group in groups:
        for item in group:
            item.end()
    for copy in moved:
        copy.wait()


def bring(sizes, sent_x, sent_grad, square, down, small):
    low = jnp.bfloat16
    batch, members, two, rows, width = sent_x.shape
    r = square.shape[2]
    got = jax.ShapeDtypeStruct((batch, two, members, rows, width), low)
    outs = [
        got,
        got,
        jax.ShapeDtypeStruct((LAYERS, square.shape[1]) + sizes + (r, width), low),
        jax.ShapeDtypeStruct((LAYERS,) + sizes + (down.shape[1], r, width), low),
        jax.ShapeDtypeStruct((LAYERS,) + sizes + (8, width), low),
    ]
    per_item = 1 + sum(n - 1 for n in sizes) + 4 + sizes[0] + sizes[3]
    count = 7 * LAYERS * per_item + 2 * members
    return pl.pallas_call(
        lambda *refs: bring_kernel(sizes, *refs),
        out_shape=outs,
        in_specs=[HBM] * 5,
        out_specs=[HBM] * 5,
        scratch_shapes=[pltpu.SemaphoreType.DMA((count,)), pltpu.SemaphoreType.DMA((count,))],
        compiler_params=pltpu.CompilerParams(collective_id=0, has_side_effects=True),
        name="bring",
    )(sent_x, sent_grad, square, down, small)


def pick(array, at, axis):
    return lax.dynamic_index_in_dim(array, at, axis, keepdims=False)


def gather_rows(grid, rows):
    count, width = rows.shape
    half = width // 2
    xs, cs, outs, ins = grid.sizes
    x, c, o, i = grid.at
    column = jnp.zeros((outs, count, width), rows.dtype)
    for step in range(outs):
        piece = rows if step == 0 else grid.send(rows, 2, step)
        column = lax.dynamic_update_slice(column, piece[None], ((o - step) % outs, 0, 0))
    pieces = {}
    for side, (first, second) in enumerate(((0, 3), (3, 0))):
        start = column[:, :, side * half : (side + 1) * half]
        line = [start] + [grid.send(start, first, k) for k in range(1, grid.sizes[first])]
        for far, piece in enumerate(line):
            for near in range(grid.sizes[second]):
                moved = piece if near == 0 else grid.send(piece, second, near)
                kx, ki = (far, near) if first == 0 else (near, far)
                pieces[side, kx, ki, 0] = moved
    for (side, kx, ki, unused), piece in list(pieces.items()):
        pieces[side, kx, ki, 1] = grid.send(piece, 1, 1)
    whole = jnp.zeros((xs, cs, outs, ins, count, width), rows.dtype)
    for (side, kx, ki, kc), piece in pieces.items():
        place = ((x - kx) % xs, (c - kc) % cs, 0, (i - ki) % ins, 0, side * half)
        whole = lax.dynamic_update_slice(whole, piece[None, None, :, None], place)
    return whole


def scatter_rows(grid, whole):
    width = whole.shape[-1]
    half = width // 2
    low = whole.dtype
    x, c, o, i = grid.at
    here = pick(whole, c, 1).astype(jnp.float32)
    there = grid.send(pick(whole, 1 - c, 1), 1, 1).astype(jnp.float32)
    both = (here + there).astype(low)
    sides = []
    for side, order in enumerate(((3, 0), (0, 3))):
        part = both[..., side * half : (side + 1) * half]
        left = [0, 2, 3]
        for axis in order + (2,):
            at = left.index(axis)
            left.remove(axis)
            mine = grid.at[axis]
            size = grid.sizes[axis]
            total = pick(part, mine, at).astype(jnp.float32)
            for k in range(1, size):
                total = total + grid.send(pick(part, (mine + k) % size, at), axis, k).astype(jnp.float32)
            part = total if axis == 2 else total.astype(low)
        sides.append(part)
    return jnp.concatenate(sides, axis=-1)


def bin_mask(first_blocks, second_blocks, random_pair):
    block_ids = jnp.arange(NBLK)
    later_seg = block_ids >= first_blocks
    rel_block = jnp.where(later_seg, block_ids - first_blocks, block_ids)
    seg_len = jnp.where(later_seg, second_blocks, first_blocks)
    live_block = block_ids < first_blocks + second_blocks
    rand_rows = jnp.where(
        later_seg[:, None],
        jnp.take(random_pair[1], rel_block, axis=0),
        jnp.take(random_pair[0], rel_block, axis=0),
    )
    picked = jnp.remainder(rand_rows, seg_len[:, None])
    row_rel = rel_block[:, None]
    col_rel = rel_block[None, :]
    row_len = seg_len[:, None]
    nearby = jnp.abs(row_rel - col_rel) <= 1
    global_hit = (
        (col_rel == 0) | (col_rel == row_len - 1) | (row_rel == 0) | (row_rel == row_len - 1)
    )
    random_hit = jnp.any(picked[:, :, None] == rel_block[None, None, :], axis=1)
    same_seg = (
        (later_seg[:, None] == later_seg[None, :]) & live_block[:, None] & live_block[None, :]
    )
    allowed = (nearby | global_hit | random_hit) & same_seg
    return jnp.repeat(jnp.repeat(allowed, BLOCK, axis=0), BLOCK, axis=1)


def dot(left, right):
    return jnp.dot(left, right, preferred_element_type=jnp.float32)


def dot_back(left, right):
    return lax.dot_general(left, right, (((1,), (1,)), ((), ())), preferred_element_type=jnp.float32)


def dot_weight(left, right):
    return lax.dot_general(left, right, (((0,), (0,)), ((), ())), preferred_element_type=jnp.float32)


LOW = jnp.bfloat16
LANES = 128
BQ, BV, BO, GA, BA, BD, GF, BF, BU = range(9)


def layer_norm(residual):
    center = residual - jnp.mean(residual, axis=-1, keepdims=True)
    inv_std = lax.rsqrt(jnp.mean(center * center, axis=-1, keepdims=True) + epsilon)
    return (center * inv_std, inv_std)


def norm_back(grad_out, normed, inv_std, gain):
    scaled = grad_out * gain
    return inv_std * (
        scaled
        - jnp.mean(scaled, axis=-1, keepdims=True)
        - normed * jnp.mean(scaled * normed, axis=-1, keepdims=True)
    )


def gelu_parts(u):
    root = 0.7978845608028654
    t = jnp.tanh(root * (u + 0.044715 * (u * u * u)))
    half = 0.5 * (1.0 + t)
    slope = half + 0.5 * u * (1.0 - t * t) * (root * (1.0 + 3 * 0.044715 * (u * u)))
    return (u * half, slope)


def lanes_of(pair, head):
    return pair[:, head * HEAD_DIM : (head + 1) * HEAD_DIM]


def pair_at(pair, offset=0):
    return pl.ds(pl.multiple_of(offset + pair * 2 * HEAD_DIM, 2 * HEAD_DIM), 2 * HEAD_DIM)


def lane_ids(rows):
    return lax.broadcasted_iota(jnp.int32, (rows, LANES), 1)


def attn_fwd_kernel(x_ref, w_ref, v_ref, mask_ref, qkv_ref, ctx_ref, stat_ref, normed_ref):
    rows, width = x_ref.shape
    act = x_ref[...].astype(LOW)
    for j, bias in enumerate((BQ, None, BV)):
        out = dot(act, w_ref[0, j])
        if bias is not None:
            out = out + v_ref[0, bias : bias + 1, :]
        qkv_ref[:, j * width : (j + 1) * width] = out.astype(LOW)
    scale = HEAD_DIM ** (-0.5)
    lanes = lane_ids(rows)
    stat_ref[...] = jnp.zeros_like(stat_ref)

    def pair_step(pair, carry):
        q = qkv_ref[:, pair_at(pair)]
        k = qkv_ref[:, pair_at(pair, width)]
        v = qkv_ref[:, pair_at(pair, 2 * width)]
        mixed = []
        for head in range(2):
            s = dot_back(lanes_of(q, head), lanes_of(k, head)) * scale
            s = jnp.where(mask_ref[0] > 0, s, NEG)
            top = jnp.max(s, axis=-1, keepdims=True)
            e = jnp.exp(s - top)
            total = jnp.sum(e, axis=-1, keepdims=True)
            mixed.append(dot(e.astype(LOW), lanes_of(v, head)) / total)
            log_total = top + jnp.log(total)
            stat_ref[...] = jnp.where(lanes == 2 * pair + head, log_total, stat_ref[...])
        ctx_ref[:, pair_at(pair)] = jnp.concatenate(mixed, axis=1).astype(LOW)
        return carry

    lax.fori_loop(0, HEADS // 2, pair_step, 0)
    resid = x_ref[...].astype(jnp.float32) + dot(ctx_ref[...], w_ref[0, 3])
    normed, inv = layer_norm(resid + v_ref[0, BO : BO + 1, :])
    normed_ref[...] = normed
    stat_ref[...] = jnp.where(lanes == HEADS, inv, stat_ref[...])


def attn_fwd(x, square, vectors, mask, layer_at):
    rows, width = x.shape
    bins, block = mask.shape[:2]
    row = lambda n: pl.BlockSpec((block, n), lambda b: (b, 0))
    f32 = jnp.float32
    return pl.pallas_call(
        attn_fwd_kernel,
        grid=(bins,),
        in_specs=[
            row(width),
            pl.BlockSpec((1, 4, width, width), lambda b: (layer_at, 0, 0, 0)),
            pl.BlockSpec((1,) + vectors.shape[1:], lambda b: (layer_at, 0, 0)),
            pl.BlockSpec((1, block, block), lambda b: (b, 0, 0)),
        ],
        out_specs=[row(3 * width), row(width), row(LANES), row(width)],
        out_shape=[
            jax.ShapeDtypeStruct((rows, 3 * width), LOW),
            jax.ShapeDtypeStruct((rows, width), LOW),
            jax.ShapeDtypeStruct((rows, LANES), f32),
            jax.ShapeDtypeStruct((rows, width), f32),
        ],
        name="attn_fwd",
    )(x, square, vectors, mask)


def middle_of(normed_ref, v_ref):
    return normed_ref[...] * v_ref[0, GA : GA + 1, :] + v_ref[0, BA : BA + 1, :]


def bias_up_of(v_ref, at, count):
    picked = v_ref[0, BU : BU + 1, :]
    for j in range(1, count):
        picked = jnp.where(at == j, v_ref[0, BU + j : BU + j + 1, :], picked)
    return picked


def mlp_fwd_kernel(
    count, normed_ref, wu_ref, wd_ref, v_ref, up_ref, out_ref, low_ref, fnorm_ref, stat_ref, mid, acc
):
    at = pl.program_id(0)

    @pl.when(at == 0)
    def _():
        mid[...] = middle_of(normed_ref, v_ref).astype(LOW)
        acc[...] = jnp.zeros_like(acc)

    up = dot(mid[...], wu_ref[0, 0]) + bias_up_of(v_ref, at, count)
    up_ref[...] = up
    acc[...] += dot(gelu_parts(up)[0].astype(LOW), wd_ref[0])

    @pl.when(at == count - 1)
    def _():
        resid = middle_of(normed_ref, v_ref) + acc[...] + v_ref[0, BD : BD + 1, :]
        normed, inv = layer_norm(resid)
        fnorm_ref[...] = normed
        stat_ref[...] = jnp.broadcast_to(inv, stat_ref.shape)
        out = normed * v_ref[0, GF : GF + 1, :] + v_ref[0, BF : BF + 1, :]
        out_ref[...] = out
        low_ref[...] = out.astype(LOW)


def mlp_fwd(normed, square, down, vectors, layer_at):
    rows, width = normed.shape
    count = down.shape[1] // width
    whole = lambda n: pl.BlockSpec((rows, n), lambda j: (0, 0))
    f32 = jnp.float32
    return pl.pallas_call(
        lambda *refs: mlp_fwd_kernel(count, *refs),
        grid=(count,),
        in_specs=[
            whole(width),
            pl.BlockSpec((1, 1, width, width), lambda j: (layer_at, 4 + j, 0, 0)),
            pl.BlockSpec((1, width, width), lambda j: (layer_at, j, 0)),
            pl.BlockSpec((1,) + vectors.shape[1:], lambda j: (layer_at, 0, 0)),
        ],
        out_specs=[
            pl.BlockSpec((rows, width), lambda j: (0, j)),
            whole(width),
            whole(width),
            whole(width),
            whole(LANES),
        ],
        out_shape=[
            jax.ShapeDtypeStruct((rows, count * width), f32),
            jax.ShapeDtypeStruct((rows, width), f32),
            jax.ShapeDtypeStruct((rows, width), LOW),
            jax.ShapeDtypeStruct((rows, width), f32),
            jax.ShapeDtypeStruct((rows, LANES), f32),
        ],
        scratch_shapes=[pltpu.VMEM((rows, width), LOW), pltpu.VMEM((rows, width), f32)],
        name="mlp_fwd",
    )(normed, square, down, vectors)


def sum_rows(values):
    return jnp.sum(values, axis=0, keepdims=True)


def mlp_bwd_kernel(
    count,
    grad_ref,
    fnorm_ref,
    fstat_ref,
    normed_ref,
    stat_ref,
    up_ref,
    wu_ref,
    wd_ref,
    v_ref,
    dwu_ref,
    dwd_ref,
    grad_a_ref,
    vec_ref,
    mid,
    grad_f,
    low_f,
    acc,
):
    at = pl.program_id(0)

    @pl.when(at == 0)
    def _():
        grad_out, normed = grad_ref[...].astype(jnp.float32), fnorm_ref[...]
        vec_ref[...] = jnp.zeros_like(vec_ref)
        vec_ref[GF : GF + 1, :] = sum_rows(grad_out * normed)
        vec_ref[BF : BF + 1, :] = sum_rows(grad_out)
        grad = norm_back(grad_out, normed, fstat_ref[:, :1], v_ref[0, GF : GF + 1, :])
        vec_ref[BD : BD + 1, :] = sum_rows(grad)
        grad_f[...] = grad
        low_f[...] = grad.astype(LOW)
        mid[...] = middle_of(normed_ref, v_ref).astype(LOW)
        acc[...] = jnp.zeros_like(acc)

    act, slope = gelu_parts(up_ref[...])
    dwd_ref[...] = dot_weight(act.astype(LOW), low_f[...]).astype(LOW)
    grad_up = dot_back(low_f[...], wd_ref[0]) * slope
    vec_ref[pl.ds(BU + at, 1), :] = sum_rows(grad_up)
    low_up = grad_up.astype(LOW)
    dwu_ref[0] = dot_weight(mid[...], low_up).astype(LOW)
    acc[...] += dot_back(low_up, wu_ref[0, 0])

    @pl.when(at == count - 1)
    def _():
        grad_mid, normed = grad_f[...] + acc[...], normed_ref[...]
        vec_ref[GA : GA + 1, :] = sum_rows(grad_mid * normed)
        vec_ref[BA : BA + 1, :] = sum_rows(grad_mid)
        inv = stat_ref[:, HEADS : HEADS + 1]
        grad = norm_back(grad_mid, normed, inv, v_ref[0, GA : GA + 1, :])
        vec_ref[BO : BO + 1, :] = sum_rows(grad)
        grad_a_ref[...] = grad


def mlp_bwd(grad, fnorm, fstat, normed, stat, up, square, down, vectors, layer_at):
    rows, width = normed.shape
    count = down.shape[1] // width
    whole = lambda n: pl.BlockSpec((rows, n), lambda j: (0, 0))
    f32 = jnp.float32
    vec_rows = vectors.shape[1]
    return pl.pallas_call(
        lambda *refs: mlp_bwd_kernel(count, *refs),
        grid=(count,),
        in_specs=[
            whole(width),
            whole(width),
            whole(LANES),
            whole(width),
            whole(LANES),
            pl.BlockSpec((rows, width), lambda j: (0, j)),
            pl.BlockSpec((1, 1, width, width), lambda j: (layer_at, 4 + j, 0, 0)),
            pl.BlockSpec((1, width, width), lambda j: (layer_at, j, 0)),
            pl.BlockSpec((1, vec_rows, width), lambda j: (layer_at, 0, 0)),
        ],
        out_specs=[
            pl.BlockSpec((1, width, width), lambda j: (j, 0, 0)),
            pl.BlockSpec((width, width), lambda j: (j, 0)),
            whole(width),
            pl.BlockSpec((vec_rows, width), lambda j: (0, 0)),
        ],
        out_shape=[
            jax.ShapeDtypeStruct((count, width, width), LOW),
            jax.ShapeDtypeStruct((count * width, width), LOW),
            jax.ShapeDtypeStruct((rows, width), f32),
            jax.ShapeDtypeStruct((vec_rows, width), f32),
        ],
        scratch_shapes=[
            pltpu.VMEM((rows, width), LOW),
            pltpu.VMEM((rows, width), f32),
            pltpu.VMEM((rows, width), LOW),
            pltpu.VMEM((rows, width), f32),
        ],
        name="mlp_bwd",
    )(grad, fnorm, fstat, normed, stat, up, square, down, vectors)


def attn_bwd_kernel(
    grad_ref, qkv_ref, stat_ref, mask_ref, w_ref, vec_in, dqkv_ref, grad_in_ref, low_ref, vec_ref, gctx
):
    rows, width = grad_ref.shape

    @pl.when(pl.program_id(0) == 0)
    def _():
        vec_ref[...] = vec_in[...]

    low_ref[...] = grad_ref[...].astype(LOW)
    gctx[...] = dot_back(low_ref[...], w_ref[0, 3]).astype(LOW)
    scale = HEAD_DIM ** (-0.5)
    lanes = lane_ids(rows)

    def pair_step(pair, carry):
        q = qkv_ref[:, pair_at(pair)]
        k = qkv_ref[:, pair_at(pair, width)]
        v = qkv_ref[:, pair_at(pair, 2 * width)]
        g = gctx[:, pair_at(pair)]
        grads = [[], [], []]
        for head in range(2):
            qh, kh, vh, gh = (lanes_of(t, head) for t in (q, k, v, g))
            log_total = jnp.sum(
                jnp.where(lanes == 2 * pair + head, stat_ref[...], 0.0), axis=-1, keepdims=True
            )
            s = dot_back(qh, kh) * scale
            s = jnp.where(mask_ref[0] > 0, s, NEG)
            p = jnp.exp(s - log_total)
            grad_p = dot_back(gh, vh)
            inner = jnp.sum(grad_p * p, axis=-1, keepdims=True)
            low_s = (p * (grad_p - inner)).astype(LOW)
            grads[0].append(dot(low_s, kh) * scale)
            grads[1].append(dot_weight(low_s, qh) * scale)
            grads[2].append(dot_weight(p.astype(LOW), gh))
        for j, row in ((0, BQ), (1, None), (2, BV)):
            both = jnp.concatenate(grads[j], axis=1)
            dqkv_ref[:, pair_at(pair, j * width)] = both.astype(LOW)
            if row is not None:
                vec_ref[row : row + 1, pair_at(pair)] += sum_rows(both)
        return carry

    lax.fori_loop(0, HEADS // 2, pair_step, 0)
    total = grad_ref[...]
    for j in range(3):
        total = total + dot_back(dqkv_ref[:, j * width : (j + 1) * width], w_ref[0, j])
    grad_in_ref[...] = total


def attn_bwd(grad_a, qkv, stat, mask, square, vec, layer_at):
    rows, width = grad_a.shape
    bins, block = mask.shape[:2]
    row = lambda n: pl.BlockSpec((block, n), lambda b: (b, 0))
    fixed = pl.BlockSpec(vec.shape, lambda b: (0, 0))
    f32 = jnp.float32
    return pl.pallas_call(
        attn_bwd_kernel,
        grid=(bins,),
        in_specs=[
            row(width),
            row(3 * width),
            row(LANES),
            pl.BlockSpec((1, block, block), lambda b: (b, 0, 0)),
            pl.BlockSpec((1, 4, width, width), lambda b: (layer_at, 0, 0, 0)),
            fixed,
        ],
        out_specs=[row(3 * width), row(width), row(width), fixed],
        out_shape=[
            jax.ShapeDtypeStruct((rows, 3 * width), LOW),
            jax.ShapeDtypeStruct((rows, width), f32),
            jax.ShapeDtypeStruct((rows, width), LOW),
            jax.ShapeDtypeStruct(vec.shape, f32),
        ],
        scratch_shapes=[pltpu.VMEM((block, width), LOW)],
        name="attn_bwd",
    )(grad_a, qkv, stat, mask, square, vec)


def attn_dw_kernel(act_ref, dqkv_ref, ctx_ref, low_ref, out_ref):
    at = pl.program_id(0)

    @pl.when(at < 3)
    def _():
        out_ref[0] = dot_weight(act_ref[...].astype(LOW), dqkv_ref[...]).astype(LOW)

    @pl.when(at == 3)
    def _():
        out_ref[0] = dot_weight(ctx_ref[...], low_ref[...]).astype(LOW)


def attn_dw(act, dqkv, ctx, low):
    rows, width = act.shape
    whole = pl.BlockSpec((rows, width), lambda j: (0, 0))
    return pl.pallas_call(
        attn_dw_kernel,
        grid=(4,),
        in_specs=[
            whole,
            pl.BlockSpec((rows, width), lambda j: (0, jnp.minimum(j, 2))),
            whole,
            whole,
        ],
        out_specs=pl.BlockSpec((1, width, width), lambda j: (j, 0, 0)),
        out_shape=jax.ShapeDtypeStruct((4, width, width), LOW),
        name="attn_dw",
    )(act, dqkv, ctx, low)


SMALL = ("bq", "bv", "bo", "ga", "ba", "bd", "gf", "bf", "bu")


def pack_attn(p, layer_at):
    wq = p["wqkv"][layer_at]
    rows, width = p["wo"][layer_at].shape
    small = jnp.concatenate([p[name][layer_at] for name in SMALL])
    pad = 8 * width - small.shape[0]
    small = jnp.pad(small, (0, pad)).reshape(8, width)
    parts = [wq[:, j * width : (j + 1) * width] for j in range(3)] + [p["wo"][layer_at], small]
    return jnp.concatenate(parts, axis=0)


def pack_mlp(p, layer_at):
    width = p["wd"].shape[-1]
    wu = p["wu"][layer_at]
    count = wu.shape[1] // width
    parts = [wu[:, j * width : (j + 1) * width] for j in range(count)] + [p["wd"][layer_at]]
    return jnp.concatenate(parts, axis=0)


def small_rows(p, layer_at, width):
    small = jnp.concatenate([p[name][layer_at] for name in SMALL])
    return jnp.pad(small, (0, 8 * width - small.shape[0])).reshape(8, width)


def vectors_of(all_small, rows):
    layers, width = all_small.shape[0], all_small.shape[-1]
    flat = all_small.reshape(layers, -1, 8 * width).astype(jnp.float32)
    even = flat[:, :, : 8 * rows].reshape(layers, -1, 8, rows).transpose(0, 2, 1, 3)
    up = flat[:, :, 8 * rows : 12 * rows]
    return jnp.concatenate([even.reshape(layers, 8, width), up.reshape(layers, 4, width)], axis=1)


def small_of(vec, rows):
    even = vec[:BU].reshape(BU, -1, rows).transpose(1, 0, 2).reshape(-1, BU * rows)
    return jnp.concatenate([even, vec[BU:].reshape(even.shape[0], -1)], axis=1)


def forward(hidden, act_in, w, mask, layer_at):
    square, down, vectors = w
    qkv, ctx, stat, normed = attn_fwd(hidden, square, vectors, mask, layer_at)
    up, out, out_low, fnorm, fstat = mlp_fwd(normed, square, down, vectors, layer_at)
    return out, out_low, (act_in, qkv, ctx, stat, normed, up, fnorm, fstat)


def backward(grad, kept, w, mask, layer_at):
    square, down, vectors = w
    act_in, qkv, ctx, stat, normed, up, fnorm, fstat = kept
    dwu, dwd, grad_a, vec = mlp_bwd(
        grad, fnorm, fstat, normed, stat, up, square, down, vectors, layer_at
    )
    dqkv, grad_in, low_a, vec = attn_bwd(grad_a, qkv, stat, mask, square, vec, layer_at)
    return grad_in, (attn_dw(act_in, dqkv, ctx, low_a), dwu, dwd, vec)


def whole_attn(grid, square, vec, rows):
    width = square.shape[-1]
    shape = grid.sizes
    small = small_of(vec, rows)
    small = jnp.pad(small, ((0, 0), (0, 8 * width - small.shape[1])))
    parts = [square[j].reshape(shape + (rows, width)) for j in range(4)]
    parts.append(small.astype(LOW).reshape(shape + (8, width)))
    return jnp.concatenate(parts, axis=-2)


def whole_mlp(grid, dwu, dwd, rows):
    width = dwd.shape[-1]
    shape = grid.sizes
    parts = [dwu[j].reshape(shape + (rows, width)) for j in range(dwu.shape[0])]
    parts.append(dwd.reshape(shape + (-1, width)))
    return jnp.concatenate(parts, axis=-2)


def shift_down(rows, amount):
    doubled = jnp.concatenate([jnp.zeros_like(rows), rows], axis=0)
    return lax.dynamic_slice_in_dim(doubled, rows.shape[0] - amount, rows.shape[0], 0)


def shift_up(rows, amount):
    doubled = jnp.concatenate([rows, jnp.zeros_like(rows)], axis=0)
    return lax.dynamic_slice_in_dim(doubled, amount, rows.shape[0], 0)


def pack_bin(slots, first_len, second_len):
    positions = jnp.arange(slots.shape[1])[:, None]
    later = shift_down(jnp.where(positions < second_len, slots[1], 0), first_len)
    return jnp.where(positions < first_len, slots[0], later)


def unpack_bin(rows, first_len, second_len):
    positions = jnp.arange(rows.shape[0])[:, None]
    first = jnp.where(positions < first_len, rows, 0)
    second = jnp.where(positions < second_len, shift_up(rows, first_len), 0)
    return jnp.stack([first, second])


def per_device(tokens_in, cotangent, lengths, bin_deal, random_blocks, *weights):
    names = ("wqkv", "bq", "bv", "wo", "bo", "ga", "ba", "wu", "bu", "wd", "bd", "gf", "bf")
    p = dict(zip(names, weights))
    rows = p["wo"].shape[1]
    members = lax.axis_size("fsdp")
    member = lax.axis_index("fsdp")
    group_at = lax.axis_index("dp")
    grid = Grid(lax.axis_size("dp"), members)
    slot_count = 2 * members
    slot_ids = jnp.arange(slot_count)
    deal_here = lax.dynamic_index_in_dim(bin_deal, group_at, 1, keepdims=False)
    slot_hits = (deal_here[:, :, None] == slot_ids[None, None, :]).astype(jnp.int32)
    source_of = jnp.sum(slot_hits * slot_ids[None, :, None], axis=1)
    lengths_here = lax.dynamic_slice_in_dim(lengths, group_at * slot_count, slot_count, 1)
    bin_lengths = jnp.take_along_axis(lengths_here, source_of, axis=1)
    random_here = lax.dynamic_slice_in_dim(random_blocks, group_at * slot_count, slot_count, 1)
    batch_count, unused_slots, rows_dev, width = tokens_in.shape
    bin_len = rows_dev * members
    order_index = source_of[:, :, None, None]

    def dealt(array):
        sent = jnp.take_along_axis(array, order_index, axis=1)
        return sent.reshape(batch_count, members, 2, rows_dev, width)

    blocks = lambda w: w.reshape(LAYERS, rows, -1, width).transpose(0, 2, 1, 3)
    square = jnp.concatenate([blocks(p["wqkv"]), blocks(p["wo"]), blocks(p["wu"])], axis=1)
    down = p["wd"].reshape(LAYERS, -1, rows, width)
    small = jnp.stack([small_rows(p, layer_at, width) for layer_at in range(LAYERS)])
    got_x, got_grad, *gathered = bring(
        grid.sizes, dealt(tokens_in), dealt(cotangent), square, down, small
    )
    arrived_x = got_x.reshape(batch_count, 2, bin_len, width)
    arrived_grad = got_grad.reshape(batch_count, 2, bin_len, width)
    square, down, small = gathered
    side = rows * grid.count
    w = (
        square.reshape(LAYERS, -1, side, width),
        down.reshape(LAYERS, -1, width),
        vectors_of(small, rows),
    )
    slot_pair = lax.dynamic_slice_in_dim(bin_lengths, 2 * member, 2, 1)
    random_pair = lax.dynamic_slice_in_dim(random_here, 2 * member, 2, 1)
    allowed = jax.vmap(bin_mask)(slot_pair[:, 0], slot_pair[:, 1], random_pair)
    first_len = slot_pair[:, 0] * BLOCK
    second_len = slot_pair[:, 1] * BLOCK

    def packed(slots):
        bins = [pack_bin(slots[m], first_len[m], second_len[m]) for m in range(batch_count)]
        return jnp.concatenate(bins, axis=0)

    def given_back(bins):
        bins = bins.reshape(batch_count, bin_len, width)
        slots = [unpack_bin(bins[m], first_len[m], second_len[m]) for m in range(batch_count)]
        sent = jnp.stack(slots)[:, None]
        back = lax.all_to_all(sent, "fsdp", split_axis=3, concat_axis=1, tiled=True)
        back = back.reshape(batch_count, slot_count, rows_dev, width)
        return jnp.take_along_axis(back, deal_here[:, :, None, None], axis=1)

    mask = allowed.astype(jnp.float32)
    hidden = act_in = packed(arrived_x)
    kept = []
    for layer_at in range(LAYERS):
        hidden, act_in, stored = forward(hidden, act_in, w, mask, layer_at)
        kept.append(stored)
    output = given_back(act_in)
    grad = packed(arrived_grad)
    sums = [None] * LAYERS
    for layer_at in reversed(range(LAYERS)):
        grad, (dws, dwu, dwd, vec) = backward(grad, kept[layer_at], w, mask, layer_at)
        sums[layer_at] = (
            scatter_rows(grid, whole_attn(grid, dws, vec, rows)),
            scatter_rows(grid, whole_mlp(grid, dwu, dwd, rows)),
        )
    input_grad = given_back(grad.astype(jnp.bfloat16))
    out = {name: [] for name in names}
    for attn, mlp in sums:
        blocks = [attn[j * rows : (j + 1) * rows] for j in range(4)]
        out["wqkv"].append(jnp.concatenate(blocks[:3], axis=1))
        out["wo"].append(blocks[3])
        small = attn[4 * rows :].reshape(-1)
        at = 0
        for name in SMALL:
            count = rows * (4 if name == "bu" else 1)
            out[name].append(small[at : at + count])
            at += count
        half = mlp.shape[0] // 2
        ups = [mlp[j * rows : (j + 1) * rows] for j in range(half // rows)]
        out["wu"].append(jnp.concatenate(ups, axis=1))
        out["wd"].append(mlp[half:])
    return (output, input_grad) + tuple(jnp.stack(out[name]) for name in names)


def solution(mesh):
    tokens = P(None, "dp", "fsdp", None)
    matrix = P(None, AXES, None)
    vector = P(None, AXES)
    weights = (matrix, vector, vector, matrix, vector, vector, vector)
    weights += (matrix, vector, matrix, vector, vector, vector)
    return jax.shard_map(
        per_device,
        mesh=mesh,
        in_specs=(tokens, tokens, P(), P(), P()) + weights,
        out_specs=(tokens, tokens) + weights,
        check_vma=False,
    )
```

```python
import jax
import jax.numpy as jnp
from jax import lax
from jax.experimental import pallas as pl
from jax.experimental.pallas import tpu as pltpu
from jax.sharding import PartitionSpec as P

HEADS = 12
BLOCK = 64
NBLK = 6
LAYERS = 2
CORES = 2
AXES = ("dp", "fsdp")
NEG = -1000000000.0
HEAD_DIM = 64
VMEM_BYTES = 67043328


epsilon = 1e-06


def split_fsdp(count):
    inner = 1
    while (2 * inner) ** 2 <= count:
        inner *= 2
    return (count // inner, inner)


class Grid:
    def __init__(self, dp_count, fsdp_count):
        outer, inner = split_fsdp(fsdp_count)
        self.sizes = (dp_count // CORES, CORES, outer, inner)
        dp_at, fsdp_at = lax.axis_index("dp"), lax.axis_index("fsdp")
        self.at = (dp_at // CORES, dp_at % CORES, fsdp_at // inner, fsdp_at % inner)

        self.count = dp_count * fsdp_count


ALL = slice(None)
HBM = pl.BlockSpec(memory_space=pl.ANY)


class Links:
    def __init__(self, sizes, send_sem, recv_sem):
        outer, inner = sizes[2:]
        dp_at, fsdp_at = lax.axis_index("dp"), lax.axis_index("fsdp")
        self.sizes = sizes
        self.at = (dp_at // CORES, dp_at % CORES, fsdp_at // inner, fsdp_at % inner)
        self.send_sem, self.recv_sem = send_sem, recv_sem
        self.used = 0

    def device(self, place):
        return (place[0] * CORES + place[1], place[2] * self.sizes[3] + place[3])

    def along(self, axis, offset):
        place = list(self.at)
        place[axis] = (place[axis] + offset) % self.sizes[axis]
        return self.device(place)

    def start(self, source, target, device):
        copy = pltpu.make_async_remote_copy(
            src_ref=source,
            dst_ref=target,
            send_sem=self.send_sem.at[self.used],
            recv_sem=self.recv_sem.at[self.used],
            device_id=device,
            device_id_type=pl.DeviceIdType.MESH,
        )
        self.used += 1
        copy.start()
        return copy

    def start_here(self, source, target):
        copy = pltpu.make_async_copy(source, target, self.recv_sem.at[self.used])
        self.used += 1
        copy.start()
        return copy

    def greet(self, devices):
        barrier = pltpu.get_barrier_semaphore()
        for device in devices:
            pl.semaphore_signal(barrier, inc=1, device_id=device, device_id_type=pl.DeviceIdType.MESH)
        pl.semaphore_wait(barrier, len(devices))

    def partners(self):
        found = [self.along(axis, k) for axis in (0, 1) for k in range(1, self.sizes[axis])]
        count = self.sizes[2] * self.sizes[3]
        return found + [self.member(k) for k in range(1, count)]

    def member(self, offset):
        count = self.sizes[2] * self.sizes[3]
        flat = self.at[2] * self.sizes[3] + self.at[3]
        return (self.at[0] * CORES + self.at[1], (flat + offset) % count)


class Gather:
    def __init__(self, links, source, target, order):
        self.links, self.source, self.target, self.order = links, source, target, order
        self.sent = []
        self.across = []

    def begin(self):
        links = self.links
        spot = self.target(*links.at)
        self.own = links.start_here(self.source, spot)
        self.column = [
            links.start(self.source, spot, links.along(2, k)) for k in range(1, links.sizes[2])
        ]

    def hand_over(self, spot):
        self.across.append(self.links.start(spot, spot, self.links.along(1, 1)))

    def first(self):
        links = self.links
        x, c, o, i = links.at
        self.own.wait()
        for copy in self.column:
            copy.wait_recv()
        spot = self.target(x, c, ALL, i)
        axis = self.order[0]
        self.line = [
            links.start(spot, spot, links.along(axis, k)) for k in range(1, links.sizes[axis])
        ]
        self.hand_over(spot)

    def second(self):
        links = self.links
        x, c, o, i = links.at
        for copy in self.line:
            copy.wait_recv()
        first, second = self.order
        spot = self.target(ALL, c, ALL, i) if first == 0 else self.target(x, c, ALL, ALL)
        self.sheet = [
            links.start(spot, spot, links.along(second, k)) for k in range(1, links.sizes[second])
        ]
        for k in range(1, links.sizes[first]):
            near = (links.at[first] - k) % links.sizes[first]
            self.hand_over(
                self.target(near, c, ALL, i) if first == 0 else self.target(x, c, ALL, near)
            )

    def third(self):
        links = self.links
        c = links.at[1]
        second = self.order[1]
        for k, copy in enumerate(self.sheet, 1):
            copy.wait_recv()
            near = (links.at[second] - k) % links.sizes[second]
            self.hand_over(
                self.target(near, c, ALL, ALL) if second == 0 else self.target(ALL, c, ALL, near)
            )

    def end(self):
        for copy in self.across:
            copy.wait()
        for copy in self.column + self.line + self.sheet:
            copy.wait_send()


def deal_out(links, source, target):
    count = links.sizes[2] * links.sizes[3]
    me = links.at[2] * links.sizes[3] + links.at[3]
    spot = target.at[:, :, me]
    copies = [links.start_here(source.at[:, me], spot)]
    for k in range(1, count):
        copies.append(links.start(source.at[:, (me + k) % count], spot, links.member(k)))
    return copies


def deal_back(links, source, target):
    count = links.sizes[2] * links.sizes[3]
    me = links.at[2] * links.sizes[3] + links.at[3]
    spot = target.at[:, me]
    copies = [links.start_here(source.at[:, :, me], spot)]
    for k in range(1, count):
        copies.append(links.start(source.at[:, :, (me + k) % count], spot, links.member(k)))
    return copies


def gathers_of(links, layer_at, square, down, small, all_square, all_down, all_small):
    def of_square(start, order):
        blocks = slice(start, start + 2)
        return Gather(
            links,
            square.at[layer_at, blocks],
            lambda *place: all_square.at[(layer_at, blocks) + place],
            order,
        )

    def of_down(start, order):
        blocks = slice(start, start + 2)
        return Gather(
            links,
            down.at[layer_at, blocks],
            lambda *place: all_down.at[(layer_at,) + place + (blocks,)],
            order,
        )

    tiny = Gather(
        links, small.at[layer_at], lambda *place: all_small.at[(layer_at,) + place], (0, 3)
    )
    return [
        [tiny, of_square(0, (0, 3)), of_square(2, (3, 0))],
        [of_square(4, (0, 3)), of_square(6, (3, 0))],
        [of_down(0, (0, 3)), of_down(2, (3, 0))],
    ]


def bring_kernel(sizes, *refs):
    sent_x, square, down, small = refs[:4]
    got_x, all_square, all_down, all_small = refs[4:8]
    links = Links(sizes, *refs[8:])
    links.greet(links.partners())
    groups = []
    for layer_at in range(LAYERS):
        groups += gathers_of(
            links, layer_at, square, down, small, all_square, all_down, all_small
        )
    for group in groups:
        for item in group:
            item.begin()
    moved = deal_out(links, sent_x, got_x)
    for at in range(len(groups) + 2):
        if at < len(groups):
            for item in groups[at]:
                item.first()
        if 0 < at <= len(groups):
            for item in groups[at - 1]:
                item.second()
        if at > 1:
            for item in groups[at - 2]:
                item.third()
    for group in groups:
        for item in group:
            item.end()
    for copy in moved:
        copy.wait()


def bring(sizes, sent_x, square, down, small):
    low = jnp.bfloat16
    batch, members, two, rows, width = sent_x.shape
    r = square.shape[2]
    got = jax.ShapeDtypeStruct((batch, two, members, rows, width), low)
    outs = [
        got,
        jax.ShapeDtypeStruct((LAYERS, square.shape[1]) + sizes + (r, width), low),
        jax.ShapeDtypeStruct((LAYERS,) + sizes + (down.shape[1], r, width), low),
        jax.ShapeDtypeStruct((LAYERS,) + sizes + (8, width), low),
    ]
    per_item = 1 + sum(n - 1 for n in sizes) + 4 + sizes[0] + sizes[3]
    count = 7 * LAYERS * per_item + members
    return pl.pallas_call(
        lambda *refs: bring_kernel(sizes, *refs),
        out_shape=outs,
        in_specs=[HBM] * 4,
        out_specs=[HBM] * 4,
        scratch_shapes=[pltpu.SemaphoreType.DMA((count,)), pltpu.SemaphoreType.DMA((count,))],
        compiler_params=pltpu.CompilerParams(collective_id=0, has_side_effects=True),
        name="bring",
    )(sent_x, square, down, small)


def each(dims, body):
    total = 1
    for n in dims:
        total *= n

    def step(flat, carry):
        at = []
        for n in reversed(dims):
            at.insert(0, flat % n)
            flat = flat // n
        body(tuple(at))
        return carry

    lax.fori_loop(0, total, step, 0)


def wide(ref, at):
    return ref[at].astype(jnp.float32)


class Sum:
    def __init__(self, links, source, order, lead, bufs, out_ref):
        self.links, self.source, self.order, self.lead = links, source, order, lead
        self.mine, self.theirs, self.first, self.half, self.second, self.quarter, self.last, self.out = bufs
        self.out_ref = out_ref
        self.sent = []

    def send(self, source, target, axis, offset):
        copy = self.links.start(source, target, self.links.along(axis, offset))
        self.sent.append(copy)
        return copy

    def begin(self):
        c = self.links.at[1]
        self.here = self.links.start_here(self.source(c), self.mine)
        self.there = self.send(self.source(1 - c), self.theirs, 1, 1)

    def at(self, *place):
        return (ALL,) * self.lead + place

    def spread(self, ref, axes, axis, into):
        size, me = self.links.sizes[axis], self.links.at[axis]
        found = []
        for k in range(1, size):
            place = [ALL] * len(axes)
            place[axes.index(axis)] = (me + k) % size
            found.append(self.send(ref.at[self.at(*place)], into.at[k - 1], axis, k))
        return found

    def fold(self, ref, axes, axis, arrived, into):
        size, me = self.links.sizes[axis], self.links.at[axis]
        spot = axes.index(axis) + self.lead

        def add(at):
            total = wide(ref, at[:spot] + (me,) + at[spot:])
            for k in range(size - 1):
                total = total + wide(arrived, (k,) + at)
            into[at] = total.astype(into.dtype)

        each(into.shape[:-2], add)

    def stage_one(self):
        self.here.wait()
        self.there.wait_recv()

        def add(at):
            self.mine[at] = (wide(self.mine, at) + wide(self.theirs, at)).astype(LOW)

        each(self.mine.shape[:-2], add)
        self.moving = self.spread(self.mine, (0, 2, 3), self.order[0], self.first)

    def stage_two(self):
        for copy in self.moving:
            copy.wait_recv()
        self.fold(self.mine, (0, 2, 3), self.order[0], self.first, self.half)
        axes = (2, 3) if self.order[0] == 0 else (0, 2)
        self.moving = self.spread(self.half, axes, self.order[1], self.second)

    def stage_three(self):
        for copy in self.moving:
            copy.wait_recv()
        axes = (2, 3) if self.order[0] == 0 else (0, 2)
        self.fold(self.half, axes, self.order[1], self.second, self.quarter)
        self.moving = self.spread(self.quarter, (2,), 2, self.last)

    def stage_four(self):
        for copy in self.moving:
            copy.wait_recv()
        self.fold(self.quarter, (2,), 2, self.last, self.out)
        self.result = self.links.start_here(self.out, self.out_ref)

    def end(self):
        self.result.wait()
        for copy in self.sent:
            copy.wait_send()


class Whole:
    def __init__(self, links, source, bufs, out_ref):
        self.links, self.source, self.out_ref = links, source, out_ref
        self.held, self.arrived = bufs[:5], bufs[5:]
        self.sent = []

    def begin(self):
        self.here = self.links.start_here(self.source, self.held[0])

    def send(self, at, axis):
        self.moving = [
            self.links.start(
                self.held[at], self.arrived[at].at[k - 1], self.links.along(axis, k)
            )
            for k in range(1, self.links.sizes[axis])
        ]
        self.sent += self.moving

    def fold(self, at):
        for copy in self.moving:
            copy.wait_recv()
        total = self.held[at][...]
        for k in range(self.arrived[at].shape[0]):
            total = total + self.arrived[at][k]
        self.held[at + 1][...] = total

    def stage_one(self):
        self.here.wait()
        self.send(0, 1)

    def stage_two(self):
        self.fold(0)
        self.send(1, 0)

    def stage_three(self):
        self.fold(1)
        self.send(2, 3)

    def stage_four(self):
        self.fold(2)
        self.send(3, 2)

    def end(self):
        self.fold(3)
        result = self.links.start_here(self.held[4], self.out_ref)
        result.wait()
        for copy in self.sent:
            copy.wait_send()


def whole_buffers(sizes, shape):
    f32 = jnp.float32
    arrived = [pltpu.VMEM((sizes[axis] - 1,) + shape, f32) for axis in (1, 0, 3, 2)]
    return [pltpu.VMEM(shape, f32)] * 5 + arrived


def sum_buffers(sizes, order, lead, tail):
    x, c, o, i = sizes
    whole = lead + (x, o, i) + tail
    half = lead + ((x, o) if order[0] == 3 else (o, i)) + tail
    quarter = lead + (o,) + tail
    low = [
        whole,
        whole,
        (sizes[order[0]] - 1,) + half,
        half,
        (sizes[order[1]] - 1,) + quarter,
        quarter,
        (o - 1,) + lead + tail,
    ]
    return [pltpu.VMEM(shape, LOW) for shape in low] + [pltpu.VMEM(lead + tail, jnp.float32)]


def home_kernel(sizes, layouts, *refs):
    inputs, refs = refs[: 3 * LAYERS], refs[3 * LAYERS :]
    vec, sent, g_square, g_down, g_vec, back = refs[:6]
    links = Links(sizes, *refs[6:8])
    whole = Whole(links, vec, refs[8:17], g_vec)
    refs = refs[17:]
    links.greet(links.partners())
    sums = []
    for layer_at, kind, start, order, lead, tail in layouts:
        dws, dwu, dwd = inputs[3 * layer_at : 3 * layer_at + 3]
        bufs, refs = refs[:8], refs[8:]
        blocks = slice(start, start + 2)
        if kind == "down":
            source = lambda core, blocks=blocks, dwd=dwd: dwd.at[:, core, :, :, blocks]
            out = g_down.at[layer_at, blocks]
        else:
            array = dws if kind == "attn" else dwu
            source = lambda core, blocks=blocks, array=array: array.at[blocks, :, core]
            out = g_square.at[layer_at, blocks if kind == "attn" else slice(start + 4, start + 6)]
        sums.append(Sum(links, source, order, len(lead), bufs, out))
    groups = [sums[at : at + 2] for at in range(0, len(sums), 2)]
    groups[0].append(whole)
    sums.append(whole)
    for group in groups:
        for item in group:
            item.begin()
    moved = deal_back(links, sent, back)
    stages = ("stage_one", "stage_two", "stage_three", "stage_four")
    for turn in range(len(groups) + len(stages) - 1):
        for depth in range(len(stages)):
            if 0 <= turn - depth < len(groups):
                for item in groups[turn - depth]:
                    getattr(item, stages[depth])()
    for item in sums:
        item.end()
    for copy in moved:
        copy.wait()


def take_home(sizes, grads, vec, sent):
    r, width = grads[0][0].shape[-2:]
    tail = (r, width)
    y_first, x_first = (3, 0), (0, 3)
    layouts = []
    for layer_at in reversed(range(LAYERS)):
        for kind in ("down", "up", "attn"):
            lead, piece = ((), (2,) + tail) if kind == "down" else ((2,), tail)
            layouts += [
                (layer_at, kind, 0, y_first, lead, piece),
                (layer_at, kind, 2, x_first, lead, piece),
            ]
    members = sizes[2] * sizes[3]
    f32 = jnp.float32
    batch, two, count, rows = sent.shape[:4]
    outs = [
        jax.ShapeDtypeStruct((LAYERS, 8, r, width), f32),
        jax.ShapeDtypeStruct((LAYERS, 4, r, width), f32),
        jax.ShapeDtypeStruct(vec.shape, f32),
        jax.ShapeDtypeStruct((batch, count, two, rows, width), LOW),
    ]
    args = [array for group in grads for array in group] + [vec, sent]
    scratch = whole_buffers(sizes, vec.shape)
    for layer_at, kind, start, order, lead, piece in layouts:
        scratch += sum_buffers(sizes, order, lead, piece)
    count = (len(layouts) + 1) * (3 + sum(n - 1 for n in sizes)) + members
    sems = [pltpu.SemaphoreType.DMA((count,)), pltpu.SemaphoreType.DMA((count,))]
    return pl.pallas_call(
        lambda *refs: home_kernel(sizes, layouts, *refs),
        out_shape=outs,
        in_specs=[HBM] * len(args),
        out_specs=[HBM] * len(outs),
        scratch_shapes=sems + scratch,
        compiler_params=pltpu.CompilerParams(
            collective_id=1, has_side_effects=True, vmem_limit_bytes=VMEM_BYTES
        ),
        name="take_home",
    )(*args)


def bin_mask(first_blocks, second_blocks, random_pair):
    block_ids = jnp.arange(NBLK)
    later_seg = block_ids >= first_blocks
    rel_block = jnp.where(later_seg, block_ids - first_blocks, block_ids)
    seg_len = jnp.where(later_seg, second_blocks, first_blocks)
    live_block = block_ids < first_blocks + second_blocks
    rand_rows = jnp.where(
        later_seg[:, None],
        jnp.take(random_pair[1], rel_block, axis=0),
        jnp.take(random_pair[0], rel_block, axis=0),
    )
    picked = jnp.remainder(rand_rows, seg_len[:, None])
    row_rel = rel_block[:, None]
    col_rel = rel_block[None, :]
    row_len = seg_len[:, None]
    nearby = jnp.abs(row_rel - col_rel) <= 1
    global_hit = (
        (col_rel == 0) | (col_rel == row_len - 1) | (row_rel == 0) | (row_rel == row_len - 1)
    )
    random_hit = jnp.any(picked[:, :, None] == rel_block[None, None, :], axis=1)
    same_seg = (
        (later_seg[:, None] == later_seg[None, :]) & live_block[:, None] & live_block[None, :]
    )
    allowed = (nearby | global_hit | random_hit) & same_seg
    return jnp.repeat(jnp.repeat(allowed, BLOCK, axis=0), BLOCK, axis=1)


def dot(left, right):
    return jnp.dot(left, right, preferred_element_type=jnp.float32)


def dot_back(left, right):
    return lax.dot_general(left, right, (((1,), (1,)), ((), ())), preferred_element_type=jnp.float32)


def dot_weight(left, right):
    return lax.dot_general(left, right, (((0,), (0,)), ((), ())), preferred_element_type=jnp.float32)


LOW = jnp.bfloat16
LANES = 128
BQ, BV, BO, GA, BA, BD, GF, BF, BU = range(9)


def layer_norm(residual):
    center = residual - jnp.mean(residual, axis=-1, keepdims=True)
    inv_std = lax.rsqrt(jnp.mean(center * center, axis=-1, keepdims=True) + epsilon)
    return (center * inv_std, inv_std)


def norm_back(grad_out, normed, inv_std, gain):
    scaled = grad_out * gain
    return inv_std * (
        scaled
        - jnp.mean(scaled, axis=-1, keepdims=True)
        - normed * jnp.mean(scaled * normed, axis=-1, keepdims=True)
    )


def gelu_parts(u):
    root = 0.7978845608028654
    t = jnp.tanh(root * (u + 0.044715 * (u * u * u)))
    half = 0.5 * (1.0 + t)
    slope = half + 0.5 * u * (1.0 - t * t) * (root * (1.0 + 3 * 0.044715 * (u * u)))
    return (u * half, slope)


def lanes_of(pair, head):
    return pair[:, head * HEAD_DIM : (head + 1) * HEAD_DIM]


def pair_at(pair, offset=0):
    return pl.ds(pl.multiple_of(offset + pair * 2 * HEAD_DIM, 2 * HEAD_DIM), 2 * HEAD_DIM)


def lane_ids(rows):
    return lax.broadcasted_iota(jnp.int32, (rows, LANES), 1)


def attn_fwd_kernel(x_ref, w_ref, v_ref, mask_ref, qkv_ref, ctx_ref, stat_ref, normed_ref):
    rows, width = x_ref.shape
    act = x_ref[...].astype(LOW)
    for j, bias in enumerate((BQ, None, BV)):
        out = dot(act, w_ref[0, j])
        if bias is not None:
            out = out + v_ref[0, bias : bias + 1, :]
        qkv_ref[:, j * width : (j + 1) * width] = out.astype(LOW)
    scale = HEAD_DIM ** (-0.5)
    lanes = lane_ids(rows)
    stat_ref[...] = jnp.zeros_like(stat_ref)

    def pair_step(pair, carry):
        q = qkv_ref[:, pair_at(pair)]
        k = qkv_ref[:, pair_at(pair, width)]
        v = qkv_ref[:, pair_at(pair, 2 * width)]
        mixed = []
        for head in range(2):
            s = dot_back(lanes_of(q, head), lanes_of(k, head)) * scale
            s = jnp.where(mask_ref[0] > 0, s, NEG)
            top = jnp.max(s, axis=-1, keepdims=True)
            e = jnp.exp(s - top)
            total = jnp.sum(e, axis=-1, keepdims=True)
            mixed.append(dot(e.astype(LOW), lanes_of(v, head)) / total)
            log_total = top + jnp.log(total)
            stat_ref[...] = jnp.where(lanes == 2 * pair + head, log_total, stat_ref[...])
        ctx_ref[:, pair_at(pair)] = jnp.concatenate(mixed, axis=1).astype(LOW)
        return carry

    lax.fori_loop(0, HEADS // 2, pair_step, 0)
    resid = x_ref[...].astype(jnp.float32) + dot(ctx_ref[...], w_ref[0, 3])
    normed, inv = layer_norm(resid + v_ref[0, BO : BO + 1, :])
    normed_ref[...] = normed
    stat_ref[...] = jnp.where(lanes == HEADS, inv, stat_ref[...])


def attn_fwd(x, square, vectors, mask, layer_at):
    rows, width = x.shape
    bins, block = mask.shape[:2]
    row = lambda n: pl.BlockSpec((block, n), lambda b: (b, 0))
    f32 = jnp.float32
    return pl.pallas_call(
        attn_fwd_kernel,
        grid=(bins,),
        in_specs=[
            row(width),
            pl.BlockSpec((1, 4, width, width), lambda b: (layer_at, 0, 0, 0)),
            pl.BlockSpec((1,) + vectors.shape[1:], lambda b: (layer_at, 0, 0)),
            pl.BlockSpec((1, block, block), lambda b: (b, 0, 0)),
        ],
        out_specs=[row(3 * width), row(width), row(LANES), row(width)],
        out_shape=[
            jax.ShapeDtypeStruct((rows, 3 * width), LOW),
            jax.ShapeDtypeStruct((rows, width), LOW),
            jax.ShapeDtypeStruct((rows, LANES), f32),
            jax.ShapeDtypeStruct((rows, width), f32),
        ],
        name="attn_fwd",
    )(x, square, vectors, mask)


def middle_of(normed_ref, v_ref):
    return normed_ref[...] * v_ref[0, GA : GA + 1, :] + v_ref[0, BA : BA + 1, :]


def bias_up_of(v_ref, at, count):
    picked = v_ref[0, BU : BU + 1, :]
    for j in range(1, count):
        picked = jnp.where(at == j, v_ref[0, BU + j : BU + j + 1, :], picked)
    return picked


def mlp_fwd_kernel(
    count, normed_ref, wu_ref, wd_ref, v_ref, up_ref, out_ref, low_ref, fnorm_ref, stat_ref, mid, acc
):
    at = pl.program_id(0)

    @pl.when(at == 0)
    def _():
        mid[...] = middle_of(normed_ref, v_ref).astype(LOW)
        acc[...] = jnp.zeros_like(acc)

    up = dot(mid[...], wu_ref[0, 0]) + bias_up_of(v_ref, at, count)
    up_ref[...] = up
    acc[...] += dot(gelu_parts(up)[0].astype(LOW), wd_ref[0])

    @pl.when(at == count - 1)
    def _():
        resid = middle_of(normed_ref, v_ref) + acc[...] + v_ref[0, BD : BD + 1, :]
        normed, inv = layer_norm(resid)
        fnorm_ref[...] = normed
        stat_ref[...] = jnp.broadcast_to(inv, stat_ref.shape)
        out = normed * v_ref[0, GF : GF + 1, :] + v_ref[0, BF : BF + 1, :]
        out_ref[...] = out
        low_ref[...] = out.astype(LOW)


def mlp_fwd(normed, square, down, vectors, layer_at):
    rows, width = normed.shape
    count = down.shape[1] // width
    whole = lambda n: pl.BlockSpec((rows, n), lambda j: (0, 0))
    f32 = jnp.float32
    return pl.pallas_call(
        lambda *refs: mlp_fwd_kernel(count, *refs),
        grid=(count,),
        in_specs=[
            whole(width),
            pl.BlockSpec((1, 1, width, width), lambda j: (layer_at, 4 + j, 0, 0)),
            pl.BlockSpec((1, width, width), lambda j: (layer_at, j, 0)),
            pl.BlockSpec((1,) + vectors.shape[1:], lambda j: (layer_at, 0, 0)),
        ],
        out_specs=[
            pl.BlockSpec((rows, width), lambda j: (0, j)),
            whole(width),
            whole(width),
            whole(width),
            whole(LANES),
        ],
        out_shape=[
            jax.ShapeDtypeStruct((rows, count * width), f32),
            jax.ShapeDtypeStruct((rows, width), f32),
            jax.ShapeDtypeStruct((rows, width), LOW),
            jax.ShapeDtypeStruct((rows, width), f32),
            jax.ShapeDtypeStruct((rows, LANES), f32),
        ],
        scratch_shapes=[pltpu.VMEM((rows, width), LOW), pltpu.VMEM((rows, width), f32)],
        name="mlp_fwd",
    )(normed, square, down, vectors)


def sum_rows(values):
    return jnp.sum(values, axis=0, keepdims=True)


def mlp_bwd_kernel(
    count,
    grad_ref,
    fnorm_ref,
    fstat_ref,
    normed_ref,
    stat_ref,
    up_ref,
    wu_ref,
    wd_ref,
    v_ref,
    dwu_ref,
    dwd_ref,
    grad_a_ref,
    vec_ref,
    mid,
    grad_f,
    low_f,
    acc,
):
    at = pl.program_id(0)

    @pl.when(at == 0)
    def _():
        grad_out, normed = grad_ref[...].astype(jnp.float32), fnorm_ref[...]
        vec_ref[...] = jnp.zeros_like(vec_ref)
        vec_ref[GF : GF + 1, :] = sum_rows(grad_out * normed)
        vec_ref[BF : BF + 1, :] = sum_rows(grad_out)
        grad = norm_back(grad_out, normed, fstat_ref[:, :1], v_ref[0, GF : GF + 1, :])
        vec_ref[BD : BD + 1, :] = sum_rows(grad)
        grad_f[...] = grad
        low_f[...] = grad.astype(LOW)
        mid[...] = middle_of(normed_ref, v_ref).astype(LOW)
        acc[...] = jnp.zeros_like(acc)

    act, slope = gelu_parts(up_ref[...])
    dwd_ref[...] = dot_weight(act.astype(LOW), low_f[...]).astype(LOW)
    grad_up = dot_back(low_f[...], wd_ref[0]) * slope
    vec_ref[pl.ds(BU + at, 1), :] = sum_rows(grad_up)
    low_up = grad_up.astype(LOW)
    dwu_ref[0] = dot_weight(mid[...], low_up).astype(LOW)
    acc[...] += dot_back(low_up, wu_ref[0, 0])

    @pl.when(at == count - 1)
    def _():
        grad_mid, normed = grad_f[...] + acc[...], normed_ref[...]
        vec_ref[GA : GA + 1, :] = sum_rows(grad_mid * normed)
        vec_ref[BA : BA + 1, :] = sum_rows(grad_mid)
        inv = stat_ref[:, HEADS : HEADS + 1]
        grad = norm_back(grad_mid, normed, inv, v_ref[0, GA : GA + 1, :])
        vec_ref[BO : BO + 1, :] = sum_rows(grad)
        grad_a_ref[...] = grad


def mlp_bwd(grad, fnorm, fstat, normed, stat, up, square, down, vectors, layer_at):
    rows, width = normed.shape
    count = down.shape[1] // width
    whole = lambda n: pl.BlockSpec((rows, n), lambda j: (0, 0))
    f32 = jnp.float32
    vec_rows = vectors.shape[1]
    return pl.pallas_call(
        lambda *refs: mlp_bwd_kernel(count, *refs),
        grid=(count,),
        in_specs=[
            whole(width),
            whole(width),
            whole(LANES),
            whole(width),
            whole(LANES),
            pl.BlockSpec((rows, width), lambda j: (0, j)),
            pl.BlockSpec((1, 1, width, width), lambda j: (layer_at, 4 + j, 0, 0)),
            pl.BlockSpec((1, width, width), lambda j: (layer_at, j, 0)),
            pl.BlockSpec((1, vec_rows, width), lambda j: (layer_at, 0, 0)),
        ],
        out_specs=[
            pl.BlockSpec((1, width, width), lambda j: (j, 0, 0)),
            pl.BlockSpec((width, width), lambda j: (j, 0)),
            whole(width),
            pl.BlockSpec((vec_rows, width), lambda j: (0, 0)),
        ],
        out_shape=[
            jax.ShapeDtypeStruct((count, width, width), LOW),
            jax.ShapeDtypeStruct((count * width, width), LOW),
            jax.ShapeDtypeStruct((rows, width), f32),
            jax.ShapeDtypeStruct((vec_rows, width), f32),
        ],
        scratch_shapes=[
            pltpu.VMEM((rows, width), LOW),
            pltpu.VMEM((rows, width), f32),
            pltpu.VMEM((rows, width), LOW),
            pltpu.VMEM((rows, width), f32),
        ],
        name="mlp_bwd",
    )(grad, fnorm, fstat, normed, stat, up, square, down, vectors)


def attn_bwd_kernel(
    grad_ref, qkv_ref, stat_ref, mask_ref, w_ref, vec_in, dqkv_ref, grad_in_ref, low_ref, vec_ref, gctx
):
    rows, width = grad_ref.shape

    @pl.when(pl.program_id(0) == 0)
    def _():
        vec_ref[...] = vec_in[...]

    low_ref[...] = grad_ref[...].astype(LOW)
    gctx[...] = dot_back(low_ref[...], w_ref[0, 3]).astype(LOW)
    scale = HEAD_DIM ** (-0.5)
    lanes = lane_ids(rows)

    def pair_step(pair, carry):
        q = qkv_ref[:, pair_at(pair)]
        k = qkv_ref[:, pair_at(pair, width)]
        v = qkv_ref[:, pair_at(pair, 2 * width)]
        g = gctx[:, pair_at(pair)]
        grads = [[], [], []]
        for head in range(2):
            qh, kh, vh, gh = (lanes_of(t, head) for t in (q, k, v, g))
            log_total = jnp.sum(
                jnp.where(lanes == 2 * pair + head, stat_ref[...], 0.0), axis=-1, keepdims=True
            )
            s = dot_back(qh, kh) * scale
            s = jnp.where(mask_ref[0] > 0, s, NEG)
            p = jnp.exp(s - log_total)
            grad_p = dot_back(gh, vh)
            inner = jnp.sum(grad_p * p, axis=-1, keepdims=True)
            low_s = (p * (grad_p - inner)).astype(LOW)
            grads[0].append(dot(low_s, kh) * scale)
            grads[1].append(dot_weight(low_s, qh) * scale)
            grads[2].append(dot_weight(p.astype(LOW), gh))
        for j, row in ((0, BQ), (1, None), (2, BV)):
            both = jnp.concatenate(grads[j], axis=1)
            dqkv_ref[:, pair_at(pair, j * width)] = both.astype(LOW)
            if row is not None:
                vec_ref[row : row + 1, pair_at(pair)] += sum_rows(both)
        return carry

    lax.fori_loop(0, HEADS // 2, pair_step, 0)
    total = grad_ref[...]
    for j in range(3):
        total = total + dot_back(dqkv_ref[:, j * width : (j + 1) * width], w_ref[0, j])
    grad_in_ref[...] = total


def attn_bwd(grad_a, qkv, stat, mask, square, vec, layer_at):
    rows, width = grad_a.shape
    bins, block = mask.shape[:2]
    row = lambda n: pl.BlockSpec((block, n), lambda b: (b, 0))
    fixed = pl.BlockSpec(vec.shape, lambda b: (0, 0))
    f32 = jnp.float32
    return pl.pallas_call(
        attn_bwd_kernel,
        grid=(bins,),
        in_specs=[
            row(width),
            row(3 * width),
            row(LANES),
            pl.BlockSpec((1, block, block), lambda b: (b, 0, 0)),
            pl.BlockSpec((1, 4, width, width), lambda b: (layer_at, 0, 0, 0)),
            fixed,
        ],
        out_specs=[row(3 * width), row(width), row(width), fixed],
        out_shape=[
            jax.ShapeDtypeStruct((rows, 3 * width), LOW),
            jax.ShapeDtypeStruct((rows, width), f32),
            jax.ShapeDtypeStruct((rows, width), LOW),
            jax.ShapeDtypeStruct(vec.shape, f32),
        ],
        scratch_shapes=[pltpu.VMEM((block, width), LOW)],
        name="attn_bwd",
    )(grad_a, qkv, stat, mask, square, vec)


def attn_dw_kernel(act_ref, dqkv_ref, ctx_ref, low_ref, out_ref):
    at = pl.program_id(0)

    @pl.when(at < 3)
    def _():
        out_ref[0] = dot_weight(act_ref[...].astype(LOW), dqkv_ref[...]).astype(LOW)

    @pl.when(at == 3)
    def _():
        out_ref[0] = dot_weight(ctx_ref[...], low_ref[...]).astype(LOW)


def attn_dw(act, dqkv, ctx, low):
    rows, width = act.shape
    whole = pl.BlockSpec((rows, width), lambda j: (0, 0))
    return pl.pallas_call(
        attn_dw_kernel,
        grid=(4,),
        in_specs=[
            whole,
            pl.BlockSpec((rows, width), lambda j: (0, jnp.minimum(j, 2))),
            whole,
            whole,
        ],
        out_specs=pl.BlockSpec((1, width, width), lambda j: (j, 0, 0)),
        out_shape=jax.ShapeDtypeStruct((4, width, width), LOW),
        name="attn_dw",
    )(act, dqkv, ctx, low)


SMALL = ("bq", "bv", "bo", "ga", "ba", "bd", "gf", "bf", "bu")


def small_rows(p, layer_at, width):
    small = jnp.concatenate([p[name][layer_at] for name in SMALL])
    return jnp.pad(small, (0, 8 * width - small.shape[0])).reshape(8, width)


def vectors_of(all_small, rows):
    layers, width = all_small.shape[0], all_small.shape[-1]
    flat = all_small.reshape(layers, -1, 8 * width).astype(jnp.float32)
    even = flat[:, :, : 8 * rows].reshape(layers, -1, 8, rows).transpose(0, 2, 1, 3)
    up = flat[:, :, 8 * rows : 12 * rows]
    return jnp.concatenate([even.reshape(layers, 8, width), up.reshape(layers, 4, width)], axis=1)


def forward(hidden, act_in, w, mask, layer_at):
    square, down, vectors = w
    qkv, ctx, stat, normed = attn_fwd(hidden, square, vectors, mask, layer_at)
    up, out, out_low, fnorm, fstat = mlp_fwd(normed, square, down, vectors, layer_at)
    return out, out_low, (act_in, qkv, ctx, stat, normed, up, fnorm, fstat)


def backward(grad, kept, w, mask, layer_at):
    square, down, vectors = w
    act_in, qkv, ctx, stat, normed, up, fnorm, fstat = kept
    dwu, dwd, grad_a, vec = mlp_bwd(
        grad, fnorm, fstat, normed, stat, up, square, down, vectors, layer_at
    )
    dqkv, grad_in, low_a, vec = attn_bwd(grad_a, qkv, stat, mask, square, vec, layer_at)
    return grad_in, (attn_dw(act_in, dqkv, ctx, low_a), dwu, dwd, vec)


def to_send(sizes, grads, rows):
    dws, dwu, dwd = grads
    width = dwd.shape[-1]
    split = lambda t: t.reshape((4,) + sizes + (rows, width))
    return split(dws), split(dwu), dwd.reshape(sizes + (4, rows, width))


def shift_down(rows, amount):
    doubled = jnp.concatenate([jnp.zeros_like(rows), rows], axis=0)
    return lax.dynamic_slice_in_dim(doubled, rows.shape[0] - amount, rows.shape[0], 0)


def shift_up(rows, amount):
    doubled = jnp.concatenate([rows, jnp.zeros_like(rows)], axis=0)
    return lax.dynamic_slice_in_dim(doubled, amount, rows.shape[0], 0)


def pack_bin(slots, first_len, second_len):
    positions = jnp.arange(slots.shape[1])[:, None]
    later = shift_down(jnp.where(positions < second_len, slots[1], 0), first_len)
    return jnp.where(positions < first_len, slots[0], later)


def unpack_bin(rows, first_len, second_len):
    positions = jnp.arange(rows.shape[0])[:, None]
    first = jnp.where(positions < first_len, rows, 0)
    second = jnp.where(positions < second_len, shift_up(rows, first_len), 0)
    return jnp.stack([first, second])


def per_device(tokens_in, cotangent, lengths, bin_deal, random_blocks, *weights):
    names = ("wqkv", "bq", "bv", "wo", "bo", "ga", "ba", "wu", "bu", "wd", "bd", "gf", "bf")
    p = dict(zip(names, weights))
    rows = p["wo"].shape[1]
    members = lax.axis_size("fsdp")
    member = lax.axis_index("fsdp")
    group_at = lax.axis_index("dp")
    grid = Grid(lax.axis_size("dp"), members)
    slot_count = 2 * members
    slot_ids = jnp.arange(slot_count)
    deal_here = lax.dynamic_index_in_dim(bin_deal, group_at, 1, keepdims=False)
    slot_hits = (deal_here[:, :, None] == slot_ids[None, None, :]).astype(jnp.int32)
    source_of = jnp.sum(slot_hits * slot_ids[None, :, None], axis=1)
    lengths_here = lax.dynamic_slice_in_dim(lengths, group_at * slot_count, slot_count, 1)
    bin_lengths = jnp.take_along_axis(lengths_here, source_of, axis=1)
    random_here = lax.dynamic_slice_in_dim(random_blocks, group_at * slot_count, slot_count, 1)
    batch_count, unused_slots, rows_dev, width = tokens_in.shape
    bin_len = rows_dev * members
    order_index = source_of[:, :, None, None]

    def dealt(array):
        sent = jnp.take_along_axis(array, order_index, axis=1)
        return sent.reshape(batch_count, members, 2, rows_dev, width)

    blocks = lambda w: w.reshape(LAYERS, rows, -1, width).transpose(0, 2, 1, 3)
    square = jnp.concatenate([blocks(p["wqkv"]), blocks(p["wo"]), blocks(p["wu"])], axis=1)
    down = p["wd"].reshape(LAYERS, -1, rows, width)
    small = jnp.stack([small_rows(p, layer_at, width) for layer_at in range(LAYERS)])
    sent_grad = dealt(cotangent)
    got_x, *gathered = bring(grid.sizes, dealt(tokens_in), square, down, small)
    got_x, sent_grad = lax.optimization_barrier((got_x, sent_grad))
    arrived_x = got_x.reshape(batch_count, 2, bin_len, width)
    arrived_grad = lax.all_to_all(
        sent_grad, "fsdp", split_axis=1, concat_axis=3, tiled=True
    )[:, 0]
    square, down, small = gathered
    side = rows * grid.count
    w = (
        square.reshape(LAYERS, -1, side, width),
        down.reshape(LAYERS, -1, width),
        vectors_of(small, rows),
    )
    slot_pair = lax.dynamic_slice_in_dim(bin_lengths, 2 * member, 2, 1)
    random_pair = lax.dynamic_slice_in_dim(random_here, 2 * member, 2, 1)
    allowed = jax.vmap(bin_mask)(slot_pair[:, 0], slot_pair[:, 1], random_pair)
    first_len = slot_pair[:, 0] * BLOCK
    second_len = slot_pair[:, 1] * BLOCK

    def packed(slots):
        bins = [pack_bin(slots[m], first_len[m], second_len[m]) for m in range(batch_count)]
        return jnp.concatenate(bins, axis=0)

    def to_slots(bins):
        bins = bins.reshape(batch_count, bin_len, width)
        slots = [unpack_bin(bins[m], first_len[m], second_len[m]) for m in range(batch_count)]
        return jnp.stack(slots)

    def in_order(back):
        back = back.reshape(batch_count, slot_count, rows_dev, width)
        return jnp.take_along_axis(back, deal_here[:, :, None, None], axis=1)

    mask = allowed.astype(jnp.float32)
    hidden = act_in = packed(arrived_x)
    kept = []
    for layer_at in range(LAYERS):
        hidden, act_in, stored = forward(hidden, act_in, w, mask, layer_at)
        kept.append(stored)
    sent = to_slots(act_in)[:, None]
    back = lax.all_to_all(sent, "fsdp", split_axis=3, concat_axis=1, tiled=True)
    output = in_order(back)
    arrived_grad, act_in = lax.optimization_barrier((arrived_grad, act_in))
    grad = packed(arrived_grad)
    sums, vecs = [None] * LAYERS, [None] * LAYERS
    for layer_at in reversed(range(LAYERS)):
        grad, (*grads, vecs[layer_at]) = backward(grad, kept[layer_at], w, mask, layer_at)
        sums[layer_at] = to_send(grid.sizes, grads, rows)
    sent = to_slots(grad.astype(LOW)).reshape(batch_count, 2, members, rows_dev, width)
    g_square, g_down, g_vec, back = take_home(grid.sizes, sums, jnp.stack(vecs), sent)
    input_grad = in_order(back)
    beside = lambda blocks: blocks.transpose(0, 2, 1, 3).reshape(LAYERS, rows, -1)
    out = {
        "wqkv": beside(g_square[:, :3]),
        "wo": g_square[:, 3],
        "wu": beside(g_square[:, 4:]),
        "wd": g_down.reshape(LAYERS, -1, width),
    }
    place = group_at * members + member
    for at, name in enumerate(SMALL):
        values = g_vec[:, at:].reshape(LAYERS, -1) if name == "bu" else g_vec[:, at]
        count = rows * (values.shape[1] // width)
        out[name] = lax.dynamic_slice_in_dim(values, place * count, count, 1)
    return (output, input_grad) + tuple(out[name] for name in names)


def solution(mesh):
    tokens = P(None, "dp", "fsdp", None)
    matrix = P(None, AXES, None)
    vector = P(None, AXES)
    weights = (matrix, vector, vector, matrix, vector, vector, vector)
    weights += (matrix, vector, matrix, vector, vector, vector)
    return jax.shard_map(
        per_device,
        mesh=mesh,
        in_specs=(tokens, tokens, P(), P(), P()) + weights,
        out_specs=(tokens, tokens) + weights,
        check_vma=False,
    )
```

```python
import jax
import jax.numpy as jnp
from jax import lax
from jax.experimental import pallas as pl
from jax.experimental.pallas import tpu as pltpu
from jax.sharding import PartitionSpec as P

HEADS = 12
BLOCK = 64
NBLK = 6
LAYERS = 2
CORES = 2
AXES = ("dp", "fsdp")
NEG = -1000000000.0
HEAD_DIM = 64
VMEM_BYTES = 67043328


epsilon = 1e-06


def split_fsdp(count):
    inner = 1
    while (2 * inner) ** 2 <= count:
        inner *= 2
    return (count // inner, inner)


class Grid:
    def __init__(self, dp_count, fsdp_count):
        outer, inner = split_fsdp(fsdp_count)
        self.sizes = (dp_count // CORES, CORES, outer, inner)
        dp_at, fsdp_at = lax.axis_index("dp"), lax.axis_index("fsdp")
        self.at = (dp_at // CORES, dp_at % CORES, fsdp_at // inner, fsdp_at % inner)

        self.count = dp_count * fsdp_count


ALL = slice(None)
HBM = pl.BlockSpec(memory_space=pl.ANY)


class Links:
    def __init__(self, sizes, send_sem, recv_sem):
        outer, inner = sizes[2:]
        dp_at, fsdp_at = lax.axis_index("dp"), lax.axis_index("fsdp")
        self.sizes = sizes
        self.at = (dp_at // CORES, dp_at % CORES, fsdp_at // inner, fsdp_at % inner)
        self.send_sem, self.recv_sem = send_sem, recv_sem
        self.used = 0

    def device(self, place):
        return (place[0] * CORES + place[1], place[2] * self.sizes[3] + place[3])

    def along(self, axis, offset):
        place = list(self.at)
        place[axis] = (place[axis] + offset) % self.sizes[axis]
        return self.device(place)

    def plan(self, source, target, device):
        copy = pltpu.make_async_remote_copy(
            src_ref=source,
            dst_ref=target,
            send_sem=self.send_sem.at[self.used],
            recv_sem=self.recv_sem.at[self.used],
            device_id=device,
            device_id_type=pl.DeviceIdType.MESH,
        )
        self.used += 1
        return copy

    def plan_here(self, source, target):
        copy = pltpu.make_async_copy(source, target, self.recv_sem.at[self.used])
        self.used += 1
        return copy

    def start(self, source, target, device):
        copy = self.plan(source, target, device)
        copy.start()
        return copy

    def start_here(self, source, target):
        copy = self.plan_here(source, target)
        copy.start()
        return copy

    def greet(self, devices):
        barrier = pltpu.get_barrier_semaphore()
        for device in devices:
            pl.semaphore_signal(barrier, inc=1, device_id=device, device_id_type=pl.DeviceIdType.MESH)
        pl.semaphore_wait(barrier, len(devices))

    def partners(self):
        found = [self.along(axis, k) for axis in (0, 1) for k in range(1, self.sizes[axis])]
        count = self.sizes[2] * self.sizes[3]
        return found + [self.member(k) for k in range(1, count)]

    def neighbours(self):
        return [self.along(axis, k) for axis in range(4) for k in range(1, self.sizes[axis])]

    def member(self, offset):
        count = self.sizes[2] * self.sizes[3]
        flat = self.at[2] * self.sizes[3] + self.at[3]
        return (self.at[0] * CORES + self.at[1], (flat + offset) % count)


class Gather:
    def __init__(self, links, source, target, order):
        self.links, self.source, self.target, self.order = links, source, target, order
        self.sent = []
        self.across = []

    def begin(self):
        links = self.links
        spot = self.target(*links.at)
        self.own = links.start_here(self.source, spot)
        self.column = [
            links.start(self.source, spot, links.along(2, k)) for k in range(1, links.sizes[2])
        ]

    def hand_over(self, spot):
        self.across.append(self.links.start(spot, spot, self.links.along(1, 1)))

    def first(self):
        links = self.links
        x, c, o, i = links.at
        self.own.wait()
        for copy in self.column:
            copy.wait_recv()
        spot = self.target(x, c, ALL, i)
        axis = self.order[0]
        self.line = [
            links.start(spot, spot, links.along(axis, k)) for k in range(1, links.sizes[axis])
        ]
        self.hand_over(spot)

    def second(self):
        links = self.links
        x, c, o, i = links.at
        for copy in self.line:
            copy.wait_recv()
        first, second = self.order
        spot = self.target(ALL, c, ALL, i) if first == 0 else self.target(x, c, ALL, ALL)
        self.sheet = [
            links.start(spot, spot, links.along(second, k)) for k in range(1, links.sizes[second])
        ]
        for k in range(1, links.sizes[first]):
            near = (links.at[first] - k) % links.sizes[first]
            self.hand_over(
                self.target(near, c, ALL, i) if first == 0 else self.target(x, c, ALL, near)
            )

    def third(self):
        links = self.links
        c = links.at[1]
        second = self.order[1]
        for k, copy in enumerate(self.sheet, 1):
            copy.wait_recv()
            near = (links.at[second] - k) % links.sizes[second]
            self.hand_over(
                self.target(near, c, ALL, ALL) if second == 0 else self.target(ALL, c, ALL, near)
            )

    def end(self):
        for copy in self.across:
            copy.wait()
        for copy in self.column + self.line + self.sheet:
            copy.wait_send()


def deal_out(links, source, target):
    count = links.sizes[2] * links.sizes[3]
    me = links.at[2] * links.sizes[3] + links.at[3]
    spot = target.at[:, :, me]
    copies = [links.start_here(source.at[:, me], spot)]
    for k in range(1, count):
        copies.append(links.start(source.at[:, (me + k) % count], spot, links.member(k)))
    return copies


def deal_back(links, source, target):
    count = links.sizes[2] * links.sizes[3]
    me = links.at[2] * links.sizes[3] + links.at[3]
    spot = target.at[:, me]
    copies = [links.start_here(source.at[:, :, me], spot)]
    for k in range(1, count):
        copies.append(links.start(source.at[:, :, (me + k) % count], spot, links.member(k)))
    return copies


def gathers_of(links, layer_at, square, down, small, all_square, all_down, all_small):
    def of_square(start, order):
        blocks = slice(start, start + 2)
        return Gather(
            links,
            square.at[layer_at, blocks],
            lambda *place: all_square.at[(layer_at, blocks) + place],
            order,
        )

    def of_down(start, order):
        blocks = slice(start, start + 2)
        return Gather(
            links,
            down.at[layer_at, blocks],
            lambda *place: all_down.at[(layer_at,) + place + (blocks,)],
            order,
        )

    tiny = Gather(
        links, small.at[layer_at], lambda *place: all_small.at[(layer_at,) + place], (0, 3)
    )
    return [
        [tiny, of_square(0, (0, 3)), of_square(2, (3, 0))],
        [of_square(4, (0, 3)), of_square(6, (3, 0))],
        [of_down(0, (0, 3)), of_down(2, (3, 0))],
    ]


def bring_kernel(sizes, *refs):
    sent_x, square, down, small = refs[:4]
    got_x, all_square, all_down, all_small = refs[4:8]
    links = Links(sizes, *refs[8:])
    links.greet(links.partners())
    groups = []
    for layer_at in range(LAYERS):
        groups += gathers_of(
            links, layer_at, square, down, small, all_square, all_down, all_small
        )
    for group in groups:
        for item in group:
            item.begin()
    moved = deal_out(links, sent_x, got_x)
    for at in range(len(groups) + 2):
        if at < len(groups):
            for item in groups[at]:
                item.first()
        if 0 < at <= len(groups):
            for item in groups[at - 1]:
                item.second()
        if at > 1:
            for item in groups[at - 2]:
                item.third()
    for group in groups:
        for item in group:
            item.end()
    for copy in moved:
        copy.wait()


def bring(sizes, sent_x, square, down, small):
    low = jnp.bfloat16
    batch, members, two, rows, width = sent_x.shape
    r = square.shape[2]
    got = jax.ShapeDtypeStruct((batch, two, members, rows, width), low)
    outs = [
        got,
        jax.ShapeDtypeStruct((LAYERS, square.shape[1]) + sizes + (r, width), low),
        jax.ShapeDtypeStruct((LAYERS,) + sizes + (down.shape[1], r, width), low),
        jax.ShapeDtypeStruct((LAYERS,) + sizes + (8, width), low),
    ]
    per_item = 1 + sum(n - 1 for n in sizes) + 4 + sizes[0] + sizes[3]
    count = 7 * LAYERS * per_item + members
    return pl.pallas_call(
        lambda *refs: bring_kernel(sizes, *refs),
        out_shape=outs,
        in_specs=[HBM] * 4,
        out_specs=[HBM] * 4,
        scratch_shapes=[pltpu.SemaphoreType.DMA((count,)), pltpu.SemaphoreType.DMA((count,))],
        compiler_params=pltpu.CompilerParams(collective_id=0, has_side_effects=True),
        name="bring",
    )(sent_x, square, down, small)


def each(dims, body):
    total = 1
    for n in dims:
        total *= n

    def step(flat, carry):
        at = []
        for n in reversed(dims):
            at.insert(0, flat % n)
            flat = flat // n
        body(tuple(at))
        return carry

    lax.fori_loop(0, total, step, 0)


def wide(ref, at):
    return ref[at].astype(jnp.float32)


class Sum:
    def __init__(self, links, source, order, lead, bufs, out_ref, leg="both"):
        self.links, self.order, self.lead, self.leg = links, order, lead, leg
        self.sent = []
        c = links.at[1]
        late = (2, 3) if order[0] == 0 else (0, 2)
        if leg == "late":
            self.half = bufs[0]
            self.opening = [links.plan_here(source, self.half)]
        else:
            self.mine, self.theirs, self.first, self.half = bufs[:4]
            there = self.send(source(1 - c), self.theirs, 1, 1)
            self.opening = [links.plan_here(source(c), self.mine), there]
            self.moving_first = self.spread(self.mine, (0, 2, 3), order[0], self.first)
        if leg == "early":
            self.out = self.half
            self.stages = [self.add_core, self.add_first, self.nothing, self.nothing]
        else:
            self.second, self.quarter, self.last, self.out = bufs[-4:]
            self.moving_second = self.spread(self.half, late, order[1], self.second)
            self.moving_last = self.spread(self.quarter, (2,), 2, self.last)
            self.late = late
            self.stages = [self.take_up, self.add_second, self.add_last, self.nothing]
            if leg == "both":
                self.stages = [self.add_core, self.add_first, self.add_second, self.add_last]
        self.result = links.plan_here(self.out, out_ref)

    def send(self, source, target, axis, offset):
        copy = self.links.plan(source, target, self.links.along(axis, offset))
        self.sent.append(copy)
        return copy

    def begin(self):
        for copy in self.opening:
            copy.start()

    def at(self, *place):
        return (ALL,) * self.lead + place

    def spread(self, ref, axes, axis, into):
        size, me = self.links.sizes[axis], self.links.at[axis]
        found = []
        for k in range(1, size):
            place = [ALL] * len(axes)
            place[axes.index(axis)] = (me + k) % size
            found.append(self.send(ref.at[self.at(*place)], into.at[k - 1], axis, k))
        return found

    def fold(self, ref, axes, axis, arrived, into):
        size, me = self.links.sizes[axis], self.links.at[axis]
        spot = axes.index(axis) + self.lead

        def add(at):
            total = wide(ref, at[:spot] + (me,) + at[spot:])
            for k in range(size - 1):
                total = total + wide(arrived, (k,) + at)
            into[at] = total.astype(into.dtype)

        each(into.shape[:-2], add)

    def nothing(self):
        pass

    def add_core(self):
        here, there = self.opening
        here.wait()
        there.wait_recv()

        def add(at):
            self.mine[at] = (wide(self.mine, at) + wide(self.theirs, at)).astype(LOW)

        each(self.mine.shape[:-2], add)
        for copy in self.moving_first:
            copy.start()

    def add_first(self):
        for copy in self.moving_first:
            copy.wait_recv()
        self.fold(self.mine, (0, 2, 3), self.order[0], self.first, self.half)
        for copy in [self.result] if self.leg == "early" else self.moving_second:
            copy.start()

    def take_up(self):
        self.opening[0].wait()
        for copy in self.moving_second:
            copy.start()

    def add_second(self):
        for copy in self.moving_second:
            copy.wait_recv()
        self.fold(self.half, self.late, self.order[1], self.second, self.quarter)
        for copy in self.moving_last:
            copy.start()

    def add_last(self):
        for copy in self.moving_last:
            copy.wait_recv()
        self.fold(self.quarter, (2,), 2, self.last, self.out)
        self.result.start()

    def end(self):
        self.result.wait()
        for copy in self.sent:
            copy.wait_send()


class Whole:
    def __init__(self, links, source, bufs, out_ref):
        self.links, self.source, self.out_ref = links, source, out_ref
        self.held, self.arrived = bufs[:5], bufs[5:]
        self.sent = []
        self.stages = [self.stage_one, self.stage_two, self.stage_three, self.stage_four]

    def begin(self):
        self.here = self.links.start_here(self.source, self.held[0])

    def send(self, at, axis):
        self.moving = [
            self.links.start(
                self.held[at], self.arrived[at].at[k - 1], self.links.along(axis, k)
            )
            for k in range(1, self.links.sizes[axis])
        ]
        self.sent += self.moving

    def fold(self, at):
        for copy in self.moving:
            copy.wait_recv()
        total = self.held[at][...]
        for k in range(self.arrived[at].shape[0]):
            total = total + self.arrived[at][k]
        self.held[at + 1][...] = total

    def stage_one(self):
        self.here.wait()
        self.send(0, 1)

    def stage_two(self):
        self.fold(0)
        self.send(1, 0)

    def stage_three(self):
        self.fold(1)
        self.send(2, 3)

    def stage_four(self):
        self.fold(2)
        self.send(3, 2)

    def end(self):
        self.fold(3)
        result = self.links.start_here(self.held[4], self.out_ref)
        result.wait()
        for copy in self.sent:
            copy.wait_send()


def whole_buffers(sizes, shape):
    f32 = jnp.float32
    arrived = [pltpu.VMEM((sizes[axis] - 1,) + shape, f32) for axis in (1, 0, 3, 2)]
    return [pltpu.VMEM(shape, f32)] * 5 + arrived


Y_FIRST, X_FIRST = (3, 0), (0, 3)


def pair_of(kind, r, width):
    lead, tail = ((), (2, r, width)) if kind == "down" else ((2,), (r, width))
    return [(Y_FIRST, 0, lead, tail), (X_FIRST, 2, lead, tail)]


def half_shape(sizes, order, lead, tail):
    x, c, o, i = sizes
    return lead + ((x, o) if order[0] == 3 else (o, i)) + tail


def sum_buffers(sizes, order, lead, tail, leg="both"):
    x, c, o, i = sizes
    whole = lead + (x, o, i) + tail
    half = half_shape(sizes, order, lead, tail)
    quarter = lead + (o,) + tail
    early = [whole, whole, (sizes[order[0]] - 1,) + half]
    late = [(sizes[order[1]] - 1,) + quarter, quarter, (o - 1,) + lead + tail]
    shapes = (early if leg != "late" else []) + [half] + (late if leg != "early" else [])
    out = [pltpu.VMEM(lead + tail, jnp.float32)] if leg != "early" else []
    return [pltpu.VMEM(shape, LOW) for shape in shapes] + out


def sum_count(sizes):
    return 3 + sum(n - 1 for n in sizes)


def source_of_core(kind, array, start):
    blocks = slice(start, start + 2)
    if kind == "down":
        return lambda core: array.at[:, core, :, :, blocks]
    return lambda core: array.at[blocks, :, core]


class Rider:
    def __init__(self, sizes, r, width, legs, steps, number):
        self.sizes, self.legs, self.steps, self.number = sizes, legs, steps, number
        self.items = [(kind, leg, *item) for kind, leg in legs for item in pair_of(kind, r, width)]
        self.outs, self.scratch, self.inputs = [], [], 0
        for kind, leg in legs:
            self.inputs += 2 if leg == "late" else 1
            if leg == "late":
                self.outs.append(jax.ShapeDtypeStruct((4, r, width), jnp.float32))
            else:
                for order, start, lead, tail in pair_of(kind, r, width):
                    self.outs.append(
                        jax.ShapeDtypeStruct(half_shape(sizes, order, lead, tail), LOW)
                    )
        count = len(self.items) * sum_count(sizes)
        self.scratch = [pltpu.SemaphoreType.DMA((count,)), pltpu.SemaphoreType.DMA((count,))]
        for kind, leg, order, start, lead, tail in self.items:
            self.scratch += sum_buffers(sizes, order, lead, tail, leg)

    def board(self, ins, outs, scratch):
        self.links = Links(self.sizes, *scratch[:2])
        scratch = list(scratch[2:])
        ins, outs = list(ins), list(outs)
        self.sums = {"early": [], "late": []}
        for kind, leg in self.legs:
            if leg == "early":
                array = ins.pop(0)
            else:
                final = outs.pop(0)
            for order, start, lead, tail in pair_of(kind, *scratch[0].shape[-2:]):
                count = 4 if leg == "early" else 5
                bufs = scratch[:count]
                del scratch[:count]
                if leg == "early":
                    source, out = source_of_core(kind, array, start), outs.pop(0)
                else:
                    source, out = ins.pop(0), final.at[start : start + 2]
                item = Sum(self.links, source, order, len(lead), bufs, out, leg)
                self.sums[leg].append(item)

    def begin(self):
        self.links.greet(self.links.neighbours())
        for item in self.sums["late"] + self.sums["early"]:
            item.begin()

    def stage(self, leg, at):
        for item in self.sums[leg]:
            item.stages[at]()

    def end(self):
        for item in self.sums["late"] + self.sums["early"]:
            item.end()

    def step(self, name):
        if name == "begin":
            self.begin()
        elif name == "end":
            self.end()
        else:
            leg, at = name
            if self.sums[leg]:
                self.stage(leg, at)

    def params(self):
        return pltpu.CompilerParams(
            collective_id=self.number, has_side_effects=True, vmem_limit_bytes=VMEM_BYTES
        )


def home_kernel(sizes, legs, *refs):
    inputs, refs = refs[: len(legs) + 1], refs[len(legs) + 1 :]
    vec, sent, late_sum, g_square, g_down, g_vec, back = refs[:7]
    links = Links(sizes, *refs[7:9])
    whole = Whole(links, vec, refs[9:18], g_vec)
    refs = list(refs[18:])
    links.greet(links.partners())
    inputs = list(inputs)
    groups = []
    for kind, leg in legs:
        if leg == "both":
            array = inputs.pop(0)
        group = []
        for order, start, lead, tail in pair_of(kind, *refs[0].shape[-2:]):
            count = 5 if leg == "late" else 8
            bufs = refs[:count]
            del refs[:count]
            blocks = slice(start, start + 2)
            if leg == "late":
                source, out = inputs.pop(0), late_sum.at[blocks]
            else:
                source = source_of_core(kind, array, start)
                out = g_down.at[blocks] if kind == "down" else None
                if out is None:
                    out = g_square.at[blocks if kind == "attn" else slice(start + 4, start + 6)]
            group.append(Sum(links, source, order, len(lead), bufs, out, leg))
        groups.append(group)
    groups[0].append(whole)
    sums = [item for group in groups for item in group]
    for item in sums:
        item.begin()
    moved = deal_back(links, sent, back)
    for turn in range(len(groups) + 3):
        for depth in range(4):
            if 0 <= turn - depth < len(groups):
                for item in groups[turn - depth]:
                    item.stages[depth]()
    for item in sums:
        item.end()
    for copy in moved:
        copy.wait()


def take_home(sizes, halves, grads, vec, sent):
    dws, dwu, dwd = grads
    r, width = dws.shape[-2:]
    legs = [("attn", "late"), ("down", "both"), ("up", "both"), ("attn", "both")]
    members = sizes[2] * sizes[3]
    f32 = jnp.float32
    batch, two, count, rows = sent.shape[:4]
    outs = [
        jax.ShapeDtypeStruct((4, r, width), f32),
        jax.ShapeDtypeStruct((8, r, width), f32),
        jax.ShapeDtypeStruct((4, r, width), f32),
        jax.ShapeDtypeStruct(vec.shape, f32),
        jax.ShapeDtypeStruct((batch, count, two, rows, width), LOW),
    ]
    args = [*halves, dwd, dwu, dws, vec, sent]
    scratch = whole_buffers(sizes, vec.shape)
    for kind, leg in legs:
        for order, start, lead, tail in pair_of(kind, r, width):
            scratch += sum_buffers(sizes, order, lead, tail, leg)
    count = (2 * len(legs) + 1) * sum_count(sizes) + members
    sems = [pltpu.SemaphoreType.DMA((count,)), pltpu.SemaphoreType.DMA((count,))]
    return pl.pallas_call(
        lambda *refs: home_kernel(sizes, legs, *refs),
        out_shape=outs,
        in_specs=[HBM] * len(args),
        out_specs=[HBM] * len(outs),
        scratch_shapes=sems + scratch,
        compiler_params=pltpu.CompilerParams(
            collective_id=1, has_side_effects=True, vmem_limit_bytes=VMEM_BYTES
        ),
        name="take_home",
    )(*args)


def bin_mask(first_blocks, second_blocks, random_pair):
    block_ids = jnp.arange(NBLK)
    later_seg = block_ids >= first_blocks
    rel_block = jnp.where(later_seg, block_ids - first_blocks, block_ids)
    seg_len = jnp.where(later_seg, second_blocks, first_blocks)
    live_block = block_ids < first_blocks + second_blocks
    rand_rows = jnp.where(
        later_seg[:, None],
        jnp.take(random_pair[1], rel_block, axis=0),
        jnp.take(random_pair[0], rel_block, axis=0),
    )
    picked = jnp.remainder(rand_rows, seg_len[:, None])
    row_rel = rel_block[:, None]
    col_rel = rel_block[None, :]
    row_len = seg_len[:, None]
    nearby = jnp.abs(row_rel - col_rel) <= 1
    global_hit = (
        (col_rel == 0) | (col_rel == row_len - 1) | (row_rel == 0) | (row_rel == row_len - 1)
    )
    random_hit = jnp.any(picked[:, :, None] == rel_block[None, None, :], axis=1)
    same_seg = (
        (later_seg[:, None] == later_seg[None, :]) & live_block[:, None] & live_block[None, :]
    )
    allowed = (nearby | global_hit | random_hit) & same_seg
    return jnp.repeat(jnp.repeat(allowed, BLOCK, axis=0), BLOCK, axis=1)


def dot(left, right):
    return jnp.dot(left, right, preferred_element_type=jnp.float32)


def dot_back(left, right):
    return lax.dot_general(left, right, (((1,), (1,)), ((), ())), preferred_element_type=jnp.float32)


def dot_weight(left, right):
    return lax.dot_general(left, right, (((0,), (0,)), ((), ())), preferred_element_type=jnp.float32)


LOW = jnp.bfloat16
LANES = 128
BQ, BV, BO, GA, BA, BD, GF, BF, BU = range(9)


def layer_norm(residual):
    center = residual - jnp.mean(residual, axis=-1, keepdims=True)
    inv_std = lax.rsqrt(jnp.mean(center * center, axis=-1, keepdims=True) + epsilon)
    return (center * inv_std, inv_std)


def norm_back(grad_out, normed, inv_std, gain):
    scaled = grad_out * gain
    return inv_std * (
        scaled
        - jnp.mean(scaled, axis=-1, keepdims=True)
        - normed * jnp.mean(scaled * normed, axis=-1, keepdims=True)
    )


def gelu_parts(u):
    root = 0.7978845608028654
    t = jnp.tanh(root * (u + 0.044715 * (u * u * u)))
    half = 0.5 * (1.0 + t)
    slope = half + 0.5 * u * (1.0 - t * t) * (root * (1.0 + 3 * 0.044715 * (u * u)))
    return (u * half, slope)


def lanes_of(pair, head):
    return pair[:, head * HEAD_DIM : (head + 1) * HEAD_DIM]


def pair_at(pair, offset=0):
    return pl.ds(pl.multiple_of(offset + pair * 2 * HEAD_DIM, 2 * HEAD_DIM), 2 * HEAD_DIM)


def lane_ids(rows):
    return lax.broadcasted_iota(jnp.int32, (rows, LANES), 1)


def attn_fwd_kernel(x_ref, w_ref, v_ref, mask_ref, qkv_ref, ctx_ref, stat_ref, normed_ref):
    rows, width = x_ref.shape
    act = x_ref[...].astype(LOW)
    for j, bias in enumerate((BQ, None, BV)):
        out = dot(act, w_ref[0, j])
        if bias is not None:
            out = out + v_ref[0, bias : bias + 1, :]
        qkv_ref[:, j * width : (j + 1) * width] = out.astype(LOW)
    scale = HEAD_DIM ** (-0.5)
    lanes = lane_ids(rows)
    stat_ref[...] = jnp.zeros_like(stat_ref)

    def pair_step(pair, carry):
        q = qkv_ref[:, pair_at(pair)]
        k = qkv_ref[:, pair_at(pair, width)]
        v = qkv_ref[:, pair_at(pair, 2 * width)]
        mixed = []
        for head in range(2):
            s = dot_back(lanes_of(q, head), lanes_of(k, head)) * scale
            s = jnp.where(mask_ref[0] > 0, s, NEG)
            top = jnp.max(s, axis=-1, keepdims=True)
            e = jnp.exp(s - top)
            total = jnp.sum(e, axis=-1, keepdims=True)
            mixed.append(dot(e.astype(LOW), lanes_of(v, head)) / total)
            log_total = top + jnp.log(total)
            stat_ref[...] = jnp.where(lanes == 2 * pair + head, log_total, stat_ref[...])
        ctx_ref[:, pair_at(pair)] = jnp.concatenate(mixed, axis=1).astype(LOW)
        return carry

    lax.fori_loop(0, HEADS // 2, pair_step, 0)
    resid = x_ref[...].astype(jnp.float32) + dot(ctx_ref[...], w_ref[0, 3])
    normed, inv = layer_norm(resid + v_ref[0, BO : BO + 1, :])
    normed_ref[...] = normed
    stat_ref[...] = jnp.where(lanes == HEADS, inv, stat_ref[...])


def attn_fwd(x, square, vectors, mask, layer_at):
    rows, width = x.shape
    bins, block = mask.shape[:2]
    row = lambda n: pl.BlockSpec((block, n), lambda b: (b, 0))
    f32 = jnp.float32
    return pl.pallas_call(
        attn_fwd_kernel,
        grid=(bins,),
        in_specs=[
            row(width),
            pl.BlockSpec((1, 4, width, width), lambda b: (layer_at, 0, 0, 0)),
            pl.BlockSpec((1,) + vectors.shape[1:], lambda b: (layer_at, 0, 0)),
            pl.BlockSpec((1, block, block), lambda b: (b, 0, 0)),
        ],
        out_specs=[row(3 * width), row(width), row(LANES), row(width)],
        out_shape=[
            jax.ShapeDtypeStruct((rows, 3 * width), LOW),
            jax.ShapeDtypeStruct((rows, width), LOW),
            jax.ShapeDtypeStruct((rows, LANES), f32),
            jax.ShapeDtypeStruct((rows, width), f32),
        ],
        name="attn_fwd",
    )(x, square, vectors, mask)


def middle_of(normed_ref, v_ref):
    return normed_ref[...] * v_ref[0, GA : GA + 1, :] + v_ref[0, BA : BA + 1, :]


def bias_up_of(v_ref, at, count):
    picked = v_ref[0, BU : BU + 1, :]
    for j in range(1, count):
        picked = jnp.where(at == j, v_ref[0, BU + j : BU + j + 1, :], picked)
    return picked


def mlp_fwd_kernel(
    count, normed_ref, wu_ref, wd_ref, v_ref, up_ref, out_ref, low_ref, fnorm_ref, stat_ref, mid, acc
):
    at = pl.program_id(0)

    @pl.when(at == 0)
    def _():
        mid[...] = middle_of(normed_ref, v_ref).astype(LOW)
        acc[...] = jnp.zeros_like(acc)

    up = dot(mid[...], wu_ref[0, 0]) + bias_up_of(v_ref, at, count)
    up_ref[...] = up
    acc[...] += dot(gelu_parts(up)[0].astype(LOW), wd_ref[0])

    @pl.when(at == count - 1)
    def _():
        resid = middle_of(normed_ref, v_ref) + acc[...] + v_ref[0, BD : BD + 1, :]
        normed, inv = layer_norm(resid)
        fnorm_ref[...] = normed
        stat_ref[...] = jnp.broadcast_to(inv, stat_ref.shape)
        out = normed * v_ref[0, GF : GF + 1, :] + v_ref[0, BF : BF + 1, :]
        out_ref[...] = out
        low_ref[...] = out.astype(LOW)


def mlp_fwd(normed, square, down, vectors, layer_at):
    rows, width = normed.shape
    count = down.shape[1] // width
    whole = lambda n: pl.BlockSpec((rows, n), lambda j: (0, 0))
    f32 = jnp.float32
    return pl.pallas_call(
        lambda *refs: mlp_fwd_kernel(count, *refs),
        grid=(count,),
        in_specs=[
            whole(width),
            pl.BlockSpec((1, 1, width, width), lambda j: (layer_at, 4 + j, 0, 0)),
            pl.BlockSpec((1, width, width), lambda j: (layer_at, j, 0)),
            pl.BlockSpec((1,) + vectors.shape[1:], lambda j: (layer_at, 0, 0)),
        ],
        out_specs=[
            pl.BlockSpec((rows, width), lambda j: (0, j)),
            whole(width),
            whole(width),
            whole(width),
            whole(LANES),
        ],
        out_shape=[
            jax.ShapeDtypeStruct((rows, count * width), f32),
            jax.ShapeDtypeStruct((rows, width), f32),
            jax.ShapeDtypeStruct((rows, width), LOW),
            jax.ShapeDtypeStruct((rows, width), f32),
            jax.ShapeDtypeStruct((rows, LANES), f32),
        ],
        scratch_shapes=[pltpu.VMEM((rows, width), LOW), pltpu.VMEM((rows, width), f32)],
        name="mlp_fwd",
    )(normed, square, down, vectors)


def sum_rows(values):
    return jnp.sum(values, axis=0, keepdims=True)


def aboard(refs, rider, ins, outs):
    if rider is None:
        return refs, lambda here, part: None
    rest = refs[ins + rider.inputs :]
    middle, last = len(rider.outs), len(rider.scratch)
    own = refs[:ins] + rest[:outs] + rest[outs + middle : len(rest) - last]
    rider.board(refs[ins : ins + rider.inputs], rest[outs : outs + middle], rest[len(rest) - last :])

    def ride(here, part):
        for grid_at, due, name in rider.steps:
            if due == part:

                @pl.when(here(grid_at))
                def _(name=name):
                    rider.step(name)

    return own, ride


def carried(rider, in_specs, out_specs, out_shape, scratch):
    if rider is not None:
        in_specs = in_specs + [HBM] * rider.inputs
        out_specs = out_specs + [HBM] * len(rider.outs)
        out_shape = out_shape + rider.outs
        scratch = scratch + rider.scratch
    found = dict(
        in_specs=in_specs, out_specs=out_specs, out_shape=out_shape, scratch_shapes=scratch
    )
    if rider is not None:
        found["compiler_params"] = rider.params()
    return found


MLP_STEPS = [
    (0, 0, "begin"),
    (0, 1, ("late", 0)),
    (0, 2, ("early", 0)),
    (1, 1, ("late", 1)),
    (3, 1, ("early", 1)),
    (3, 2, ("late", 2)),
    (3, 3, "end"),
]
ATTN_STEPS = [
    (0, 0, "begin"),
    (0, 2, ("late", 0)),
    (0, 3, ("early", 0)),
    (0, 6, ("late", 1)),
    (1, 4, ("early", 1)),
    (1, 7, ("late", 2)),
    (1, 7, "end"),
]


def mlp_bwd_kernel(count, rider, *refs):
    own, ride = aboard(refs, rider, 9, 4)
    grad_ref, fnorm_ref, fstat_ref, normed_ref, stat_ref, up_ref, wu_ref, wd_ref, v_ref = own[:9]
    dwu_ref, dwd_ref, grad_a_ref, vec_ref, mid, grad_f, low_f, acc = own[9:]
    at = pl.program_id(0)
    here = lambda step: at == step
    ride(here, 0)

    @pl.when(at == 0)
    def _():
        grad_out, normed = grad_ref[...].astype(jnp.float32), fnorm_ref[...]
        vec_ref[...] = jnp.zeros_like(vec_ref)
        vec_ref[GF : GF + 1, :] = sum_rows(grad_out * normed)
        vec_ref[BF : BF + 1, :] = sum_rows(grad_out)
        grad = norm_back(grad_out, normed, fstat_ref[:, :1], v_ref[0, GF : GF + 1, :])
        vec_ref[BD : BD + 1, :] = sum_rows(grad)
        grad_f[...] = grad
        low_f[...] = grad.astype(LOW)
        mid[...] = middle_of(normed_ref, v_ref).astype(LOW)
        acc[...] = jnp.zeros_like(acc)

    act, slope = gelu_parts(up_ref[...])
    dwd_ref[...] = dot_weight(act.astype(LOW), low_f[...]).astype(LOW)
    ride(here, 1)
    grad_up = dot_back(low_f[...], wd_ref[0]) * slope
    vec_ref[pl.ds(BU + at, 1), :] = sum_rows(grad_up)
    low_up = grad_up.astype(LOW)
    dwu_ref[0] = dot_weight(mid[...], low_up).astype(LOW)
    acc[...] += dot_back(low_up, wu_ref[0, 0])
    ride(here, 2)

    @pl.when(at == count - 1)
    def _():
        grad_mid, normed = grad_f[...] + acc[...], normed_ref[...]
        vec_ref[GA : GA + 1, :] = sum_rows(grad_mid * normed)
        vec_ref[BA : BA + 1, :] = sum_rows(grad_mid)
        inv = stat_ref[:, HEADS : HEADS + 1]
        grad = norm_back(grad_mid, normed, inv, v_ref[0, GA : GA + 1, :])
        vec_ref[BO : BO + 1, :] = sum_rows(grad)
        grad_a_ref[...] = grad

    ride(here, 3)


def mlp_bwd(
    grad, fnorm, fstat, normed, stat, up, square, down, vectors, layer_at, rider=None, load=()
):
    rows, width = normed.shape
    count = down.shape[1] // width
    whole = lambda n: pl.BlockSpec((rows, n), lambda j: (0, 0))
    f32 = jnp.float32
    vec_rows = vectors.shape[1]
    in_specs = [
        whole(width),
        whole(width),
        whole(LANES),
        whole(width),
        whole(LANES),
        pl.BlockSpec((rows, width), lambda j: (0, j)),
        pl.BlockSpec((1, 1, width, width), lambda j: (layer_at, 4 + j, 0, 0)),
        pl.BlockSpec((1, width, width), lambda j: (layer_at, j, 0)),
        pl.BlockSpec((1, vec_rows, width), lambda j: (layer_at, 0, 0)),
    ]
    out_specs = [
        pl.BlockSpec((1, width, width), lambda j: (j, 0, 0)),
        pl.BlockSpec((width, width), lambda j: (j, 0)),
        whole(width),
        pl.BlockSpec((vec_rows, width), lambda j: (0, 0)),
    ]
    out_shape = [
        jax.ShapeDtypeStruct((count, width, width), LOW),
        jax.ShapeDtypeStruct((count * width, width), LOW),
        jax.ShapeDtypeStruct((rows, width), f32),
        jax.ShapeDtypeStruct((vec_rows, width), f32),
    ]
    scratch = [
        pltpu.VMEM((rows, width), LOW),
        pltpu.VMEM((rows, width), f32),
        pltpu.VMEM((rows, width), LOW),
        pltpu.VMEM((rows, width), f32),
    ]
    return pl.pallas_call(
        lambda *refs: mlp_bwd_kernel(count, rider, *refs),
        grid=(count,),
        name="mlp_bwd" if rider is None else "mlp_bwd_sums",
        **carried(rider, in_specs, out_specs, out_shape, scratch),
    )(grad, fnorm, fstat, normed, stat, up, square, down, vectors, *load)


def attn_bwd_kernel(rider, *refs):
    own, ride = aboard(refs, rider, 6, 4)
    grad_ref, qkv_ref, stat_ref, mask_ref, w_ref, vec_in = own[:6]
    dqkv_ref, grad_in_ref, low_ref, vec_ref, gctx = own[6:]
    rows, width = grad_ref.shape
    bin_at = pl.program_id(0)
    ride(lambda step: bin_at == step, 0)

    @pl.when(pl.program_id(0) == 0)
    def _():
        vec_ref[...] = vec_in[...]

    low_ref[...] = grad_ref[...].astype(LOW)
    gctx[...] = dot_back(low_ref[...], w_ref[0, 3]).astype(LOW)
    scale = HEAD_DIM ** (-0.5)
    lanes = lane_ids(rows)

    def pair_step(pair, carry):
        for part in range(HEADS // 2):
            ride(lambda step: (bin_at == step) & (pair == part), 1 + part)
        q = qkv_ref[:, pair_at(pair)]
        k = qkv_ref[:, pair_at(pair, width)]
        v = qkv_ref[:, pair_at(pair, 2 * width)]
        g = gctx[:, pair_at(pair)]
        grads = [[], [], []]
        for head in range(2):
            qh, kh, vh, gh = (lanes_of(t, head) for t in (q, k, v, g))
            log_total = jnp.sum(
                jnp.where(lanes == 2 * pair + head, stat_ref[...], 0.0), axis=-1, keepdims=True
            )
            s = dot_back(qh, kh) * scale
            s = jnp.where(mask_ref[0] > 0, s, NEG)
            p = jnp.exp(s - log_total)
            grad_p = dot_back(gh, vh)
            inner = jnp.sum(grad_p * p, axis=-1, keepdims=True)
            low_s = (p * (grad_p - inner)).astype(LOW)
            grads[0].append(dot(low_s, kh) * scale)
            grads[1].append(dot_weight(low_s, qh) * scale)
            grads[2].append(dot_weight(p.astype(LOW), gh))
        for j, row in ((0, BQ), (1, None), (2, BV)):
            both = jnp.concatenate(grads[j], axis=1)
            dqkv_ref[:, pair_at(pair, j * width)] = both.astype(LOW)
            if row is not None:
                vec_ref[row : row + 1, pair_at(pair)] += sum_rows(both)
        return carry

    lax.fori_loop(0, HEADS // 2, pair_step, 0)
    total = grad_ref[...]
    for j in range(3):
        total = total + dot_back(dqkv_ref[:, j * width : (j + 1) * width], w_ref[0, j])
    grad_in_ref[...] = total
    ride(lambda step: bin_at == step, 1 + HEADS // 2)


def attn_bwd(grad_a, qkv, stat, mask, square, vec, layer_at, rider=None, load=()):
    rows, width = grad_a.shape
    bins, block = mask.shape[:2]
    row = lambda n: pl.BlockSpec((block, n), lambda b: (b, 0))
    fixed = pl.BlockSpec(vec.shape, lambda b: (0, 0))
    f32 = jnp.float32
    in_specs = [
        row(width),
        row(3 * width),
        row(LANES),
        pl.BlockSpec((1, block, block), lambda b: (b, 0, 0)),
        pl.BlockSpec((1, 4, width, width), lambda b: (layer_at, 0, 0, 0)),
        fixed,
    ]
    out_shape = [
        jax.ShapeDtypeStruct((rows, 3 * width), LOW),
        jax.ShapeDtypeStruct((rows, width), f32),
        jax.ShapeDtypeStruct((rows, width), LOW),
        jax.ShapeDtypeStruct(vec.shape, f32),
    ]
    out_specs = [row(3 * width), row(width), row(width), fixed]
    scratch = [pltpu.VMEM((block, width), LOW)]
    return pl.pallas_call(
        lambda *refs: attn_bwd_kernel(rider, *refs),
        grid=(bins,),
        name=f"attn_bwd_sums{rider.number}",
        **carried(rider, in_specs, out_specs, out_shape, scratch),
    )(grad_a, qkv, stat, mask, square, vec, *load)


def attn_dw_kernel(act_ref, dqkv_ref, ctx_ref, low_ref, out_ref):
    at = pl.program_id(0)

    @pl.when(at < 3)
    def _():
        out_ref[0] = dot_weight(act_ref[...].astype(LOW), dqkv_ref[...]).astype(LOW)

    @pl.when(at == 3)
    def _():
        out_ref[0] = dot_weight(ctx_ref[...], low_ref[...]).astype(LOW)


def attn_dw(act, dqkv, ctx, low):
    rows, width = act.shape
    whole = pl.BlockSpec((rows, width), lambda j: (0, 0))
    return pl.pallas_call(
        attn_dw_kernel,
        grid=(4,),
        in_specs=[
            whole,
            pl.BlockSpec((rows, width), lambda j: (0, jnp.minimum(j, 2))),
            whole,
            whole,
        ],
        out_specs=pl.BlockSpec((1, width, width), lambda j: (j, 0, 0)),
        out_shape=jax.ShapeDtypeStruct((4, width, width), LOW),
        name="attn_dw",
    )(act, dqkv, ctx, low)


SMALL = ("bq", "bv", "bo", "ga", "ba", "bd", "gf", "bf", "bu")


def small_rows(p, layer_at, width):
    small = jnp.concatenate([p[name][layer_at] for name in SMALL])
    return jnp.pad(small, (0, 8 * width - small.shape[0])).reshape(8, width)


def vectors_of(all_small, rows):
    layers, width = all_small.shape[0], all_small.shape[-1]
    flat = all_small.reshape(layers, -1, 8 * width).astype(jnp.float32)
    even = flat[:, :, : 8 * rows].reshape(layers, -1, 8, rows).transpose(0, 2, 1, 3)
    up = flat[:, :, 8 * rows : 12 * rows]
    return jnp.concatenate([even.reshape(layers, 8, width), up.reshape(layers, 4, width)], axis=1)


def forward(hidden, act_in, w, mask, layer_at):
    square, down, vectors = w
    qkv, ctx, stat, normed = attn_fwd(hidden, square, vectors, mask, layer_at)
    up, out, out_low, fnorm, fstat = mlp_fwd(normed, square, down, vectors, layer_at)
    return out, out_low, (act_in, qkv, ctx, stat, normed, up, fnorm, fstat)


def backward_layers(grad, back, kept, w, mask, sizes, rows):
    square, down, vectors = w
    width = square.shape[-1]

    def of_mlp(grad, layer_at, *more):
        act_in, qkv, ctx, stat, normed, up, fnorm, fstat = kept[layer_at]
        return mlp_bwd(
            grad, fnorm, fstat, normed, stat, up, square, down, vectors, layer_at, *more
        )

    def of_attn(grad_a, vec, layer_at, *more):
        act_in, qkv, ctx, stat, *unused = kept[layer_at]
        dqkv, grad_in, low_a, vec, *sums = attn_bwd(
            grad_a, qkv, stat, mask, square, vec, layer_at, *more
        )
        return grad_in, attn_dw(act_in, dqkv, ctx, low_a), vec, sums

    blocks_out = lambda t: t.reshape((4,) + sizes + (rows, width))
    rows_out = lambda t: t.reshape(sizes + (4, rows, width))
    dwu, dwd, grad_a, vec = of_mlp(grad, 1)
    rider = Rider(sizes, rows, width, [("down", "early")], ATTN_STEPS, 2)
    grad, dws, vec_late, halves = of_attn(grad_a, vec, 1, rider, [rows_out(dwd)])
    grad, back = lax.optimization_barrier((grad, back))
    rider = Rider(sizes, rows, width, [("down", "late"), ("up", "early")], MLP_STEPS, 3)
    dwu, dwd, grad_a, vec, g_down, *halves = of_mlp(grad, 0, rider, [*halves, blocks_out(dwu)])
    rider = Rider(sizes, rows, width, [("up", "late"), ("attn", "early")], ATTN_STEPS, 4)
    grad, dws, vec, (g_up, *halves) = of_attn(grad_a, vec, 0, rider, [*halves, blocks_out(dws)])
    left = (blocks_out(dws), blocks_out(dwu), rows_out(dwd))
    return grad, back, (g_up, g_down), (halves, left, jnp.stack([vec, vec_late]))


def shift_down(rows, amount):
    doubled = jnp.concatenate([jnp.zeros_like(rows), rows], axis=0)
    return lax.dynamic_slice_in_dim(doubled, rows.shape[0] - amount, rows.shape[0], 0)


def shift_up(rows, amount):
    doubled = jnp.concatenate([rows, jnp.zeros_like(rows)], axis=0)
    return lax.dynamic_slice_in_dim(doubled, amount, rows.shape[0], 0)


def pack_bin(slots, first_len, second_len):
    positions = jnp.arange(slots.shape[1])[:, None]
    later = shift_down(jnp.where(positions < second_len, slots[1], 0), first_len)
    return jnp.where(positions < first_len, slots[0], later)


def unpack_bin(rows, first_len, second_len):
    positions = jnp.arange(rows.shape[0])[:, None]
    first = jnp.where(positions < first_len, rows, 0)
    second = jnp.where(positions < second_len, shift_up(rows, first_len), 0)
    return jnp.stack([first, second])


def per_device(tokens_in, cotangent, lengths, bin_deal, random_blocks, *weights):
    names = ("wqkv", "bq", "bv", "wo", "bo", "ga", "ba", "wu", "bu", "wd", "bd", "gf", "bf")
    p = dict(zip(names, weights))
    rows = p["wo"].shape[1]
    members = lax.axis_size("fsdp")
    member = lax.axis_index("fsdp")
    group_at = lax.axis_index("dp")
    grid = Grid(lax.axis_size("dp"), members)
    slot_count = 2 * members
    slot_ids = jnp.arange(slot_count)
    deal_here = lax.dynamic_index_in_dim(bin_deal, group_at, 1, keepdims=False)
    slot_hits = (deal_here[:, :, None] == slot_ids[None, None, :]).astype(jnp.int32)
    source_of = jnp.sum(slot_hits * slot_ids[None, :, None], axis=1)
    lengths_here = lax.dynamic_slice_in_dim(lengths, group_at * slot_count, slot_count, 1)
    bin_lengths = jnp.take_along_axis(lengths_here, source_of, axis=1)
    random_here = lax.dynamic_slice_in_dim(random_blocks, group_at * slot_count, slot_count, 1)
    batch_count, unused_slots, rows_dev, width = tokens_in.shape
    bin_len = rows_dev * members
    order_index = source_of[:, :, None, None]

    def dealt(array):
        sent = jnp.take_along_axis(array, order_index, axis=1)
        return sent.reshape(batch_count, members, 2, rows_dev, width)

    blocks = lambda w: w.reshape(LAYERS, rows, -1, width).transpose(0, 2, 1, 3)
    square = jnp.concatenate([blocks(p["wqkv"]), blocks(p["wo"]), blocks(p["wu"])], axis=1)
    down = p["wd"].reshape(LAYERS, -1, rows, width)
    small = jnp.stack([small_rows(p, layer_at, width) for layer_at in range(LAYERS)])
    sent_grad = dealt(cotangent)
    got_x, *gathered = bring(grid.sizes, dealt(tokens_in), square, down, small)
    got_x, sent_grad = lax.optimization_barrier((got_x, sent_grad))
    arrived_x = got_x.reshape(batch_count, 2, bin_len, width)
    arrived_grad = lax.all_to_all(
        sent_grad, "fsdp", split_axis=1, concat_axis=3, tiled=True
    )[:, 0]
    square, down, small = gathered
    side = rows * grid.count
    w = (
        square.reshape(LAYERS, -1, side, width),
        down.reshape(LAYERS, -1, width),
        vectors_of(small, rows),
    )
    slot_pair = lax.dynamic_slice_in_dim(bin_lengths, 2 * member, 2, 1)
    random_pair = lax.dynamic_slice_in_dim(random_here, 2 * member, 2, 1)
    allowed = jax.vmap(bin_mask)(slot_pair[:, 0], slot_pair[:, 1], random_pair)
    first_len = slot_pair[:, 0] * BLOCK
    second_len = slot_pair[:, 1] * BLOCK

    def packed(slots):
        bins = [pack_bin(slots[m], first_len[m], second_len[m]) for m in range(batch_count)]
        return jnp.concatenate(bins, axis=0)

    def to_slots(bins):
        bins = bins.reshape(batch_count, bin_len, width)
        slots = [unpack_bin(bins[m], first_len[m], second_len[m]) for m in range(batch_count)]
        return jnp.stack(slots)

    def in_order(back):
        back = back.reshape(batch_count, slot_count, rows_dev, width)
        return jnp.take_along_axis(back, deal_here[:, :, None, None], axis=1)

    mask = allowed.astype(jnp.float32)
    hidden = act_in = packed(arrived_x)
    kept = []
    for layer_at in range(LAYERS):
        hidden, act_in, stored = forward(hidden, act_in, w, mask, layer_at)
        kept.append(stored)
    sent = to_slots(act_in)[:, None]
    back = lax.all_to_all(sent, "fsdp", split_axis=3, concat_axis=1, tiled=True)
    arrived_grad, act_in = lax.optimization_barrier((arrived_grad, act_in))
    grad = packed(arrived_grad)
    grad, back, (g_up, g_down_late), left = backward_layers(grad, back, kept, w, mask, grid.sizes, rows)
    output = in_order(back)
    sent = to_slots(grad.astype(LOW)).reshape(batch_count, 2, members, rows_dev, width)
    g_attn, g_square, g_down, g_vec, back = take_home(grid.sizes, *left, sent)
    input_grad = in_order(back)
    beside = lambda *pairs: jnp.stack(
        [blocks.transpose(1, 0, 2).reshape(rows, -1) for blocks in pairs]
    )
    out = {
        "wqkv": beside(g_square[:3], g_attn[:3]),
        "wo": jnp.stack([g_square[3], g_attn[3]]),
        "wu": beside(g_square[4:], g_up),
        "wd": jnp.stack([g_down.reshape(-1, width), g_down_late.reshape(-1, width)]),
    }
    place = group_at * members + member
    for at, name in enumerate(SMALL):
        values = g_vec[:, at:].reshape(LAYERS, -1) if name == "bu" else g_vec[:, at]
        count = rows * (values.shape[1] // width)
        out[name] = lax.dynamic_slice_in_dim(values, place * count, count, 1)
    return (output, input_grad) + tuple(out[name] for name in names)


def solution(mesh):
    tokens = P(None, "dp", "fsdp", None)
    matrix = P(None, AXES, None)
    vector = P(None, AXES)
    weights = (matrix, vector, vector, matrix, vector, vector, vector)
    weights += (matrix, vector, matrix, vector, vector, vector)
    return jax.shard_map(
        per_device,
        mesh=mesh,
        in_specs=(tokens, tokens, P(), P(), P()) + weights,
        out_specs=(tokens, tokens) + weights,
        check_vma=False,
    )
```

```python
import jax
import jax.numpy as jnp
from jax import lax
from jax.experimental import pallas as pl
from jax.experimental.pallas import tpu as pltpu
from jax.sharding import PartitionSpec as P

HEADS = 12
BLOCK = 64
NBLK = 6
LAYERS = 2
CORES = 2
AXES = ("dp", "fsdp")
NEG = -1000000000.0
HEAD_DIM = 64
VMEM_BYTES = 67043328
DEAL_TURNS = 8


epsilon = 1e-06


def split_fsdp(count):
    inner = 1
    while (2 * inner) ** 2 <= count:
        inner *= 2
    return (count // inner, inner)


class Grid:
    def __init__(self, dp_count, fsdp_count):
        outer, inner = split_fsdp(fsdp_count)
        self.sizes = (dp_count // CORES, CORES, outer, inner)
        dp_at, fsdp_at = lax.axis_index("dp"), lax.axis_index("fsdp")
        self.at = (dp_at // CORES, dp_at % CORES, fsdp_at // inner, fsdp_at % inner)

        self.count = dp_count * fsdp_count


ALL = slice(None)
HBM = pl.BlockSpec(memory_space=pl.ANY)


class Links:
    def __init__(self, sizes, send_sem, recv_sem):
        outer, inner = sizes[2:]
        dp_at, fsdp_at = lax.axis_index("dp"), lax.axis_index("fsdp")
        self.sizes = sizes
        self.at = (dp_at // CORES, dp_at % CORES, fsdp_at // inner, fsdp_at % inner)
        self.send_sem, self.recv_sem = send_sem, recv_sem
        self.used = 0

    def device(self, place):
        return (place[0] * CORES + place[1], place[2] * self.sizes[3] + place[3])

    def along(self, axis, offset):
        place = list(self.at)
        place[axis] = (place[axis] + offset) % self.sizes[axis]
        return self.device(place)

    def plan(self, source, target, device):
        copy = pltpu.make_async_remote_copy(
            src_ref=source,
            dst_ref=target,
            send_sem=self.send_sem.at[self.used],
            recv_sem=self.recv_sem.at[self.used],
            device_id=device,
            device_id_type=pl.DeviceIdType.MESH,
        )
        self.used += 1
        return copy

    def plan_here(self, source, target):
        copy = pltpu.make_async_copy(source, target, self.recv_sem.at[self.used])
        self.used += 1
        return copy

    def start(self, source, target, device):
        copy = self.plan(source, target, device)
        copy.start()
        return copy

    def start_here(self, source, target):
        copy = self.plan_here(source, target)
        copy.start()
        return copy

    def greet(self, devices):
        barrier = pltpu.get_barrier_semaphore()
        for device in devices:
            pl.semaphore_signal(barrier, inc=1, device_id=device, device_id_type=pl.DeviceIdType.MESH)
        pl.semaphore_wait(barrier, len(devices))

    def partners(self):
        found = [self.along(axis, k) for axis in (0, 1) for k in range(1, self.sizes[axis])]
        count = self.sizes[2] * self.sizes[3]
        return found + [self.member(k) for k in range(1, count)]

    def neighbours(self):
        return [self.along(axis, k) for axis in range(4) for k in range(1, self.sizes[axis])]

    def member(self, offset):
        count = self.sizes[2] * self.sizes[3]
        flat = self.at[2] * self.sizes[3] + self.at[3]
        return (self.at[0] * CORES + self.at[1], (flat + offset) % count)


class Gather:
    def __init__(self, links, source, target, order):
        self.links, self.source, self.target, self.order = links, source, target, order
        self.sent = []
        self.across = []

    def begin(self):
        links = self.links
        x, c, o, i = links.at
        spot = self.target(*links.at)
        self.own = links.start_here(self.source, spot)
        if links.sizes[2] != 4:
            self.column = [
                links.start(self.source, spot, links.along(2, k)) for k in range(1, links.sizes[2])
            ]
            return
        self.inside = (o == 1) | (o == 2)
        near = links.device((x, c, o + 1 - 2 * (o % 2), i))
        across = links.device((x, c, 3 - o, i))
        pair = lambda half: self.target(x, c, pl.ds(2 * half, 2), i)
        ours, others = pair(o // 2), pair(1 - o // 2)
        self.column = [links.start(self.source, spot, near)]
        self.pairs = links.plan(ours, ours, across)
        self.outwards = links.plan(others, others, near)

    def cross(self):
        if self.links.sizes[2] != 4:
            return
        self.own.wait()
        self.column[0].wait_recv()

        @pl.when(self.inside)
        def _():
            self.pairs.start()

    def spread(self):
        if self.links.sizes[2] != 4:
            return

        @pl.when(self.inside)
        def _():
            self.pairs.wait_recv()
            self.outwards.start()

    def hand_over(self, spot):
        self.across.append(self.links.start(spot, spot, self.links.along(1, 1)))

    def first(self):
        links = self.links
        x, c, o, i = links.at
        if links.sizes[2] != 4:
            self.own.wait()
            for copy in self.column:
                copy.wait_recv()
        else:

            @pl.when(~self.inside)
            def _():
                self.outwards.wait_recv()

        spot = self.target(x, c, ALL, i)
        axis = self.order[0]
        self.line = [
            links.start(spot, spot, links.along(axis, k)) for k in range(1, links.sizes[axis])
        ]
        self.hand_over(spot)

    def second(self):
        links = self.links
        x, c, o, i = links.at
        for copy in self.line:
            copy.wait_recv()
        first, second = self.order
        spot = self.target(ALL, c, ALL, i) if first == 0 else self.target(x, c, ALL, ALL)
        self.sheet = [
            links.start(spot, spot, links.along(second, k)) for k in range(1, links.sizes[second])
        ]
        for k in range(1, links.sizes[first]):
            near = (links.at[first] - k) % links.sizes[first]
            self.hand_over(
                self.target(near, c, ALL, i) if first == 0 else self.target(x, c, ALL, near)
            )

    def third(self):
        links = self.links
        c = links.at[1]
        second = self.order[1]
        for k, copy in enumerate(self.sheet, 1):
            copy.wait_recv()
            near = (links.at[second] - k) % links.sizes[second]
            self.hand_over(
                self.target(near, c, ALL, ALL) if second == 0 else self.target(ALL, c, ALL, near)
            )

    def end(self):
        for copy in self.across:
            copy.wait()
        for copy in self.column + self.line + self.sheet:
            copy.wait_send()
        if self.links.sizes[2] == 4:

            @pl.when(self.inside)
            def _():
                self.pairs.wait_send()
                self.outwards.wait_send()


def deal_out(links, source, target):
    count = links.sizes[2] * links.sizes[3]
    me = links.at[2] * links.sizes[3] + links.at[3]
    spot = target.at[:, :, me]
    starts = [
        lambda k=k: links.start(source.at[:, (me + k) % count], spot, links.member(k))
        for k in range(1, count)
    ]
    return starts + [lambda: links.start_here(source.at[:, me], spot)]


def deal_back(links, source, target):
    count = links.sizes[2] * links.sizes[3]
    me = links.at[2] * links.sizes[3] + links.at[3]
    spot = target.at[:, me]
    copies = [links.start_here(source.at[:, :, me], spot)]
    for k in range(1, count):
        copies.append(links.start(source.at[:, :, (me + k) % count], spot, links.member(k)))
    return copies


def gathers_of(links, layer_at, square, down, small, all_square, all_down, all_small):
    def of_square(start, order):
        blocks = slice(start, start + 2)
        return Gather(
            links,
            square.at[layer_at, blocks],
            lambda *place: all_square.at[(layer_at, blocks) + place],
            order,
        )

    def of_down(start, order):
        blocks = slice(start, start + 2)
        return Gather(
            links,
            down.at[layer_at, blocks],
            lambda *place: all_down.at[(layer_at,) + place + (blocks,)],
            order,
        )

    tiny = Gather(
        links, small.at[layer_at], lambda *place: all_small.at[(layer_at,) + place], (0, 3)
    )
    return [
        [tiny, of_square(0, (0, 3)), of_square(2, (3, 0))],
        [of_square(4, (0, 3)), of_square(6, (3, 0))],
        [of_down(0, (3, 0)), of_down(2, (3, 0))],
    ]


def bring_kernel(sizes, *refs):
    sent_x, square, down, small = refs[:4]
    got_x, all_square, all_down, all_small = refs[4:8]
    links = Links(sizes, *refs[8:])
    links.greet(links.partners())
    groups = []
    for layer_at in range(LAYERS):
        groups += gathers_of(
            links, layer_at, square, down, small, all_square, all_down, all_small
        )
    starts = deal_out(links, sent_x, got_x)
    share = -(-len(starts) // DEAL_TURNS)
    moved = []

    def run(step, at):
        if 0 <= at < len(groups):
            for item in groups[at]:
                getattr(item, step)()

    run("begin", 0)
    run("begin", 1)
    run("cross", 0)
    run("spread", 0)
    run("cross", 1)
    run("begin", 2)
    for at in range(len(groups) + 2):
        run("first", at)
        run("spread", at + 1)
        run("cross", at + 2)
        run("begin", at + 3)
        moved += [start() for start in starts[at * share : (at + 1) * share]]
        run("second", at - 1)
        run("third", at - 2)
    for group in groups:
        for item in group:
            item.end()
    for copy in moved:
        copy.wait()


def bring(sizes, sent_x, square, down, small):
    low = jnp.bfloat16
    batch, members, two, rows, width = sent_x.shape
    r = square.shape[2]
    got = jax.ShapeDtypeStruct((batch, two, members, rows, width), low)
    outs = [
        got,
        jax.ShapeDtypeStruct((LAYERS, square.shape[1]) + sizes + (r, width), low),
        jax.ShapeDtypeStruct((LAYERS,) + sizes + (down.shape[1], r, width), low),
        jax.ShapeDtypeStruct((LAYERS,) + sizes + (8, width), low),
    ]
    per_item = 3 + sum(n - 1 for n in sizes) + 4 + sizes[0] + sizes[3]
    count = 7 * LAYERS * per_item + members
    return pl.pallas_call(
        lambda *refs: bring_kernel(sizes, *refs),
        out_shape=outs,
        in_specs=[HBM] * 4,
        out_specs=[HBM] * 4,
        scratch_shapes=[pltpu.SemaphoreType.DMA((count,)), pltpu.SemaphoreType.DMA((count,))],
        compiler_params=pltpu.CompilerParams(collective_id=0, has_side_effects=True),
        name="bring",
    )(sent_x, square, down, small)


def each(dims, body):
    total = 1
    for n in dims:
        total *= n

    def step(flat, carry):
        at = []
        for n in reversed(dims):
            at.insert(0, flat % n)
            flat = flat // n
        body(tuple(at))
        return carry

    lax.fori_loop(0, total, step, 0)


def wide(ref, at):
    return ref[at].astype(jnp.float32)


class Sum:
    def __init__(self, links, source, order, lead, bufs, out_ref, leg="both"):
        self.links, self.order, self.lead, self.leg = links, order, lead, leg
        self.sent = []
        c = links.at[1]
        late = (2, 3) if order[0] == 0 else (0, 2)
        if leg == "late":
            self.half = bufs[0]
            self.opening = [links.plan_here(source, self.half)]
        else:
            self.mine, self.theirs, self.first, self.half = bufs[:4]
            there = self.send(source(1 - c), self.theirs, 1, 1)
            self.opening = [links.plan_here(source(c), self.mine), there]
            self.moving_first = self.spread(self.mine, (0, 2, 3), order[0], self.first)
        if leg == "early":
            self.out = self.half
            self.stages = [self.add_core, self.add_first, self.nothing, self.nothing]
        else:
            self.second, self.quarter, self.last, self.out = bufs[-4:]
            self.moving_second = self.spread(self.half, late, order[1], self.second)
            self.moving_last = self.spread(self.quarter, (2,), 2, self.last)
            self.late = late
            self.stages = [self.take_up, self.add_second, self.add_last, self.nothing]
            if leg == "both":
                self.stages = [self.add_core, self.add_first, self.add_second, self.add_last]
        self.result = links.plan_here(self.out, out_ref)

    def send(self, source, target, axis, offset):
        copy = self.links.plan(source, target, self.links.along(axis, offset))
        self.sent.append(copy)
        return copy

    def begin(self):
        for copy in self.opening:
            copy.start()

    def at(self, *place):
        return (ALL,) * self.lead + place

    def spread(self, ref, axes, axis, into):
        size, me = self.links.sizes[axis], self.links.at[axis]
        found = []
        for k in range(1, size):
            place = [ALL] * len(axes)
            place[axes.index(axis)] = (me + k) % size
            found.append(self.send(ref.at[self.at(*place)], into.at[k - 1], axis, k))
        return found

    def fold(self, ref, axes, axis, arrived, into):
        size, me = self.links.sizes[axis], self.links.at[axis]
        spot = axes.index(axis) + self.lead

        def add(at):
            if size == 2 and into.dtype == LOW:
                into[at] = ref[at[:spot] + (me,) + at[spot:]] + arrived[(0,) + at]
                return
            total = wide(ref, at[:spot] + (me,) + at[spot:])
            for k in range(size - 1):
                total = total + wide(arrived, (k,) + at)
            into[at] = total.astype(into.dtype)

        each(into.shape[:-2], add)

    def nothing(self):
        pass

    def add_core(self):
        here, there = self.opening
        here.wait()
        there.wait_recv()

        def add(at):
            self.mine[at] = self.mine[at] + self.theirs[at]

        each(self.mine.shape[:-2], add)
        for copy in self.moving_first:
            copy.start()

    def add_first(self):
        for copy in self.moving_first:
            copy.wait_recv()
        self.fold(self.mine, (0, 2, 3), self.order[0], self.first, self.half)
        for copy in [self.result] if self.leg == "early" else self.moving_second:
            copy.start()

    def take_up(self):
        self.opening[0].wait()
        for copy in self.moving_second:
            copy.start()

    def add_second(self):
        for copy in self.moving_second:
            copy.wait_recv()
        self.fold(self.half, self.late, self.order[1], self.second, self.quarter)
        for copy in self.moving_last:
            copy.start()

    def add_last(self):
        for copy in self.moving_last:
            copy.wait_recv()
        self.fold(self.quarter, (2,), 2, self.last, self.out)
        self.result.start()

    def end(self):
        self.result.wait()
        for copy in self.sent:
            copy.wait_send()


class Whole:
    def __init__(self, links, source, bufs, out_ref):
        self.links, self.source, self.out_ref = links, source, out_ref
        self.held, self.arrived = bufs[:5], bufs[5:]
        self.sent = []
        self.stages = [self.stage_one, self.stage_two, self.stage_three, self.stage_four]

    def begin(self):
        self.here = self.links.start_here(self.source, self.held[0])

    def send(self, at, axis):
        self.moving = [
            self.links.start(
                self.held[at], self.arrived[at].at[k - 1], self.links.along(axis, k)
            )
            for k in range(1, self.links.sizes[axis])
        ]
        self.sent += self.moving

    def fold(self, at):
        for copy in self.moving:
            copy.wait_recv()
        total = self.held[at][...]
        for k in range(self.arrived[at].shape[0]):
            total = total + self.arrived[at][k]
        self.held[at + 1][...] = total

    def stage_one(self):
        self.here.wait()
        self.send(0, 1)

    def stage_two(self):
        self.fold(0)
        self.send(1, 0)

    def stage_three(self):
        self.fold(1)
        self.send(2, 3)

    def stage_four(self):
        self.fold(2)
        self.send(3, 2)

    def end(self):
        self.fold(3)
        result = self.links.start_here(self.held[4], self.out_ref)
        result.wait()
        for copy in self.sent:
            copy.wait_send()


def whole_buffers(sizes, shape):
    f32 = jnp.float32
    arrived = [pltpu.VMEM((sizes[axis] - 1,) + shape, f32) for axis in (1, 0, 3, 2)]
    return [pltpu.VMEM(shape, f32)] * 5 + arrived


Y_FIRST, X_FIRST = (3, 0), (0, 3)


def pair_of(kind, r, width):
    lead, tail = ((), (2, r, width)) if kind == "down" else ((2,), (r, width))
    return [(Y_FIRST, 0, lead, tail), (X_FIRST, 2, lead, tail)]


def half_shape(sizes, order, lead, tail):
    x, c, o, i = sizes
    return lead + ((x, o) if order[0] == 3 else (o, i)) + tail


def sum_buffers(sizes, order, lead, tail, leg="both"):
    x, c, o, i = sizes
    whole = lead + (x, o, i) + tail
    half = half_shape(sizes, order, lead, tail)
    quarter = lead + (o,) + tail
    early = [whole, whole, (sizes[order[0]] - 1,) + half]
    late = [(sizes[order[1]] - 1,) + quarter, quarter, (o - 1,) + lead + tail]
    shapes = (early if leg != "late" else []) + [half] + (late if leg != "early" else [])
    out = [pltpu.VMEM(lead + tail, jnp.float32)] if leg != "early" else []
    return [pltpu.VMEM(shape, LOW) for shape in shapes] + out


def sum_count(sizes):
    return 3 + sum(n - 1 for n in sizes)


def source_of_core(kind, array, start):
    blocks = slice(start, start + 2)
    if kind == "down":
        return lambda core: array.at[:, core, :, :, blocks]
    return lambda core: array.at[blocks, :, core]


class Rider:
    def __init__(self, sizes, r, width, legs, steps, number):
        self.sizes, self.legs, self.steps, self.number = sizes, legs, steps, number
        self.items = [(kind, leg, *item) for kind, leg in legs for item in pair_of(kind, r, width)]
        self.outs, self.scratch, self.inputs = [], [], 0
        for kind, leg in legs:
            self.inputs += 2 if leg == "late" else 1
            if leg == "late":
                self.outs.append(jax.ShapeDtypeStruct((4, r, width), jnp.float32))
            else:
                for order, start, lead, tail in pair_of(kind, r, width):
                    self.outs.append(
                        jax.ShapeDtypeStruct(half_shape(sizes, order, lead, tail), LOW)
                    )
        count = len(self.items) * sum_count(sizes)
        self.scratch = [pltpu.SemaphoreType.DMA((count,)), pltpu.SemaphoreType.DMA((count,))]
        for kind, leg, order, start, lead, tail in self.items:
            self.scratch += sum_buffers(sizes, order, lead, tail, leg)

    def board(self, ins, outs, scratch):
        self.links = Links(self.sizes, *scratch[:2])
        scratch = list(scratch[2:])
        ins, outs = list(ins), list(outs)
        self.sums = {"early": [], "late": []}
        for kind, leg in self.legs:
            if leg == "early":
                array = ins.pop(0)
            else:
                final = outs.pop(0)
            for order, start, lead, tail in pair_of(kind, *scratch[0].shape[-2:]):
                count = 4 if leg == "early" else 5
                bufs = scratch[:count]
                del scratch[:count]
                if leg == "early":
                    source, out = source_of_core(kind, array, start), outs.pop(0)
                else:
                    source, out = ins.pop(0), final.at[start : start + 2]
                item = Sum(self.links, source, order, len(lead), bufs, out, leg)
                self.sums[leg].append(item)

    def begin(self):
        self.links.greet(self.links.neighbours())
        for item in self.sums["late"] + self.sums["early"]:
            item.begin()

    def stage(self, leg, at):
        for item in self.sums[leg]:
            item.stages[at]()

    def end(self):
        for item in self.sums["late"] + self.sums["early"]:
            item.end()

    def step(self, name):
        if name == "begin":
            self.begin()
        elif name == "end":
            self.end()
        else:
            leg, at = name
            if self.sums[leg]:
                self.stage(leg, at)

    def params(self):
        return pltpu.CompilerParams(
            collective_id=self.number, has_side_effects=True, vmem_limit_bytes=VMEM_BYTES
        )


def home_kernel(sizes, legs, *refs):
    inputs, refs = refs[: len(legs) + 1], refs[len(legs) + 1 :]
    vec, sent, late_sum, g_square, g_down, g_vec, back = refs[:7]
    links = Links(sizes, *refs[7:9])
    whole = Whole(links, vec, refs[9:18], g_vec)
    refs = list(refs[18:])
    links.greet(links.partners())
    inputs = list(inputs)
    groups = []
    for kind, leg in legs:
        if leg == "both":
            array = inputs.pop(0)
        group = []
        for order, start, lead, tail in pair_of(kind, *refs[0].shape[-2:]):
            count = 5 if leg == "late" else 8
            bufs = refs[:count]
            del refs[:count]
            blocks = slice(start, start + 2)
            if leg == "late":
                source, out = inputs.pop(0), late_sum.at[blocks]
            else:
                source = source_of_core(kind, array, start)
                out = g_down.at[blocks] if kind == "down" else None
                if out is None:
                    out = g_square.at[blocks if kind == "attn" else slice(start + 4, start + 6)]
            group.append(Sum(links, source, order, len(lead), bufs, out, leg))
        groups.append(group)
    groups[0].append(whole)
    sums = [item for group in groups for item in group]
    for item in sums:
        item.begin()
    moved = deal_back(links, sent, back)
    for turn in range(len(groups) + 3):
        for depth in range(4):
            if 0 <= turn - depth < len(groups):
                for item in groups[turn - depth]:
                    item.stages[depth]()
    for item in sums:
        item.end()
    for copy in moved:
        copy.wait()


def take_home(sizes, halves, grads, vec, sent):
    dws, dwu, dwd = grads
    r, width = dws.shape[-2:]
    legs = [("attn", "late"), ("down", "both"), ("up", "both"), ("attn", "both")]
    members = sizes[2] * sizes[3]
    f32 = jnp.float32
    batch, two, count, rows = sent.shape[:4]
    outs = [
        jax.ShapeDtypeStruct((4, r, width), f32),
        jax.ShapeDtypeStruct((8, r, width), f32),
        jax.ShapeDtypeStruct((4, r, width), f32),
        jax.ShapeDtypeStruct(vec.shape, f32),
        jax.ShapeDtypeStruct((batch, count, two, rows, width), LOW),
    ]
    args = [*halves, dwd, dwu, dws, vec, sent]
    scratch = whole_buffers(sizes, vec.shape)
    for kind, leg in legs:
        for order, start, lead, tail in pair_of(kind, r, width):
            scratch += sum_buffers(sizes, order, lead, tail, leg)
    count = (2 * len(legs) + 1) * sum_count(sizes) + members
    sems = [pltpu.SemaphoreType.DMA((count,)), pltpu.SemaphoreType.DMA((count,))]
    return pl.pallas_call(
        lambda *refs: home_kernel(sizes, legs, *refs),
        out_shape=outs,
        in_specs=[HBM] * len(args),
        out_specs=[HBM] * len(outs),
        scratch_shapes=sems + scratch,
        compiler_params=pltpu.CompilerParams(
            collective_id=1, has_side_effects=True, vmem_limit_bytes=VMEM_BYTES
        ),
        name="take_home",
    )(*args)


def bin_mask(first_blocks, second_blocks, random_pair):
    block_ids = jnp.arange(NBLK)
    later_seg = block_ids >= first_blocks
    rel_block = jnp.where(later_seg, block_ids - first_blocks, block_ids)
    seg_len = jnp.where(later_seg, second_blocks, first_blocks)
    live_block = block_ids < first_blocks + second_blocks
    rand_rows = jnp.where(
        later_seg[:, None],
        jnp.take(random_pair[1], rel_block, axis=0),
        jnp.take(random_pair[0], rel_block, axis=0),
    )
    picked = jnp.remainder(rand_rows, seg_len[:, None])
    row_rel = rel_block[:, None]
    col_rel = rel_block[None, :]
    row_len = seg_len[:, None]
    nearby = jnp.abs(row_rel - col_rel) <= 1
    global_hit = (
        (col_rel == 0) | (col_rel == row_len - 1) | (row_rel == 0) | (row_rel == row_len - 1)
    )
    random_hit = jnp.any(picked[:, :, None] == rel_block[None, None, :], axis=1)
    same_seg = (
        (later_seg[:, None] == later_seg[None, :]) & live_block[:, None] & live_block[None, :]
    )
    allowed = (nearby | global_hit | random_hit) & same_seg
    return jnp.repeat(jnp.repeat(allowed, BLOCK, axis=0), BLOCK, axis=1)


def dot(left, right):
    return jnp.dot(left, right, preferred_element_type=jnp.float32)


def dot_back(left, right):
    return lax.dot_general(left, right, (((1,), (1,)), ((), ())), preferred_element_type=jnp.float32)


def dot_weight(left, right):
    return lax.dot_general(left, right, (((0,), (0,)), ((), ())), preferred_element_type=jnp.float32)


LOW = jnp.bfloat16
LANES = 128
BQ, BV, BO, GA, BA, BD, GF, BF, BU = range(9)


def layer_norm(residual):
    center = residual - jnp.mean(residual, axis=-1, keepdims=True)
    inv_std = lax.rsqrt(jnp.mean(center * center, axis=-1, keepdims=True) + epsilon)
    return (center * inv_std, inv_std)


def norm_back(grad_out, normed, inv_std, gain):
    scaled = grad_out * gain
    return inv_std * (
        scaled
        - jnp.mean(scaled, axis=-1, keepdims=True)
        - normed * jnp.mean(scaled * normed, axis=-1, keepdims=True)
    )


def gelu_parts(u):
    root = 0.7978845608028654
    t = jnp.tanh(root * (u + 0.044715 * (u * u * u)))
    half = 0.5 * (1.0 + t)
    slope = half + 0.5 * u * (1.0 - t * t) * (root * (1.0 + 3 * 0.044715 * (u * u)))
    return (u * half, slope)


def lanes_of(pair, head):
    return pair[:, head * HEAD_DIM : (head + 1) * HEAD_DIM]


def pair_at(pair, offset=0):
    return pl.ds(pl.multiple_of(offset + pair * 2 * HEAD_DIM, 2 * HEAD_DIM), 2 * HEAD_DIM)


def lane_ids(rows):
    return lax.broadcasted_iota(jnp.int32, (rows, LANES), 1)


def attn_fwd_kernel(x_ref, w_ref, v_ref, mask_ref, qkv_ref, ctx_ref, stat_ref, normed_ref):
    rows, width = x_ref.shape
    act = x_ref[...].astype(LOW)
    for j, bias in enumerate((BQ, None, BV)):
        out = dot(act, w_ref[0, j])
        if bias is not None:
            out = out + v_ref[0, bias : bias + 1, :]
        qkv_ref[:, j * width : (j + 1) * width] = out.astype(LOW)
    scale = HEAD_DIM ** (-0.5)
    lanes = lane_ids(rows)
    stat_ref[...] = jnp.zeros_like(stat_ref)

    def pair_step(pair, carry):
        q = qkv_ref[:, pair_at(pair)]
        k = qkv_ref[:, pair_at(pair, width)]
        v = qkv_ref[:, pair_at(pair, 2 * width)]
        mixed = []
        for head in range(2):
            s = dot_back(lanes_of(q, head), lanes_of(k, head)) * scale
            s = jnp.where(mask_ref[0] > 0, s, NEG)
            top = jnp.max(s, axis=-1, keepdims=True)
            e = jnp.exp(s - top)
            total = jnp.sum(e, axis=-1, keepdims=True)
            mixed.append(dot(e.astype(LOW), lanes_of(v, head)) / total)
            log_total = top + jnp.log(total)
            stat_ref[...] = jnp.where(lanes == 2 * pair + head, log_total, stat_ref[...])
        ctx_ref[:, pair_at(pair)] = jnp.concatenate(mixed, axis=1).astype(LOW)
        return carry

    lax.fori_loop(0, HEADS // 2, pair_step, 0)
    resid = x_ref[...].astype(jnp.float32) + dot(ctx_ref[...], w_ref[0, 3])
    normed, inv = layer_norm(resid + v_ref[0, BO : BO + 1, :])
    normed_ref[...] = normed
    stat_ref[...] = jnp.where(lanes == HEADS, inv, stat_ref[...])


def attn_fwd(x, square, vectors, mask, layer_at):
    rows, width = x.shape
    bins, block = mask.shape[:2]
    row = lambda n: pl.BlockSpec((block, n), lambda b: (b, 0))
    f32 = jnp.float32
    return pl.pallas_call(
        attn_fwd_kernel,
        grid=(bins,),
        in_specs=[
            row(width),
            pl.BlockSpec((1, 4, width, width), lambda b: (layer_at, 0, 0, 0)),
            pl.BlockSpec((1,) + vectors.shape[1:], lambda b: (layer_at, 0, 0)),
            pl.BlockSpec((1, block, block), lambda b: (b, 0, 0)),
        ],
        out_specs=[row(3 * width), row(width), row(LANES), row(width)],
        out_shape=[
            jax.ShapeDtypeStruct((rows, 3 * width), LOW),
            jax.ShapeDtypeStruct((rows, width), LOW),
            jax.ShapeDtypeStruct((rows, LANES), f32),
            jax.ShapeDtypeStruct((rows, width), f32),
        ],
        name="attn_fwd",
    )(x, square, vectors, mask)


def middle_of(normed_ref, v_ref):
    return normed_ref[...] * v_ref[0, GA : GA + 1, :] + v_ref[0, BA : BA + 1, :]


def bias_up_of(v_ref, at, count):
    picked = v_ref[0, BU : BU + 1, :]
    for j in range(1, count):
        picked = jnp.where(at == j, v_ref[0, BU + j : BU + j + 1, :], picked)
    return picked


def mlp_fwd_kernel(
    count, normed_ref, wu_ref, wd_ref, v_ref, up_ref, out_ref, low_ref, fnorm_ref, stat_ref, mid, acc
):
    at = pl.program_id(0)

    @pl.when(at == 0)
    def _():
        mid[...] = middle_of(normed_ref, v_ref).astype(LOW)
        acc[...] = jnp.zeros_like(acc)

    up = dot(mid[...], wu_ref[0, 0]) + bias_up_of(v_ref, at, count)
    up_ref[...] = up
    acc[...] += dot(gelu_parts(up)[0].astype(LOW), wd_ref[0])

    @pl.when(at == count - 1)
    def _():
        resid = middle_of(normed_ref, v_ref) + acc[...] + v_ref[0, BD : BD + 1, :]
        normed, inv = layer_norm(resid)
        fnorm_ref[...] = normed
        stat_ref[...] = jnp.broadcast_to(inv, stat_ref.shape)
        out = normed * v_ref[0, GF : GF + 1, :] + v_ref[0, BF : BF + 1, :]
        out_ref[...] = out
        low_ref[...] = out.astype(LOW)


def mlp_fwd(normed, square, down, vectors, layer_at):
    rows, width = normed.shape
    count = down.shape[1] // width
    whole = lambda n: pl.BlockSpec((rows, n), lambda j: (0, 0))
    f32 = jnp.float32
    return pl.pallas_call(
        lambda *refs: mlp_fwd_kernel(count, *refs),
        grid=(count,),
        in_specs=[
            whole(width),
            pl.BlockSpec((1, 1, width, width), lambda j: (layer_at, 4 + j, 0, 0)),
            pl.BlockSpec((1, width, width), lambda j: (layer_at, j, 0)),
            pl.BlockSpec((1,) + vectors.shape[1:], lambda j: (layer_at, 0, 0)),
        ],
        out_specs=[
            pl.BlockSpec((rows, width), lambda j: (0, j)),
            whole(width),
            whole(width),
            whole(width),
            whole(LANES),
        ],
        out_shape=[
            jax.ShapeDtypeStruct((rows, count * width), f32),
            jax.ShapeDtypeStruct((rows, width), f32),
            jax.ShapeDtypeStruct((rows, width), LOW),
            jax.ShapeDtypeStruct((rows, width), f32),
            jax.ShapeDtypeStruct((rows, LANES), f32),
        ],
        scratch_shapes=[pltpu.VMEM((rows, width), LOW), pltpu.VMEM((rows, width), f32)],
        name="mlp_fwd",
    )(normed, square, down, vectors)


def sum_rows(values):
    return jnp.sum(values, axis=0, keepdims=True)


def aboard(refs, rider, ins, outs):
    if rider is None:
        return refs, lambda here, part: None
    rest = refs[ins + rider.inputs :]
    middle, last = len(rider.outs), len(rider.scratch)
    own = refs[:ins] + rest[:outs] + rest[outs + middle : len(rest) - last]
    rider.board(refs[ins : ins + rider.inputs], rest[outs : outs + middle], rest[len(rest) - last :])

    def ride(here, part):
        for grid_at, due, name in rider.steps:
            if due == part:

                @pl.when(here(grid_at))
                def _(name=name):
                    rider.step(name)

    return own, ride


def carried(rider, in_specs, out_specs, out_shape, scratch):
    if rider is not None:
        in_specs = in_specs + [HBM] * rider.inputs
        out_specs = out_specs + [HBM] * len(rider.outs)
        out_shape = out_shape + rider.outs
        scratch = scratch + rider.scratch
    found = dict(
        in_specs=in_specs, out_specs=out_specs, out_shape=out_shape, scratch_shapes=scratch
    )
    if rider is not None:
        found["compiler_params"] = rider.params()
    return found


MLP_STEPS = [
    (0, 0, "begin"),
    (0, 1, ("late", 0)),
    (0, 2, ("early", 0)),
    (1, 1, ("late", 1)),
    (3, 1, ("early", 1)),
    (3, 2, ("late", 2)),
    (3, 3, "end"),
]
ATTN_STEPS = [
    (0, 0, "begin"),
    (0, 2, ("late", 0)),
    (0, 3, ("early", 0)),
    (0, 6, ("late", 1)),
    (1, 4, ("early", 1)),
    (1, 7, ("late", 2)),
    (1, 7, "end"),
]


def mlp_bwd_kernel(count, rider, *refs):
    own, ride = aboard(refs, rider, 9, 4)
    grad_ref, fnorm_ref, fstat_ref, normed_ref, stat_ref, up_ref, wu_ref, wd_ref, v_ref = own[:9]
    dwu_ref, dwd_ref, grad_a_ref, vec_ref, mid, grad_f, low_f, acc = own[9:]
    at = pl.program_id(0)
    here = lambda step: at == step
    ride(here, 0)

    @pl.when(at == 0)
    def _():
        grad_out, normed = grad_ref[...].astype(jnp.float32), fnorm_ref[...]
        vec_ref[...] = jnp.zeros_like(vec_ref)
        vec_ref[GF : GF + 1, :] = sum_rows(grad_out * normed)
        vec_ref[BF : BF + 1, :] = sum_rows(grad_out)
        grad = norm_back(grad_out, normed, fstat_ref[:, :1], v_ref[0, GF : GF + 1, :])
        vec_ref[BD : BD + 1, :] = sum_rows(grad)
        grad_f[...] = grad
        low_f[...] = grad.astype(LOW)
        mid[...] = middle_of(normed_ref, v_ref).astype(LOW)
        acc[...] = jnp.zeros_like(acc)

    act, slope = gelu_parts(up_ref[...])
    dwd_ref[...] = dot_weight(act.astype(LOW), low_f[...]).astype(LOW)
    ride(here, 1)
    grad_up = dot_back(low_f[...], wd_ref[0]) * slope
    vec_ref[pl.ds(BU + at, 1), :] = sum_rows(grad_up)
    low_up = grad_up.astype(LOW)
    dwu_ref[0] = dot_weight(mid[...], low_up).astype(LOW)
    acc[...] += dot_back(low_up, wu_ref[0, 0])
    ride(here, 2)

    @pl.when(at == count - 1)
    def _():
        grad_mid, normed = grad_f[...] + acc[...], normed_ref[...]
        vec_ref[GA : GA + 1, :] = sum_rows(grad_mid * normed)
        vec_ref[BA : BA + 1, :] = sum_rows(grad_mid)
        inv = stat_ref[:, HEADS : HEADS + 1]
        grad = norm_back(grad_mid, normed, inv, v_ref[0, GA : GA + 1, :])
        vec_ref[BO : BO + 1, :] = sum_rows(grad)
        grad_a_ref[...] = grad

    ride(here, 3)


def mlp_bwd(
    grad, fnorm, fstat, normed, stat, up, square, down, vectors, layer_at, rider=None, load=()
):
    rows, width = normed.shape
    count = down.shape[1] // width
    whole = lambda n: pl.BlockSpec((rows, n), lambda j: (0, 0))
    f32 = jnp.float32
    vec_rows = vectors.shape[1]
    in_specs = [
        whole(width),
        whole(width),
        whole(LANES),
        whole(width),
        whole(LANES),
        pl.BlockSpec((rows, width), lambda j: (0, j)),
        pl.BlockSpec((1, 1, width, width), lambda j: (layer_at, 4 + j, 0, 0)),
        pl.BlockSpec((1, width, width), lambda j: (layer_at, j, 0)),
        pl.BlockSpec((1, vec_rows, width), lambda j: (layer_at, 0, 0)),
    ]
    out_specs = [
        pl.BlockSpec((1, width, width), lambda j: (j, 0, 0)),
        pl.BlockSpec((width, width), lambda j: (j, 0)),
        whole(width),
        pl.BlockSpec((vec_rows, width), lambda j: (0, 0)),
    ]
    out_shape = [
        jax.ShapeDtypeStruct((count, width, width), LOW),
        jax.ShapeDtypeStruct((count * width, width), LOW),
        jax.ShapeDtypeStruct((rows, width), f32),
        jax.ShapeDtypeStruct((vec_rows, width), f32),
    ]
    scratch = [
        pltpu.VMEM((rows, width), LOW),
        pltpu.VMEM((rows, width), f32),
        pltpu.VMEM((rows, width), LOW),
        pltpu.VMEM((rows, width), f32),
    ]
    return pl.pallas_call(
        lambda *refs: mlp_bwd_kernel(count, rider, *refs),
        grid=(count,),
        name="mlp_bwd" if rider is None else "mlp_bwd_sums",
        **carried(rider, in_specs, out_specs, out_shape, scratch),
    )(grad, fnorm, fstat, normed, stat, up, square, down, vectors, *load)


def attn_bwd_kernel(rider, *refs):
    own, ride = aboard(refs, rider, 6, 4)
    grad_ref, qkv_ref, stat_ref, mask_ref, w_ref, vec_in = own[:6]
    dqkv_ref, grad_in_ref, low_ref, vec_ref, gctx = own[6:]
    rows, width = grad_ref.shape
    bin_at = pl.program_id(0)
    ride(lambda step: bin_at == step, 0)

    @pl.when(pl.program_id(0) == 0)
    def _():
        vec_ref[...] = vec_in[...]

    low_ref[...] = grad_ref[...].astype(LOW)
    gctx[...] = dot_back(low_ref[...], w_ref[0, 3]).astype(LOW)
    scale = HEAD_DIM ** (-0.5)
    lanes = lane_ids(rows)

    def pair_step(pair, carry):
        for part in range(HEADS // 2):
            ride(lambda step: (bin_at == step) & (pair == part), 1 + part)
        q = qkv_ref[:, pair_at(pair)]
        k = qkv_ref[:, pair_at(pair, width)]
        v = qkv_ref[:, pair_at(pair, 2 * width)]
        g = gctx[:, pair_at(pair)]
        grads = [[], [], []]
        for head in range(2):
            qh, kh, vh, gh = (lanes_of(t, head) for t in (q, k, v, g))
            log_total = jnp.sum(
                jnp.where(lanes == 2 * pair + head, stat_ref[...], 0.0), axis=-1, keepdims=True
            )
            s = dot_back(qh, kh) * scale
            s = jnp.where(mask_ref[0] > 0, s, NEG)
            p = jnp.exp(s - log_total)
            grad_p = dot_back(gh, vh)
            inner = jnp.sum(grad_p * p, axis=-1, keepdims=True)
            low_s = (p * (grad_p - inner)).astype(LOW)
            grads[0].append(dot(low_s, kh) * scale)
            grads[1].append(dot_weight(low_s, qh) * scale)
            grads[2].append(dot_weight(p.astype(LOW), gh))
        for j, row in ((0, BQ), (1, None), (2, BV)):
            both = jnp.concatenate(grads[j], axis=1)
            dqkv_ref[:, pair_at(pair, j * width)] = both.astype(LOW)
            if row is not None:
                vec_ref[row : row + 1, pair_at(pair)] += sum_rows(both)
        return carry

    lax.fori_loop(0, HEADS // 2, pair_step, 0)
    total = grad_ref[...]
    for j in range(3):
        total = total + dot_back(dqkv_ref[:, j * width : (j + 1) * width], w_ref[0, j])
    grad_in_ref[...] = total
    ride(lambda step: bin_at == step, 1 + HEADS // 2)


def attn_bwd(grad_a, qkv, stat, mask, square, vec, layer_at, rider=None, load=()):
    rows, width = grad_a.shape
    bins, block = mask.shape[:2]
    row = lambda n: pl.BlockSpec((block, n), lambda b: (b, 0))
    fixed = pl.BlockSpec(vec.shape, lambda b: (0, 0))
    f32 = jnp.float32
    in_specs = [
        row(width),
        row(3 * width),
        row(LANES),
        pl.BlockSpec((1, block, block), lambda b: (b, 0, 0)),
        pl.BlockSpec((1, 4, width, width), lambda b: (layer_at, 0, 0, 0)),
        fixed,
    ]
    out_shape = [
        jax.ShapeDtypeStruct((rows, 3 * width), LOW),
        jax.ShapeDtypeStruct((rows, width), f32),
        jax.ShapeDtypeStruct((rows, width), LOW),
        jax.ShapeDtypeStruct(vec.shape, f32),
    ]
    out_specs = [row(3 * width), row(width), row(width), fixed]
    scratch = [pltpu.VMEM((block, width), LOW)]
    return pl.pallas_call(
        lambda *refs: attn_bwd_kernel(rider, *refs),
        grid=(bins,),
        name=f"attn_bwd_sums{rider.number}",
        **carried(rider, in_specs, out_specs, out_shape, scratch),
    )(grad_a, qkv, stat, mask, square, vec, *load)


def attn_dw_kernel(act_ref, dqkv_ref, ctx_ref, low_ref, out_ref):
    at = pl.program_id(0)

    @pl.when(at < 3)
    def _():
        out_ref[0] = dot_weight(act_ref[...].astype(LOW), dqkv_ref[...]).astype(LOW)

    @pl.when(at == 3)
    def _():
        out_ref[0] = dot_weight(ctx_ref[...], low_ref[...]).astype(LOW)


def attn_dw(act, dqkv, ctx, low):
    rows, width = act.shape
    whole = pl.BlockSpec((rows, width), lambda j: (0, 0))
    return pl.pallas_call(
        attn_dw_kernel,
        grid=(4,),
        in_specs=[
            whole,
            pl.BlockSpec((rows, width), lambda j: (0, jnp.minimum(j, 2))),
            whole,
            whole,
        ],
        out_specs=pl.BlockSpec((1, width, width), lambda j: (j, 0, 0)),
        out_shape=jax.ShapeDtypeStruct((4, width, width), LOW),
        name="attn_dw",
    )(act, dqkv, ctx, low)


SMALL = ("bq", "bv", "bo", "ga", "ba", "bd", "gf", "bf", "bu")


def small_rows(p, layer_at, width):
    small = jnp.concatenate([p[name][layer_at] for name in SMALL])
    return jnp.pad(small, (0, 8 * width - small.shape[0])).reshape(8, width)


def vectors_of(all_small, rows):
    layers, width = all_small.shape[0], all_small.shape[-1]
    flat = all_small.reshape(layers, -1, 8 * width).astype(jnp.float32)
    even = flat[:, :, : 8 * rows].reshape(layers, -1, 8, rows).transpose(0, 2, 1, 3)
    up = flat[:, :, 8 * rows : 12 * rows]
    return jnp.concatenate([even.reshape(layers, 8, width), up.reshape(layers, 4, width)], axis=1)


def forward(hidden, act_in, w, mask, layer_at):
    square, down, vectors = w
    qkv, ctx, stat, normed = attn_fwd(hidden, square, vectors, mask, layer_at)
    up, out, out_low, fnorm, fstat = mlp_fwd(normed, square, down, vectors, layer_at)
    return out, out_low, (act_in, qkv, ctx, stat, normed, up, fnorm, fstat)


def backward_layers(grad, back, kept, w, mask, sizes, rows):
    square, down, vectors = w
    width = square.shape[-1]

    def of_mlp(grad, layer_at, *more):
        act_in, qkv, ctx, stat, normed, up, fnorm, fstat = kept[layer_at]
        return mlp_bwd(
            grad, fnorm, fstat, normed, stat, up, square, down, vectors, layer_at, *more
        )

    def of_attn(grad_a, vec, layer_at, *more):
        act_in, qkv, ctx, stat, *unused = kept[layer_at]
        dqkv, grad_in, low_a, vec, *sums = attn_bwd(
            grad_a, qkv, stat, mask, square, vec, layer_at, *more
        )
        return grad_in, attn_dw(act_in, dqkv, ctx, low_a), vec, sums

    blocks_out = lambda t: t.reshape((4,) + sizes + (rows, width))
    rows_out = lambda t: t.reshape(sizes + (4, rows, width))
    dwu, dwd, grad_a, vec = of_mlp(grad, 1)
    rider = Rider(sizes, rows, width, [("down", "early")], ATTN_STEPS, 2)
    grad, dws, vec_late, halves = of_attn(grad_a, vec, 1, rider, [rows_out(dwd)])
    grad, back = lax.optimization_barrier((grad, back))
    rider = Rider(sizes, rows, width, [("down", "late"), ("up", "early")], MLP_STEPS, 3)
    dwu, dwd, grad_a, vec, g_down, *halves = of_mlp(grad, 0, rider, [*halves, blocks_out(dwu)])
    rider = Rider(sizes, rows, width, [("up", "late"), ("attn", "early")], ATTN_STEPS, 4)
    grad, dws, vec, (g_up, *halves) = of_attn(grad_a, vec, 0, rider, [*halves, blocks_out(dws)])
    left = (blocks_out(dws), blocks_out(dwu), rows_out(dwd))
    return grad, back, (g_up, g_down), (halves, left, jnp.stack([vec, vec_late]))


def shift_down(rows, amount):
    doubled = jnp.concatenate([jnp.zeros_like(rows), rows], axis=0)
    return lax.dynamic_slice_in_dim(doubled, rows.shape[0] - amount, rows.shape[0], 0)


def shift_up(rows, amount):
    doubled = jnp.concatenate([rows, jnp.zeros_like(rows)], axis=0)
    return lax.dynamic_slice_in_dim(doubled, amount, rows.shape[0], 0)


def pack_bin(slots, first_len, second_len):
    positions = jnp.arange(slots.shape[1])[:, None]
    later = shift_down(jnp.where(positions < second_len, slots[1], 0), first_len)
    return jnp.where(positions < first_len, slots[0], later)


def unpack_bin(rows, first_len, second_len):
    positions = jnp.arange(rows.shape[0])[:, None]
    first = jnp.where(positions < first_len, rows, 0)
    second = jnp.where(positions < second_len, shift_up(rows, first_len), 0)
    return jnp.stack([first, second])


def per_device(tokens_in, cotangent, lengths, bin_deal, random_blocks, *weights):
    names = ("wqkv", "bq", "bv", "wo", "bo", "ga", "ba", "wu", "bu", "wd", "bd", "gf", "bf")
    p = dict(zip(names, weights))
    rows = p["wo"].shape[1]
    members = lax.axis_size("fsdp")
    member = lax.axis_index("fsdp")
    group_at = lax.axis_index("dp")
    grid = Grid(lax.axis_size("dp"), members)
    slot_count = 2 * members
    slot_ids = jnp.arange(slot_count)
    deal_here = lax.dynamic_index_in_dim(bin_deal, group_at, 1, keepdims=False)
    slot_hits = (deal_here[:, :, None] == slot_ids[None, None, :]).astype(jnp.int32)
    source_of = jnp.sum(slot_hits * slot_ids[None, :, None], axis=1)
    lengths_here = lax.dynamic_slice_in_dim(lengths, group_at * slot_count, slot_count, 1)
    bin_lengths = jnp.take_along_axis(lengths_here, source_of, axis=1)
    random_here = lax.dynamic_slice_in_dim(random_blocks, group_at * slot_count, slot_count, 1)
    batch_count, unused_slots, rows_dev, width = tokens_in.shape
    bin_len = rows_dev * members
    order_index = source_of[:, :, None, None]

    def dealt(array):
        sent = jnp.take_along_axis(array, order_index, axis=1)
        return sent.reshape(batch_count, members, 2, rows_dev, width)

    blocks = lambda w: w.reshape(LAYERS, rows, -1, width).transpose(0, 2, 1, 3)
    square = jnp.concatenate([blocks(p["wqkv"]), blocks(p["wo"]), blocks(p["wu"])], axis=1)
    down = p["wd"].reshape(LAYERS, -1, rows, width)
    small = jnp.stack([small_rows(p, layer_at, width) for layer_at in range(LAYERS)])
    sent_grad = dealt(cotangent)
    got_x, *gathered = bring(grid.sizes, dealt(tokens_in), square, down, small)
    got_x, sent_grad = lax.optimization_barrier((got_x, sent_grad))
    arrived_x = got_x.reshape(batch_count, 2, bin_len, width)
    arrived_grad = lax.all_to_all(
        sent_grad, "fsdp", split_axis=1, concat_axis=3, tiled=True
    )[:, 0]
    square, down, small = gathered
    side = rows * grid.count
    w = (
        square.reshape(LAYERS, -1, side, width),
        down.reshape(LAYERS, -1, width),
        vectors_of(small, rows),
    )
    slot_pair = lax.dynamic_slice_in_dim(bin_lengths, 2 * member, 2, 1)
    random_pair = lax.dynamic_slice_in_dim(random_here, 2 * member, 2, 1)
    allowed = jax.vmap(bin_mask)(slot_pair[:, 0], slot_pair[:, 1], random_pair)
    first_len = slot_pair[:, 0] * BLOCK
    second_len = slot_pair[:, 1] * BLOCK

    def packed(slots):
        bins = [pack_bin(slots[m], first_len[m], second_len[m]) for m in range(batch_count)]
        return jnp.concatenate(bins, axis=0)

    def to_slots(bins):
        bins = bins.reshape(batch_count, bin_len, width)
        slots = [unpack_bin(bins[m], first_len[m], second_len[m]) for m in range(batch_count)]
        return jnp.stack(slots)

    def in_order(back):
        back = back.reshape(batch_count, slot_count, rows_dev, width)
        return jnp.take_along_axis(back, deal_here[:, :, None, None], axis=1)

    mask = allowed.astype(jnp.float32)
    hidden = act_in = packed(arrived_x)
    kept = []
    for layer_at in range(LAYERS):
        hidden, act_in, stored = forward(hidden, act_in, w, mask, layer_at)
        kept.append(stored)
    sent = to_slots(act_in)[:, None]
    back = lax.all_to_all(sent, "fsdp", split_axis=3, concat_axis=1, tiled=True)
    arrived_grad, act_in = lax.optimization_barrier((arrived_grad, act_in))
    grad = packed(arrived_grad)
    grad, back, (g_up, g_down_late), left = backward_layers(grad, back, kept, w, mask, grid.sizes, rows)
    output = in_order(back)
    sent = to_slots(grad.astype(LOW)).reshape(batch_count, 2, members, rows_dev, width)
    g_attn, g_square, g_down, g_vec, back = take_home(grid.sizes, *left, sent)
    input_grad = in_order(back)
    beside = lambda *pairs: jnp.stack(
        [blocks.transpose(1, 0, 2).reshape(rows, -1) for blocks in pairs]
    )
    out = {
        "wqkv": beside(g_square[:3], g_attn[:3]),
        "wo": jnp.stack([g_square[3], g_attn[3]]),
        "wu": beside(g_square[4:], g_up),
        "wd": jnp.stack([g_down.reshape(-1, width), g_down_late.reshape(-1, width)]),
    }
    place = group_at * members + member
    for at, name in enumerate(SMALL):
        values = g_vec[:, at:].reshape(LAYERS, -1) if name == "bu" else g_vec[:, at]
        count = rows * (values.shape[1] // width)
        out[name] = lax.dynamic_slice_in_dim(values, place * count, count, 1)
    return (output, input_grad) + tuple(out[name] for name in names)


def solution(mesh):
    tokens = P(None, "dp", "fsdp", None)
    matrix = P(None, AXES, None)
    vector = P(None, AXES)
    weights = (matrix, vector, vector, matrix, vector, vector, vector)
    weights += (matrix, vector, matrix, vector, vector, vector)
    return jax.shard_map(
        per_device,
        mesh=mesh,
        in_specs=(tokens, tokens, P(), P(), P()) + weights,
        out_specs=(tokens, tokens) + weights,
        check_vma=False,
    )
```

```python
import jax
import jax.numpy as jnp
from jax import lax
from jax.experimental import pallas as pl
from jax.experimental.pallas import tpu as pltpu
from jax.sharding import PartitionSpec as P

HEADS = 12
BLOCK = 64
NBLK = 6
LAYERS = 2
CORES = 2
AXES = ("dp", "fsdp")
NEG = -1000000000.0
HEAD_DIM = 64
VMEM_BYTES = 67043328
DEAL_TURNS = 8


epsilon = 1e-06


def split_fsdp(count):
    inner = 1
    while (2 * inner) ** 2 <= count:
        inner *= 2
    return (count // inner, inner)


class Grid:
    def __init__(self, dp_count, fsdp_count):
        outer, inner = split_fsdp(fsdp_count)
        self.sizes = (dp_count // CORES, CORES, outer, inner)
        dp_at, fsdp_at = lax.axis_index("dp"), lax.axis_index("fsdp")
        self.at = (dp_at // CORES, dp_at % CORES, fsdp_at // inner, fsdp_at % inner)

        self.count = dp_count * fsdp_count


ALL = slice(None)
HBM = pl.BlockSpec(memory_space=pl.ANY)


class Links:
    def __init__(self, sizes, send_sem, recv_sem):
        outer, inner = sizes[2:]
        dp_at, fsdp_at = lax.axis_index("dp"), lax.axis_index("fsdp")
        self.sizes = sizes
        self.at = (dp_at // CORES, dp_at % CORES, fsdp_at // inner, fsdp_at % inner)
        self.send_sem, self.recv_sem = send_sem, recv_sem
        self.used = 0

    def device(self, place):
        return (place[0] * CORES + place[1], place[2] * self.sizes[3] + place[3])

    def along(self, axis, offset):
        place = list(self.at)
        place[axis] = (place[axis] + offset) % self.sizes[axis]
        return self.device(place)

    def plan(self, source, target, device):
        copy = pltpu.make_async_remote_copy(
            src_ref=source,
            dst_ref=target,
            send_sem=self.send_sem.at[self.used],
            recv_sem=self.recv_sem.at[self.used],
            device_id=device,
            device_id_type=pl.DeviceIdType.MESH,
        )
        self.used += 1
        return copy

    def plan_here(self, source, target):
        copy = pltpu.make_async_copy(source, target, self.recv_sem.at[self.used])
        self.used += 1
        return copy

    def start(self, source, target, device):
        copy = self.plan(source, target, device)
        copy.start()
        return copy

    def start_here(self, source, target):
        copy = self.plan_here(source, target)
        copy.start()
        return copy

    def greet(self, devices):
        barrier = pltpu.get_barrier_semaphore()
        for device in devices:
            pl.semaphore_signal(barrier, inc=1, device_id=device, device_id_type=pl.DeviceIdType.MESH)
        pl.semaphore_wait(barrier, len(devices))

    def partners(self):
        found = [self.along(axis, k) for axis in (0, 1) for k in range(1, self.sizes[axis])]
        count = self.sizes[2] * self.sizes[3]
        return found + [self.member(k) for k in range(1, count)]

    def neighbours(self):
        return [self.along(axis, k) for axis in range(4) for k in range(1, self.sizes[axis])]

    def member(self, offset):
        count = self.sizes[2] * self.sizes[3]
        flat = self.at[2] * self.sizes[3] + self.at[3]
        return (self.at[0] * CORES + self.at[1], (flat + offset) % count)


class Gather:
    def __init__(self, links, source, target, order):
        self.links, self.source, self.target, self.order = links, source, target, order
        self.sent = []
        self.across = []

    def begin(self):
        links = self.links
        x, c, o, i = links.at
        spot = self.target(*links.at)
        self.own = links.start_here(self.source, spot)
        if links.sizes[2] != 4:
            self.column = [
                links.start(self.source, spot, links.along(2, k)) for k in range(1, links.sizes[2])
            ]
            return
        self.inside = (o == 1) | (o == 2)
        near = links.device((x, c, o + 1 - 2 * (o % 2), i))
        across = links.device((x, c, 3 - o, i))
        pair = lambda half: self.target(x, c, pl.ds(2 * half, 2), i)
        ours, others = pair(o // 2), pair(1 - o // 2)
        self.column = [links.start(self.source, spot, near)]
        self.pairs = links.plan(ours, ours, across)
        self.outwards = links.plan(others, others, near)

    def cross(self):
        if self.links.sizes[2] != 4:
            return
        self.own.wait()
        self.column[0].wait_recv()

        @pl.when(self.inside)
        def _():
            self.pairs.start()

    def spread(self):
        if self.links.sizes[2] != 4:
            return

        @pl.when(self.inside)
        def _():
            self.pairs.wait_recv()
            self.outwards.start()

    def hand_over(self, spot):
        self.across.append(self.links.start(spot, spot, self.links.along(1, 1)))

    def first(self):
        links = self.links
        x, c, o, i = links.at
        if links.sizes[2] != 4:
            self.own.wait()
            for copy in self.column:
                copy.wait_recv()
        else:

            @pl.when(~self.inside)
            def _():
                self.outwards.wait_recv()

        spot = self.target(x, c, ALL, i)
        axis = self.order[0]
        self.line = [
            links.start(spot, spot, links.along(axis, k)) for k in range(1, links.sizes[axis])
        ]
        self.hand_over(spot)

    def second(self):
        links = self.links
        x, c, o, i = links.at
        for copy in self.line:
            copy.wait_recv()
        first, second = self.order
        spot = self.target(ALL, c, ALL, i) if first == 0 else self.target(x, c, ALL, ALL)
        self.sheet = [
            links.start(spot, spot, links.along(second, k)) for k in range(1, links.sizes[second])
        ]
        for k in range(1, links.sizes[first]):
            near = (links.at[first] - k) % links.sizes[first]
            self.hand_over(
                self.target(near, c, ALL, i) if first == 0 else self.target(x, c, ALL, near)
            )

    def third(self):
        links = self.links
        c = links.at[1]
        second = self.order[1]
        for k, copy in enumerate(self.sheet, 1):
            copy.wait_recv()
            near = (links.at[second] - k) % links.sizes[second]
            self.hand_over(
                self.target(near, c, ALL, ALL) if second == 0 else self.target(ALL, c, ALL, near)
            )

    def end(self):
        for copy in self.across:
            copy.wait()
        for copy in self.column + self.line + self.sheet:
            copy.wait_send()
        if self.links.sizes[2] == 4:

            @pl.when(self.inside)
            def _():
                self.pairs.wait_send()
                self.outwards.wait_send()


def deal_out(links, source, target):
    count = links.sizes[2] * links.sizes[3]
    me = links.at[2] * links.sizes[3] + links.at[3]
    spot = target.at[:, :, me]
    starts = [
        lambda k=k: links.start(source.at[:, (me + k) % count], spot, links.member(k))
        for k in range(1, count)
    ]
    return starts + [lambda: links.start_here(source.at[:, me], spot)]


def deal_back(links, source, target):
    count = links.sizes[2] * links.sizes[3]
    me = links.at[2] * links.sizes[3] + links.at[3]
    spot = target.at[:, me]
    copies = [links.start_here(source.at[:, :, me], spot)]
    for k in range(1, count):
        copies.append(links.start(source.at[:, :, (me + k) % count], spot, links.member(k)))
    return copies


def gathers_of(links, layer_at, square, down, small, all_square, all_down, all_small):
    def of_square(start, order):
        blocks = slice(start, start + 2)
        return Gather(
            links,
            square.at[layer_at, blocks],
            lambda *place: all_square.at[(layer_at, blocks) + place],
            order,
        )

    def of_down(start, order):
        blocks = slice(start, start + 2)
        return Gather(
            links,
            down.at[layer_at, blocks],
            lambda *place: all_down.at[(layer_at,) + place + (blocks,)],
            order,
        )

    tiny = Gather(
        links, small.at[layer_at], lambda *place: all_small.at[(layer_at,) + place], (0, 3)
    )
    return [
        [tiny, of_square(0, (0, 3)), of_square(2, (3, 0))],
        [of_square(4, (0, 3)), of_square(6, (3, 0))],
        [of_down(0, (3, 0)), of_down(2, (3, 0))],
    ]


def bring_kernel(sizes, *refs):
    sent_x, square, down, small = refs[:4]
    got_x, all_square, all_down, all_small = refs[4:8]
    links = Links(sizes, *refs[8:])
    links.greet(links.partners())
    groups = []
    for layer_at in range(LAYERS):
        groups += gathers_of(
            links, layer_at, square, down, small, all_square, all_down, all_small
        )
    starts = deal_out(links, sent_x, got_x)
    share = -(-len(starts) // DEAL_TURNS)
    moved = []

    def run(step, at):
        if 0 <= at < len(groups):
            for item in groups[at]:
                getattr(item, step)()

    run("begin", 0)
    run("begin", 1)
    run("cross", 0)
    run("spread", 0)
    run("cross", 1)
    run("begin", 2)
    for at in range(len(groups) + 2):
        run("first", at)
        run("spread", at + 1)
        run("cross", at + 2)
        run("begin", at + 3)
        moved += [start() for start in starts[at * share : (at + 1) * share]]
        run("second", at - 1)
        run("third", at - 2)
    for group in groups:
        for item in group:
            item.end()
    for copy in moved:
        copy.wait()


def bring(sizes, sent_x, square, down, small):
    low = jnp.bfloat16
    batch, members, two, rows, width = sent_x.shape
    r = square.shape[2]
    got = jax.ShapeDtypeStruct((batch, two, members, rows, width), low)
    outs = [
        got,
        jax.ShapeDtypeStruct((LAYERS, square.shape[1]) + sizes + (r, width), low),
        jax.ShapeDtypeStruct((LAYERS,) + sizes + (down.shape[1], r, width), low),
        jax.ShapeDtypeStruct((LAYERS,) + sizes + (8, width), low),
    ]
    per_item = 3 + sum(n - 1 for n in sizes) + 4 + sizes[0] + sizes[3]
    count = 7 * LAYERS * per_item + members
    return pl.pallas_call(
        lambda *refs: bring_kernel(sizes, *refs),
        out_shape=outs,
        in_specs=[HBM] * 4,
        out_specs=[HBM] * 4,
        scratch_shapes=[pltpu.SemaphoreType.DMA((count,)), pltpu.SemaphoreType.DMA((count,))],
        compiler_params=pltpu.CompilerParams(collective_id=0, has_side_effects=True),
        name="bring",
    )(sent_x, square, down, small)


def each(dims, body):
    total = 1
    for n in dims:
        total *= n

    def step(flat, carry):
        at = []
        for n in reversed(dims):
            at.insert(0, flat % n)
            flat = flat // n
        body(tuple(at))
        return carry

    lax.fori_loop(0, total, step, 0)


def wide(ref, at):
    return ref[at].astype(jnp.float32)


class Sum:
    def __init__(self, links, source, order, lead, bufs, out_ref, leg="both"):
        self.links, self.order, self.lead, self.leg = links, order, lead, leg
        self.sent = []
        c = links.at[1]
        late = (2, 3) if order[0] == 0 else (0, 2)
        if leg == "late":
            self.half = bufs[0]
            self.opening = [links.plan_here(source, self.half)]
        else:
            self.mine, self.theirs, self.first, self.half = bufs[:4]
            there = self.send(source(1 - c), self.theirs, 1, 1)
            self.opening = [links.plan_here(source(c), self.mine), there]
            self.moving_first = self.spread(self.mine, (0, 2, 3), order[0], self.first)
        if leg == "early":
            self.out = self.half
            self.stages = [self.add_core, self.add_first, self.nothing, self.nothing]
        else:
            self.second, self.quarter, self.last, self.out = bufs[-4:]
            self.moving_second = self.spread(self.half, late, order[1], self.second)
            self.moving_last = self.spread(self.quarter, (2,), 2, self.last)
            self.late = late
            self.stages = [self.take_up, self.add_second, self.add_last, self.nothing]
            if leg == "both":
                self.stages = [self.add_core, self.add_first, self.add_second, self.add_last]
        if isinstance(out_ref, list):
            self.results = [links.plan_here(self.out.at[j], ref) for j, ref in enumerate(out_ref)]
        else:
            self.results = [links.plan_here(self.out, out_ref)]

    def send(self, source, target, axis, offset):
        copy = self.links.plan(source, target, self.links.along(axis, offset))
        self.sent.append(copy)
        return copy

    def begin(self):
        for copy in self.opening:
            copy.start()

    def at(self, *place):
        return (ALL,) * self.lead + place

    def spread(self, ref, axes, axis, into):
        size, me = self.links.sizes[axis], self.links.at[axis]
        found = []
        for k in range(1, size):
            place = [ALL] * len(axes)
            place[axes.index(axis)] = (me + k) % size
            found.append(self.send(ref.at[self.at(*place)], into.at[k - 1], axis, k))
        return found

    def fold(self, ref, axes, axis, arrived, into):
        size, me = self.links.sizes[axis], self.links.at[axis]
        spot = axes.index(axis) + self.lead

        def add(at):
            if size == 2 and into.dtype == LOW:
                into[at] = ref[at[:spot] + (me,) + at[spot:]] + arrived[(0,) + at]
                return
            total = wide(ref, at[:spot] + (me,) + at[spot:])
            for k in range(size - 1):
                total = total + wide(arrived, (k,) + at)
            into[at] = total.astype(into.dtype)

        each(into.shape[:-2], add)

    def nothing(self):
        pass

    def add_core(self):
        here, there = self.opening
        here.wait()
        there.wait_recv()

        def add(at):
            self.mine[at] = self.mine[at] + self.theirs[at]

        each(self.mine.shape[:-2], add)
        for copy in self.moving_first:
            copy.start()

    def add_first(self):
        for copy in self.moving_first:
            copy.wait_recv()
        self.fold(self.mine, (0, 2, 3), self.order[0], self.first, self.half)
        for copy in self.results if self.leg == "early" else self.moving_second:
            copy.start()

    def take_up(self):
        self.opening[0].wait()
        for copy in self.moving_second:
            copy.start()

    def add_second(self):
        for copy in self.moving_second:
            copy.wait_recv()
        self.fold(self.half, self.late, self.order[1], self.second, self.quarter)
        for copy in self.moving_last:
            copy.start()

    def add_last(self):
        for copy in self.moving_last:
            copy.wait_recv()
        self.fold(self.quarter, (2,), 2, self.last, self.out)
        for copy in self.results:
            copy.start()

    def end(self):
        for copy in self.results:
            copy.wait()
        for copy in self.sent:
            copy.wait_send()


class Whole:
    def __init__(self, links, source, bufs, out_ref):
        self.links, self.source, self.out_ref = links, source, out_ref
        self.held, self.arrived = bufs[:5], bufs[5:]
        self.sent = []
        self.stages = [self.stage_one, self.stage_two, self.stage_three, self.stage_four]

    def begin(self):
        self.here = self.links.start_here(self.source, self.held[0])

    def send(self, at, axis):
        self.moving = [
            self.links.start(
                self.held[at], self.arrived[at].at[k - 1], self.links.along(axis, k)
            )
            for k in range(1, self.links.sizes[axis])
        ]
        self.sent += self.moving

    def fold(self, at):
        for copy in self.moving:
            copy.wait_recv()
        total = self.held[at][...]
        for k in range(self.arrived[at].shape[0]):
            total = total + self.arrived[at][k]
        self.held[at + 1][...] = total

    def stage_one(self):
        self.here.wait()
        self.send(0, 1)

    def stage_two(self):
        self.fold(0)
        self.send(1, 0)

    def stage_three(self):
        self.fold(1)
        self.send(2, 3)

    def stage_four(self):
        self.fold(2)
        self.send(3, 2)

    def end(self):
        self.fold(3)
        result = self.links.start_here(self.held[4], self.out_ref)
        result.wait()
        for copy in self.sent:
            copy.wait_send()


def whole_buffers(sizes, shape):
    f32 = jnp.float32
    arrived = [pltpu.VMEM((sizes[axis] - 1,) + shape, f32) for axis in (1, 0, 3, 2)]
    return [pltpu.VMEM(shape, f32)] * 5 + arrived


Y_FIRST, X_FIRST = (3, 0), (0, 3)


def pair_of(kind, r, width):
    lead, tail = ((), (2, r, width)) if kind == "down" else ((2,), (r, width))
    return [(Y_FIRST, 0, lead, tail), (X_FIRST, 2, lead, tail)]


def half_shape(sizes, order, lead, tail):
    x, c, o, i = sizes
    return lead + ((x, o) if order[0] == 3 else (o, i)) + tail


def sum_buffers(sizes, order, lead, tail, leg="both"):
    x, c, o, i = sizes
    whole = lead + (x, o, i) + tail
    half = half_shape(sizes, order, lead, tail)
    quarter = lead + (o,) + tail
    early = [whole, whole, (sizes[order[0]] - 1,) + half]
    late = [(sizes[order[1]] - 1,) + quarter, quarter, (o - 1,) + lead + tail]
    shapes = (early if leg != "late" else []) + [half] + (late if leg != "early" else [])
    out = [pltpu.VMEM(lead + tail, jnp.float32)] if leg != "early" else []
    return [pltpu.VMEM(shape, LOW) for shape in shapes] + out


def sum_count(sizes):
    return 4 + sum(n - 1 for n in sizes)


def source_of_core(kind, array, start):
    blocks = slice(start, start + 2)
    if kind == "down":
        return lambda core: array.at[:, core, :, :, blocks]
    return lambda core: array.at[blocks, :, core]


class Rider:
    def __init__(self, sizes, r, width, legs, steps, number):
        self.sizes, self.legs, self.steps, self.number = sizes, legs, steps, number
        self.items = [(kind, leg, *item) for kind, leg in legs for item in pair_of(kind, r, width)]
        self.outs, self.scratch, self.inputs = [], [], 0
        for kind, leg in legs:
            self.inputs += 2 if leg == "late" else 1
            if leg == "late":
                self.outs.append(jax.ShapeDtypeStruct((4, r, width), jnp.float32))
            else:
                for order, start, lead, tail in pair_of(kind, r, width):
                    self.outs.append(
                        jax.ShapeDtypeStruct(half_shape(sizes, order, lead, tail), LOW)
                    )
        count = len(self.items) * sum_count(sizes)
        self.scratch = [pltpu.SemaphoreType.DMA((count,)), pltpu.SemaphoreType.DMA((count,))]
        for kind, leg, order, start, lead, tail in self.items:
            self.scratch += sum_buffers(sizes, order, lead, tail, leg)

    def board(self, ins, outs, scratch):
        self.links = Links(self.sizes, *scratch[:2])
        scratch = list(scratch[2:])
        ins, outs = list(ins), list(outs)
        self.sums = {"early": [], "late": []}
        for kind, leg in self.legs:
            if leg == "early":
                array = ins.pop(0)
            else:
                final = outs.pop(0)
            for order, start, lead, tail in pair_of(kind, *scratch[0].shape[-2:]):
                count = 4 if leg == "early" else 5
                bufs = scratch[:count]
                del scratch[:count]
                if leg == "early":
                    source, out = source_of_core(kind, array, start), outs.pop(0)
                else:
                    source, out = ins.pop(0), final.at[start : start + 2]
                item = Sum(self.links, source, order, len(lead), bufs, out, leg)
                self.sums[leg].append(item)

    def begin(self):
        self.links.greet(self.links.neighbours())
        for item in self.sums["late"] + self.sums["early"]:
            item.begin()

    def stage(self, leg, at):
        for item in self.sums[leg]:
            item.stages[at]()

    def end(self):
        for item in self.sums["late"] + self.sums["early"]:
            item.end()

    def step(self, name):
        if name == "begin":
            self.begin()
        elif name == "end":
            self.end()
        else:
            leg, at = name
            if self.sums[leg]:
                self.stage(leg, at)

    def params(self):
        return pltpu.CompilerParams(
            collective_id=self.number, has_side_effects=True, vmem_limit_bytes=VMEM_BYTES
        )


def home_kernel(sizes, legs, *refs):
    inputs, refs = refs[: len(legs) + 1], refs[len(legs) + 1 :]
    vec, sent, late_up, late_down, g_qkv, g_out, g_up, g_down, g_vec, back = refs[:10]
    links = Links(sizes, *refs[10:12])
    whole = Whole(links, vec, refs[12:21], g_vec)
    refs = list(refs[21:])
    width = vec.shape[-1]

    def place(layer_at, kind, j):
        if kind == "down":
            return g_down.at[layer_at, j]
        if kind == "attn" and j == 3:
            return g_out.at[layer_at]
        return (g_qkv if kind == "attn" else g_up).at[layer_at, :, j * width : (j + 1) * width]

    links.greet(links.partners())
    inputs = list(inputs)
    groups = []
    for kind, leg in legs:
        if leg == "both":
            array = inputs.pop(0)
        group = []
        for order, start, lead, tail in pair_of(kind, *refs[0].shape[-2:]):
            count = 5 if leg == "late" else 8
            bufs = refs[:count]
            del refs[:count]
            source = inputs.pop(0) if leg == "late" else source_of_core(kind, array, start)
            out = [place(int(leg == "late"), kind, j) for j in (start, start + 1)]
            group.append(Sum(links, source, order, len(lead), bufs, out, leg))
        groups.append(group)
    groups[0].append(whole)
    sums = [item for group in groups for item in group]
    for item in sums:
        item.begin()
    moved = deal_back(links, sent, back)
    for j in range(4):
        moved.append(links.start_here(late_up.at[j], place(1, "up", j)))
        moved.append(links.start_here(late_down.at[j], place(1, "down", j)))
    for turn in range(len(groups) + 3):
        for depth in range(4):
            if 0 <= turn - depth < len(groups):
                for item in groups[turn - depth]:
                    item.stages[depth]()
    for item in sums:
        item.end()
    for copy in moved:
        copy.wait()


def take_home(sizes, halves, grads, vec, sent, late):
    dws, dwu, dwd = grads
    r, width = dws.shape[-2:]
    legs = [("attn", "late"), ("down", "both"), ("up", "both"), ("attn", "both")]
    members = sizes[2] * sizes[3]
    f32 = jnp.float32
    batch, two, count, rows = sent.shape[:4]
    outs = [
        jax.ShapeDtypeStruct((LAYERS, r, 3 * width), f32),
        jax.ShapeDtypeStruct((LAYERS, r, width), f32),
        jax.ShapeDtypeStruct((LAYERS, r, 4 * width), f32),
        jax.ShapeDtypeStruct((LAYERS, 4, r, width), f32),
        jax.ShapeDtypeStruct(vec.shape, f32),
        jax.ShapeDtypeStruct((batch, count, two, rows, width), LOW),
    ]
    args = [*halves, dwd, dwu, dws, vec, sent, *late]
    scratch = whole_buffers(sizes, vec.shape)
    for kind, leg in legs:
        for order, start, lead, tail in pair_of(kind, r, width):
            scratch += sum_buffers(sizes, order, lead, tail, leg)
    count = (2 * len(legs) + 1) * sum_count(sizes) + members + 8
    sems = [pltpu.SemaphoreType.DMA((count,)), pltpu.SemaphoreType.DMA((count,))]
    return pl.pallas_call(
        lambda *refs: home_kernel(sizes, legs, *refs),
        out_shape=outs,
        in_specs=[HBM] * len(args),
        out_specs=[HBM] * len(outs),
        scratch_shapes=sems + scratch,
        compiler_params=pltpu.CompilerParams(
            collective_id=1, has_side_effects=True, vmem_limit_bytes=VMEM_BYTES
        ),
        name="take_home",
    )(*args)


def bin_mask(first_blocks, second_blocks, random_pair):
    block_ids = jnp.arange(NBLK)
    later_seg = block_ids >= first_blocks
    rel_block = jnp.where(later_seg, block_ids - first_blocks, block_ids)
    seg_len = jnp.where(later_seg, second_blocks, first_blocks)
    live_block = block_ids < first_blocks + second_blocks
    rand_rows = jnp.where(
        later_seg[:, None],
        jnp.take(random_pair[1], rel_block, axis=0),
        jnp.take(random_pair[0], rel_block, axis=0),
    )
    picked = jnp.remainder(rand_rows, seg_len[:, None])
    row_rel = rel_block[:, None]
    col_rel = rel_block[None, :]
    row_len = seg_len[:, None]
    nearby = jnp.abs(row_rel - col_rel) <= 1
    global_hit = (
        (col_rel == 0) | (col_rel == row_len - 1) | (row_rel == 0) | (row_rel == row_len - 1)
    )
    random_hit = jnp.any(picked[:, :, None] == rel_block[None, None, :], axis=1)
    same_seg = (
        (later_seg[:, None] == later_seg[None, :]) & live_block[:, None] & live_block[None, :]
    )
    allowed = (nearby | global_hit | random_hit) & same_seg
    return jnp.repeat(jnp.repeat(allowed, BLOCK, axis=0), BLOCK, axis=1)


def dot(left, right):
    return jnp.dot(left, right, preferred_element_type=jnp.float32)


def dot_back(left, right):
    return lax.dot_general(left, right, (((1,), (1,)), ((), ())), preferred_element_type=jnp.float32)


def dot_weight(left, right):
    return lax.dot_general(left, right, (((0,), (0,)), ((), ())), preferred_element_type=jnp.float32)


LOW = jnp.bfloat16
LANES = 128
BQ, BV, BO, GA, BA, BD, GF, BF, BU = range(9)


def layer_norm(residual):
    center = residual - jnp.mean(residual, axis=-1, keepdims=True)
    inv_std = lax.rsqrt(jnp.mean(center * center, axis=-1, keepdims=True) + epsilon)
    return (center * inv_std, inv_std)


def norm_back(grad_out, normed, inv_std, gain):
    scaled = grad_out * gain
    return inv_std * (
        scaled
        - jnp.mean(scaled, axis=-1, keepdims=True)
        - normed * jnp.mean(scaled * normed, axis=-1, keepdims=True)
    )


def gelu_parts(u):
    root = 0.7978845608028654
    t = jnp.tanh(root * (u + 0.044715 * (u * u * u)))
    half = 0.5 * (1.0 + t)
    slope = half + 0.5 * u * (1.0 - t * t) * (root * (1.0 + 3 * 0.044715 * (u * u)))
    return (u * half, slope)


def lanes_of(pair, head):
    return pair[:, head * HEAD_DIM : (head + 1) * HEAD_DIM]


def pair_at(pair, offset=0):
    return pl.ds(pl.multiple_of(offset + pair * 2 * HEAD_DIM, 2 * HEAD_DIM), 2 * HEAD_DIM)


def lane_ids(rows):
    return lax.broadcasted_iota(jnp.int32, (rows, LANES), 1)


def attn_fwd_kernel(x_ref, w_ref, v_ref, mask_ref, qkv_ref, ctx_ref, stat_ref, normed_ref):
    rows, width = x_ref.shape
    act = x_ref[...].astype(LOW)
    for j, bias in enumerate((BQ, None, BV)):
        out = dot(act, w_ref[0, j])
        if bias is not None:
            out = out + v_ref[0, bias : bias + 1, :]
        qkv_ref[:, j * width : (j + 1) * width] = out.astype(LOW)
    scale = HEAD_DIM ** (-0.5)
    lanes = lane_ids(rows)
    stat_ref[...] = jnp.zeros_like(stat_ref)

    def pair_step(pair, carry):
        q = qkv_ref[:, pair_at(pair)]
        k = qkv_ref[:, pair_at(pair, width)]
        v = qkv_ref[:, pair_at(pair, 2 * width)]
        mixed = []
        for head in range(2):
            s = dot_back(lanes_of(q, head), lanes_of(k, head)) * scale
            s = jnp.where(mask_ref[0] > 0, s, NEG)
            top = jnp.max(s, axis=-1, keepdims=True)
            e = jnp.exp(s - top)
            total = jnp.sum(e, axis=-1, keepdims=True)
            mixed.append(dot(e.astype(LOW), lanes_of(v, head)) / total)
            log_total = top + jnp.log(total)
            stat_ref[...] = jnp.where(lanes == 2 * pair + head, log_total, stat_ref[...])
        ctx_ref[:, pair_at(pair)] = jnp.concatenate(mixed, axis=1).astype(LOW)
        return carry

    lax.fori_loop(0, HEADS // 2, pair_step, 0)
    resid = x_ref[...].astype(jnp.float32) + dot(ctx_ref[...], w_ref[0, 3])
    normed, inv = layer_norm(resid + v_ref[0, BO : BO + 1, :])
    normed_ref[...] = normed
    stat_ref[...] = jnp.where(lanes == HEADS, inv, stat_ref[...])


def attn_fwd(x, square, vectors, mask, layer_at):
    rows, width = x.shape
    bins, block = mask.shape[:2]
    row = lambda n: pl.BlockSpec((block, n), lambda b: (b, 0))
    f32 = jnp.float32
    return pl.pallas_call(
        attn_fwd_kernel,
        grid=(bins,),
        in_specs=[
            row(width),
            pl.BlockSpec((1, 4, width, width), lambda b: (layer_at, 0, 0, 0)),
            pl.BlockSpec((1,) + vectors.shape[1:], lambda b: (layer_at, 0, 0)),
            pl.BlockSpec((1, block, block), lambda b: (b, 0, 0)),
        ],
        out_specs=[row(3 * width), row(width), row(LANES), row(width)],
        out_shape=[
            jax.ShapeDtypeStruct((rows, 3 * width), LOW),
            jax.ShapeDtypeStruct((rows, width), LOW),
            jax.ShapeDtypeStruct((rows, LANES), f32),
            jax.ShapeDtypeStruct((rows, width), f32),
        ],
        name="attn_fwd",
    )(x, square, vectors, mask)


def middle_of(normed_ref, v_ref):
    return normed_ref[...] * v_ref[0, GA : GA + 1, :] + v_ref[0, BA : BA + 1, :]


def bias_up_of(v_ref, at, count):
    picked = v_ref[0, BU : BU + 1, :]
    for j in range(1, count):
        picked = jnp.where(at == j, v_ref[0, BU + j : BU + j + 1, :], picked)
    return picked


def mlp_fwd_kernel(
    count, normed_ref, wu_ref, wd_ref, v_ref, up_ref, out_ref, low_ref, fnorm_ref, stat_ref, mid, acc
):
    at = pl.program_id(0)

    @pl.when(at == 0)
    def _():
        mid[...] = middle_of(normed_ref, v_ref).astype(LOW)
        acc[...] = jnp.zeros_like(acc)

    up = dot(mid[...], wu_ref[0, 0]) + bias_up_of(v_ref, at, count)
    up_ref[...] = up
    acc[...] += dot(gelu_parts(up)[0].astype(LOW), wd_ref[0])

    @pl.when(at == count - 1)
    def _():
        resid = middle_of(normed_ref, v_ref) + acc[...] + v_ref[0, BD : BD + 1, :]
        normed, inv = layer_norm(resid)
        fnorm_ref[...] = normed
        stat_ref[...] = jnp.broadcast_to(inv, stat_ref.shape)
        out = normed * v_ref[0, GF : GF + 1, :] + v_ref[0, BF : BF + 1, :]
        out_ref[...] = out
        low_ref[...] = out.astype(LOW)


def mlp_fwd(normed, square, down, vectors, layer_at):
    rows, width = normed.shape
    count = down.shape[1] // width
    whole = lambda n: pl.BlockSpec((rows, n), lambda j: (0, 0))
    f32 = jnp.float32
    return pl.pallas_call(
        lambda *refs: mlp_fwd_kernel(count, *refs),
        grid=(count,),
        in_specs=[
            whole(width),
            pl.BlockSpec((1, 1, width, width), lambda j: (layer_at, 4 + j, 0, 0)),
            pl.BlockSpec((1, width, width), lambda j: (layer_at, j, 0)),
            pl.BlockSpec((1,) + vectors.shape[1:], lambda j: (layer_at, 0, 0)),
        ],
        out_specs=[
            pl.BlockSpec((rows, width), lambda j: (0, j)),
            whole(width),
            whole(width),
            whole(width),
            whole(LANES),
        ],
        out_shape=[
            jax.ShapeDtypeStruct((rows, count * width), f32),
            jax.ShapeDtypeStruct((rows, width), f32),
            jax.ShapeDtypeStruct((rows, width), LOW),
            jax.ShapeDtypeStruct((rows, width), f32),
            jax.ShapeDtypeStruct((rows, LANES), f32),
        ],
        scratch_shapes=[pltpu.VMEM((rows, width), LOW), pltpu.VMEM((rows, width), f32)],
        name="mlp_fwd",
    )(normed, square, down, vectors)


def sum_rows(values):
    return jnp.sum(values, axis=0, keepdims=True)


def aboard(refs, rider, ins, outs):
    if rider is None:
        return refs, lambda here, part: None
    rest = refs[ins + rider.inputs :]
    middle, last = len(rider.outs), len(rider.scratch)
    own = refs[:ins] + rest[:outs] + rest[outs + middle : len(rest) - last]
    rider.board(refs[ins : ins + rider.inputs], rest[outs : outs + middle], rest[len(rest) - last :])

    def ride(here, part):
        for grid_at, due, name in rider.steps:
            if due == part:

                @pl.when(here(grid_at))
                def _(name=name):
                    rider.step(name)

    return own, ride


def carried(rider, in_specs, out_specs, out_shape, scratch):
    if rider is not None:
        in_specs = in_specs + [HBM] * rider.inputs
        out_specs = out_specs + [HBM] * len(rider.outs)
        out_shape = out_shape + rider.outs
        scratch = scratch + rider.scratch
    found = dict(
        in_specs=in_specs, out_specs=out_specs, out_shape=out_shape, scratch_shapes=scratch
    )
    if rider is not None:
        found["compiler_params"] = rider.params()
    return found


MLP_STEPS = [
    (0, 0, "begin"),
    (0, 1, ("late", 0)),
    (0, 2, ("early", 0)),
    (1, 1, ("late", 1)),
    (3, 1, ("early", 1)),
    (3, 2, ("late", 2)),
    (3, 3, "end"),
]
ATTN_STEPS = [
    (0, 0, "begin"),
    (0, 2, ("late", 0)),
    (0, 3, ("early", 0)),
    (0, 6, ("late", 1)),
    (1, 4, ("early", 1)),
    (1, 7, ("late", 2)),
    (1, 7, "end"),
]


def mlp_bwd_kernel(count, rider, *refs):
    own, ride = aboard(refs, rider, 9, 4)
    grad_ref, fnorm_ref, fstat_ref, normed_ref, stat_ref, up_ref, wu_ref, wd_ref, v_ref = own[:9]
    dwu_ref, dwd_ref, grad_a_ref, vec_ref, mid, grad_f, low_f, acc = own[9:]
    at = pl.program_id(0)
    here = lambda step: at == step
    ride(here, 0)

    @pl.when(at == 0)
    def _():
        grad_out, normed = grad_ref[...].astype(jnp.float32), fnorm_ref[...]
        vec_ref[...] = jnp.zeros_like(vec_ref)
        vec_ref[GF : GF + 1, :] = sum_rows(grad_out * normed)
        vec_ref[BF : BF + 1, :] = sum_rows(grad_out)
        grad = norm_back(grad_out, normed, fstat_ref[:, :1], v_ref[0, GF : GF + 1, :])
        vec_ref[BD : BD + 1, :] = sum_rows(grad)
        grad_f[...] = grad
        low_f[...] = grad.astype(LOW)
        mid[...] = middle_of(normed_ref, v_ref).astype(LOW)
        acc[...] = jnp.zeros_like(acc)

    act, slope = gelu_parts(up_ref[...])
    dwd_ref[...] = dot_weight(act.astype(LOW), low_f[...]).astype(LOW)
    ride(here, 1)
    grad_up = dot_back(low_f[...], wd_ref[0]) * slope
    vec_ref[pl.ds(BU + at, 1), :] = sum_rows(grad_up)
    low_up = grad_up.astype(LOW)
    dwu_ref[0] = dot_weight(mid[...], low_up).astype(LOW)
    acc[...] += dot_back(low_up, wu_ref[0, 0])
    ride(here, 2)

    @pl.when(at == count - 1)
    def _():
        grad_mid, normed = grad_f[...] + acc[...], normed_ref[...]
        vec_ref[GA : GA + 1, :] = sum_rows(grad_mid * normed)
        vec_ref[BA : BA + 1, :] = sum_rows(grad_mid)
        inv = stat_ref[:, HEADS : HEADS + 1]
        grad = norm_back(grad_mid, normed, inv, v_ref[0, GA : GA + 1, :])
        vec_ref[BO : BO + 1, :] = sum_rows(grad)
        grad_a_ref[...] = grad

    ride(here, 3)


def mlp_bwd(
    grad, fnorm, fstat, normed, stat, up, square, down, vectors, layer_at, rider=None, load=()
):
    rows, width = normed.shape
    count = down.shape[1] // width
    whole = lambda n: pl.BlockSpec((rows, n), lambda j: (0, 0))
    f32 = jnp.float32
    vec_rows = vectors.shape[1]
    in_specs = [
        whole(width),
        whole(width),
        whole(LANES),
        whole(width),
        whole(LANES),
        pl.BlockSpec((rows, width), lambda j: (0, j)),
        pl.BlockSpec((1, 1, width, width), lambda j: (layer_at, 4 + j, 0, 0)),
        pl.BlockSpec((1, width, width), lambda j: (layer_at, j, 0)),
        pl.BlockSpec((1, vec_rows, width), lambda j: (layer_at, 0, 0)),
    ]
    out_specs = [
        pl.BlockSpec((1, width, width), lambda j: (j, 0, 0)),
        pl.BlockSpec((width, width), lambda j: (j, 0)),
        whole(width),
        pl.BlockSpec((vec_rows, width), lambda j: (0, 0)),
    ]
    out_shape = [
        jax.ShapeDtypeStruct((count, width, width), LOW),
        jax.ShapeDtypeStruct((count * width, width), LOW),
        jax.ShapeDtypeStruct((rows, width), f32),
        jax.ShapeDtypeStruct((vec_rows, width), f32),
    ]
    scratch = [
        pltpu.VMEM((rows, width), LOW),
        pltpu.VMEM((rows, width), f32),
        pltpu.VMEM((rows, width), LOW),
        pltpu.VMEM((rows, width), f32),
    ]
    return pl.pallas_call(
        lambda *refs: mlp_bwd_kernel(count, rider, *refs),
        grid=(count,),
        name="mlp_bwd" if rider is None else "mlp_bwd_sums",
        **carried(rider, in_specs, out_specs, out_shape, scratch),
    )(grad, fnorm, fstat, normed, stat, up, square, down, vectors, *load)


def attn_bwd_kernel(rider, *refs):
    own, ride = aboard(refs, rider, 6, 4)
    grad_ref, qkv_ref, stat_ref, mask_ref, w_ref, vec_in = own[:6]
    dqkv_ref, grad_in_ref, low_ref, vec_ref, gctx = own[6:]
    rows, width = grad_ref.shape
    bin_at = pl.program_id(0)
    ride(lambda step: bin_at == step, 0)

    @pl.when(pl.program_id(0) == 0)
    def _():
        vec_ref[...] = vec_in[...]

    low_ref[...] = grad_ref[...].astype(LOW)
    gctx[...] = dot_back(low_ref[...], w_ref[0, 3]).astype(LOW)
    scale = HEAD_DIM ** (-0.5)
    lanes = lane_ids(rows)

    def pair_step(pair, carry):
        for part in range(HEADS // 2):
            ride(lambda step: (bin_at == step) & (pair == part), 1 + part)
        q = qkv_ref[:, pair_at(pair)]
        k = qkv_ref[:, pair_at(pair, width)]
        v = qkv_ref[:, pair_at(pair, 2 * width)]
        g = gctx[:, pair_at(pair)]
        grads = [[], [], []]
        for head in range(2):
            qh, kh, vh, gh = (lanes_of(t, head) for t in (q, k, v, g))
            log_total = jnp.sum(
                jnp.where(lanes == 2 * pair + head, stat_ref[...], 0.0), axis=-1, keepdims=True
            )
            s = dot_back(qh, kh) * scale
            s = jnp.where(mask_ref[0] > 0, s, NEG)
            p = jnp.exp(s - log_total)
            grad_p = dot_back(gh, vh)
            inner = jnp.sum(grad_p * p, axis=-1, keepdims=True)
            low_s = (p * (grad_p - inner)).astype(LOW)
            grads[0].append(dot(low_s, kh) * scale)
            grads[1].append(dot_weight(low_s, qh) * scale)
            grads[2].append(dot_weight(p.astype(LOW), gh))
        for j, row in ((0, BQ), (1, None), (2, BV)):
            both = jnp.concatenate(grads[j], axis=1)
            dqkv_ref[:, pair_at(pair, j * width)] = both.astype(LOW)
            if row is not None:
                vec_ref[row : row + 1, pair_at(pair)] += sum_rows(both)
        return carry

    lax.fori_loop(0, HEADS // 2, pair_step, 0)
    total = grad_ref[...]
    for j in range(3):
        total = total + dot_back(dqkv_ref[:, j * width : (j + 1) * width], w_ref[0, j])
    grad_in_ref[...] = total
    ride(lambda step: bin_at == step, 1 + HEADS // 2)


def attn_bwd(grad_a, qkv, stat, mask, square, vec, layer_at, rider=None, load=()):
    rows, width = grad_a.shape
    bins, block = mask.shape[:2]
    row = lambda n: pl.BlockSpec((block, n), lambda b: (b, 0))
    fixed = pl.BlockSpec(vec.shape, lambda b: (0, 0))
    f32 = jnp.float32
    in_specs = [
        row(width),
        row(3 * width),
        row(LANES),
        pl.BlockSpec((1, block, block), lambda b: (b, 0, 0)),
        pl.BlockSpec((1, 4, width, width), lambda b: (layer_at, 0, 0, 0)),
        fixed,
    ]
    out_shape = [
        jax.ShapeDtypeStruct((rows, 3 * width), LOW),
        jax.ShapeDtypeStruct((rows, width), f32),
        jax.ShapeDtypeStruct((rows, width), LOW),
        jax.ShapeDtypeStruct(vec.shape, f32),
    ]
    out_specs = [row(3 * width), row(width), row(width), fixed]
    scratch = [pltpu.VMEM((block, width), LOW)]
    return pl.pallas_call(
        lambda *refs: attn_bwd_kernel(rider, *refs),
        grid=(bins,),
        name=f"attn_bwd_sums{rider.number}",
        **carried(rider, in_specs, out_specs, out_shape, scratch),
    )(grad_a, qkv, stat, mask, square, vec, *load)


def attn_dw_kernel(act_ref, dqkv_ref, ctx_ref, low_ref, out_ref):
    at = pl.program_id(0)

    @pl.when(at < 3)
    def _():
        out_ref[0] = dot_weight(act_ref[...].astype(LOW), dqkv_ref[...]).astype(LOW)

    @pl.when(at == 3)
    def _():
        out_ref[0] = dot_weight(ctx_ref[...], low_ref[...]).astype(LOW)


def attn_dw(act, dqkv, ctx, low):
    rows, width = act.shape
    whole = pl.BlockSpec((rows, width), lambda j: (0, 0))
    return pl.pallas_call(
        attn_dw_kernel,
        grid=(4,),
        in_specs=[
            whole,
            pl.BlockSpec((rows, width), lambda j: (0, jnp.minimum(j, 2))),
            whole,
            whole,
        ],
        out_specs=pl.BlockSpec((1, width, width), lambda j: (j, 0, 0)),
        out_shape=jax.ShapeDtypeStruct((4, width, width), LOW),
        name="attn_dw",
    )(act, dqkv, ctx, low)


SMALL = ("bq", "bv", "bo", "ga", "ba", "bd", "gf", "bf", "bu")


def small_rows(p, layer_at, width):
    small = jnp.concatenate([p[name][layer_at] for name in SMALL])
    return jnp.pad(small, (0, 8 * width - small.shape[0])).reshape(8, width)


def vectors_of(all_small, rows):
    layers, width = all_small.shape[0], all_small.shape[-1]
    flat = all_small.reshape(layers, -1, 8 * width).astype(jnp.float32)
    even = flat[:, :, : 8 * rows].reshape(layers, -1, 8, rows).transpose(0, 2, 1, 3)
    up = flat[:, :, 8 * rows : 12 * rows]
    return jnp.concatenate([even.reshape(layers, 8, width), up.reshape(layers, 4, width)], axis=1)


def forward(hidden, act_in, w, mask, layer_at):
    square, down, vectors = w
    qkv, ctx, stat, normed = attn_fwd(hidden, square, vectors, mask, layer_at)
    up, out, out_low, fnorm, fstat = mlp_fwd(normed, square, down, vectors, layer_at)
    return out, out_low, (act_in, qkv, ctx, stat, normed, up, fnorm, fstat)


def backward_layers(grad, back, kept, w, mask, sizes, rows):
    square, down, vectors = w
    width = square.shape[-1]

    def of_mlp(grad, layer_at, *more):
        act_in, qkv, ctx, stat, normed, up, fnorm, fstat = kept[layer_at]
        return mlp_bwd(
            grad, fnorm, fstat, normed, stat, up, square, down, vectors, layer_at, *more
        )

    def of_attn(grad_a, vec, layer_at, *more):
        act_in, qkv, ctx, stat, *unused = kept[layer_at]
        dqkv, grad_in, low_a, vec, *sums = attn_bwd(
            grad_a, qkv, stat, mask, square, vec, layer_at, *more
        )
        return grad_in, attn_dw(act_in, dqkv, ctx, low_a), vec, sums

    blocks_out = lambda t: t.reshape((4,) + sizes + (rows, width))
    rows_out = lambda t: t.reshape(sizes + (4, rows, width))
    dwu, dwd, grad_a, vec = of_mlp(grad, 1)
    rider = Rider(sizes, rows, width, [("down", "early")], ATTN_STEPS, 2)
    grad, dws, vec_late, halves = of_attn(grad_a, vec, 1, rider, [rows_out(dwd)])
    grad, back = lax.optimization_barrier((grad, back))
    rider = Rider(sizes, rows, width, [("down", "late"), ("up", "early")], MLP_STEPS, 3)
    dwu, dwd, grad_a, vec, g_down, *halves = of_mlp(grad, 0, rider, [*halves, blocks_out(dwu)])
    rider = Rider(sizes, rows, width, [("up", "late"), ("attn", "early")], ATTN_STEPS, 4)
    grad, dws, vec, (g_up, *halves) = of_attn(grad_a, vec, 0, rider, [*halves, blocks_out(dws)])
    left = (blocks_out(dws), blocks_out(dwu), rows_out(dwd))
    return grad, back, (g_up, g_down), (halves, left, jnp.stack([vec, vec_late]))


def shift_down(rows, amount):
    doubled = jnp.concatenate([jnp.zeros_like(rows), rows], axis=0)
    return lax.dynamic_slice_in_dim(doubled, rows.shape[0] - amount, rows.shape[0], 0)


def shift_up(rows, amount):
    doubled = jnp.concatenate([rows, jnp.zeros_like(rows)], axis=0)
    return lax.dynamic_slice_in_dim(doubled, amount, rows.shape[0], 0)


def pack_bin(slots, first_len, second_len):
    positions = jnp.arange(slots.shape[1])[:, None]
    later = shift_down(jnp.where(positions < second_len, slots[1], 0), first_len)
    return jnp.where(positions < first_len, slots[0], later)


def unpack_bin(rows, first_len, second_len):
    positions = jnp.arange(rows.shape[0])[:, None]
    first = jnp.where(positions < first_len, rows, 0)
    second = jnp.where(positions < second_len, shift_up(rows, first_len), 0)
    return jnp.stack([first, second])


def per_device(tokens_in, cotangent, lengths, bin_deal, random_blocks, *weights):
    names = ("wqkv", "bq", "bv", "wo", "bo", "ga", "ba", "wu", "bu", "wd", "bd", "gf", "bf")
    p = dict(zip(names, weights))
    rows = p["wo"].shape[1]
    members = lax.axis_size("fsdp")
    member = lax.axis_index("fsdp")
    group_at = lax.axis_index("dp")
    grid = Grid(lax.axis_size("dp"), members)
    slot_count = 2 * members
    slot_ids = jnp.arange(slot_count)
    deal_here = lax.dynamic_index_in_dim(bin_deal, group_at, 1, keepdims=False)
    slot_hits = (deal_here[:, :, None] == slot_ids[None, None, :]).astype(jnp.int32)
    source_of = jnp.sum(slot_hits * slot_ids[None, :, None], axis=1)
    lengths_here = lax.dynamic_slice_in_dim(lengths, group_at * slot_count, slot_count, 1)
    bin_lengths = jnp.take_along_axis(lengths_here, source_of, axis=1)
    random_here = lax.dynamic_slice_in_dim(random_blocks, group_at * slot_count, slot_count, 1)
    batch_count, unused_slots, rows_dev, width = tokens_in.shape
    bin_len = rows_dev * members
    order_index = source_of[:, :, None, None]

    def dealt(array):
        sent = jnp.take_along_axis(array, order_index, axis=1)
        return sent.reshape(batch_count, members, 2, rows_dev, width)

    blocks = lambda w: w.reshape(LAYERS, rows, -1, width).transpose(0, 2, 1, 3)
    square = jnp.concatenate([blocks(p["wqkv"]), blocks(p["wo"]), blocks(p["wu"])], axis=1)
    down = p["wd"].reshape(LAYERS, -1, rows, width)
    small = jnp.stack([small_rows(p, layer_at, width) for layer_at in range(LAYERS)])
    sent_grad = dealt(cotangent)
    got_x, *gathered = bring(grid.sizes, dealt(tokens_in), square, down, small)
    got_x, sent_grad = lax.optimization_barrier((got_x, sent_grad))
    arrived_x = got_x.reshape(batch_count, 2, bin_len, width)
    arrived_grad = lax.all_to_all(
        sent_grad, "fsdp", split_axis=1, concat_axis=3, tiled=True
    )[:, 0]
    square, down, small = gathered
    side = rows * grid.count
    w = (
        square.reshape(LAYERS, -1, side, width),
        down.reshape(LAYERS, -1, width),
        vectors_of(small, rows),
    )
    slot_pair = lax.dynamic_slice_in_dim(bin_lengths, 2 * member, 2, 1)
    random_pair = lax.dynamic_slice_in_dim(random_here, 2 * member, 2, 1)
    allowed = jax.vmap(bin_mask)(slot_pair[:, 0], slot_pair[:, 1], random_pair)
    first_len = slot_pair[:, 0] * BLOCK
    second_len = slot_pair[:, 1] * BLOCK

    def packed(slots):
        bins = [pack_bin(slots[m], first_len[m], second_len[m]) for m in range(batch_count)]
        return jnp.concatenate(bins, axis=0)

    def to_slots(bins):
        bins = bins.reshape(batch_count, bin_len, width)
        slots = [unpack_bin(bins[m], first_len[m], second_len[m]) for m in range(batch_count)]
        return jnp.stack(slots)

    def in_order(back):
        back = back.reshape(batch_count, slot_count, rows_dev, width)
        return jnp.take_along_axis(back, deal_here[:, :, None, None], axis=1)

    mask = allowed.astype(jnp.float32)
    hidden = act_in = packed(arrived_x)
    kept = []
    for layer_at in range(LAYERS):
        hidden, act_in, stored = forward(hidden, act_in, w, mask, layer_at)
        kept.append(stored)
    sent = to_slots(act_in)[:, None]
    back = lax.all_to_all(sent, "fsdp", split_axis=3, concat_axis=1, tiled=True)
    arrived_grad, act_in = lax.optimization_barrier((arrived_grad, act_in))
    grad = packed(arrived_grad)
    grad, back, (g_up, g_down_late), left = backward_layers(grad, back, kept, w, mask, grid.sizes, rows)
    output = in_order(back)
    sent = to_slots(grad.astype(LOW)).reshape(batch_count, 2, members, rows_dev, width)
    g_qkv, g_out, g_up, g_down, g_vec, back = take_home(
        grid.sizes, *left, sent, (g_up, g_down_late)
    )
    input_grad = in_order(back)
    out = {
        "wqkv": g_qkv,
        "wo": g_out,
        "wu": g_up,
        "wd": g_down.reshape(LAYERS, -1, width),
    }
    place = group_at * members + member
    for at, name in enumerate(SMALL):
        values = g_vec[:, at:].reshape(LAYERS, -1) if name == "bu" else g_vec[:, at]
        count = rows * (values.shape[1] // width)
        out[name] = lax.dynamic_slice_in_dim(values, place * count, count, 1)
    return (output, input_grad) + tuple(out[name] for name in names)


def solution(mesh):
    tokens = P(None, "dp", "fsdp", None)
    matrix = P(None, AXES, None)
    vector = P(None, AXES)
    weights = (matrix, vector, vector, matrix, vector, vector, vector)
    weights += (matrix, vector, matrix, vector, vector, vector)
    return jax.shard_map(
        per_device,
        mesh=mesh,
        in_specs=(tokens, tokens, P(), P(), P()) + weights,
        out_specs=(tokens, tokens) + weights,
        check_vma=False,
    )
```

```python
import jax
import jax.numpy as jnp
from jax import lax
from jax.experimental import pallas as pl
from jax.experimental.pallas import tpu as pltpu
from jax.sharding import PartitionSpec as P

HEADS = 12
BLOCK = 64
NBLK = 6
LAYERS = 2
CORES = 2
AXES = ("dp", "fsdp")
NEG = -1000000000.0
HEAD_DIM = 64
VMEM_BYTES = 67043328
DEAL_TURNS = 8


epsilon = 1e-06


def split_fsdp(count):
    inner = 1
    while (2 * inner) ** 2 <= count:
        inner *= 2
    return (count // inner, inner)


class Grid:
    def __init__(self, dp_count, fsdp_count):
        outer, inner = split_fsdp(fsdp_count)
        self.sizes = (dp_count // CORES, CORES, outer, inner)
        dp_at, fsdp_at = lax.axis_index("dp"), lax.axis_index("fsdp")
        self.at = (dp_at // CORES, dp_at % CORES, fsdp_at // inner, fsdp_at % inner)

        self.count = dp_count * fsdp_count


ALL = slice(None)
HBM = pl.BlockSpec(memory_space=pl.ANY)


class Links:
    def __init__(self, sizes, send_sem, recv_sem):
        outer, inner = sizes[2:]
        dp_at, fsdp_at = lax.axis_index("dp"), lax.axis_index("fsdp")
        self.sizes = sizes
        self.at = (dp_at // CORES, dp_at % CORES, fsdp_at // inner, fsdp_at % inner)
        self.send_sem, self.recv_sem = send_sem, recv_sem
        self.used = 0

    def device(self, place):
        return (place[0] * CORES + place[1], place[2] * self.sizes[3] + place[3])

    def along(self, axis, offset):
        place = list(self.at)
        place[axis] = (place[axis] + offset) % self.sizes[axis]
        return self.device(place)

    def plan(self, source, target, device):
        copy = pltpu.make_async_remote_copy(
            src_ref=source,
            dst_ref=target,
            send_sem=self.send_sem.at[self.used],
            recv_sem=self.recv_sem.at[self.used],
            device_id=device,
            device_id_type=pl.DeviceIdType.MESH,
        )
        self.used += 1
        return copy

    def plan_here(self, source, target):
        copy = pltpu.make_async_copy(source, target, self.recv_sem.at[self.used])
        self.used += 1
        return copy

    def start(self, source, target, device):
        copy = self.plan(source, target, device)
        copy.start()
        return copy

    def start_here(self, source, target):
        copy = self.plan_here(source, target)
        copy.start()
        return copy

    def greet(self, devices):
        barrier = pltpu.get_barrier_semaphore()
        for device in devices:
            pl.semaphore_signal(barrier, inc=1, device_id=device, device_id_type=pl.DeviceIdType.MESH)
        pl.semaphore_wait(barrier, len(devices))

    def partners(self):
        found = [self.along(axis, k) for axis in (0, 1) for k in range(1, self.sizes[axis])]
        count = self.sizes[2] * self.sizes[3]
        return found + [self.member(k) for k in range(1, count)]

    def neighbours(self):
        return [self.along(axis, k) for axis in range(4) for k in range(1, self.sizes[axis])]

    def member(self, offset):
        count = self.sizes[2] * self.sizes[3]
        flat = self.at[2] * self.sizes[3] + self.at[3]
        return (self.at[0] * CORES + self.at[1], (flat + offset) % count)


class Gather:
    def __init__(self, links, source, target, order):
        self.links, self.source, self.target, self.order = links, source, target, order
        self.sent = []
        self.across = []

    def begin(self):
        links = self.links
        x, c, o, i = links.at
        spot = self.target(*links.at)
        self.own = links.start_here(self.source, spot)
        if links.sizes[2] != 4:
            self.column = [
                links.start(self.source, spot, links.along(2, k)) for k in range(1, links.sizes[2])
            ]
            return
        self.inside = (o == 1) | (o == 2)
        near = links.device((x, c, o + 1 - 2 * (o % 2), i))
        across = links.device((x, c, 3 - o, i))
        pair = lambda half: self.target(x, c, pl.ds(2 * half, 2), i)
        ours, others = pair(o // 2), pair(1 - o // 2)
        self.column = [links.start(self.source, spot, near)]
        self.pairs = links.plan(ours, ours, across)
        self.outwards = links.plan(others, others, near)

    def cross(self):
        if self.links.sizes[2] != 4:
            return
        self.own.wait()
        self.column[0].wait_recv()

        @pl.when(self.inside)
        def _():
            self.pairs.start()

    def spread(self):
        if self.links.sizes[2] != 4:
            return

        @pl.when(self.inside)
        def _():
            self.pairs.wait_recv()
            self.outwards.start()

    def hand_over(self, spot):
        self.across.append(self.links.start(spot, spot, self.links.along(1, 1)))

    def first(self):
        links = self.links
        x, c, o, i = links.at
        if links.sizes[2] != 4:
            self.own.wait()
            for copy in self.column:
                copy.wait_recv()
        else:

            @pl.when(~self.inside)
            def _():
                self.outwards.wait_recv()

        spot = self.target(x, c, ALL, i)
        axis = self.order[0]
        self.line = [
            links.start(spot, spot, links.along(axis, k)) for k in range(1, links.sizes[axis])
        ]
        self.hand_over(spot)

    def second(self):
        links = self.links
        x, c, o, i = links.at
        for copy in self.line:
            copy.wait_recv()
        first, second = self.order
        spot = self.target(ALL, c, ALL, i) if first == 0 else self.target(x, c, ALL, ALL)
        self.sheet = [
            links.start(spot, spot, links.along(second, k)) for k in range(1, links.sizes[second])
        ]
        for k in range(1, links.sizes[first]):
            near = (links.at[first] - k) % links.sizes[first]
            self.hand_over(
                self.target(near, c, ALL, i) if first == 0 else self.target(x, c, ALL, near)
            )

    def third(self):
        links = self.links
        c = links.at[1]
        second = self.order[1]
        for k, copy in enumerate(self.sheet, 1):
            copy.wait_recv()
            near = (links.at[second] - k) % links.sizes[second]
            self.hand_over(
                self.target(near, c, ALL, ALL) if second == 0 else self.target(ALL, c, ALL, near)
            )

    def end(self):
        for copy in self.across:
            copy.wait()
        for copy in self.column + self.line + self.sheet:
            copy.wait_send()
        if self.links.sizes[2] == 4:

            @pl.when(self.inside)
            def _():
                self.pairs.wait_send()
                self.outwards.wait_send()


def deal_out(links, source, target):
    count = links.sizes[2] * links.sizes[3]
    me = links.at[2] * links.sizes[3] + links.at[3]
    spot = target.at[:, :, me]
    starts = [
        lambda k=k: links.start(source.at[:, (me + k) % count], spot, links.member(k))
        for k in range(1, count)
    ]
    return starts + [lambda: links.start_here(source.at[:, me], spot)]


def deal_back(links, source, target):
    count = links.sizes[2] * links.sizes[3]
    me = links.at[2] * links.sizes[3] + links.at[3]
    spot = target.at[:, me]
    copies = [links.start_here(source.at[:, :, me], spot)]
    for k in range(1, count):
        copies.append(links.start(source.at[:, :, (me + k) % count], spot, links.member(k)))
    return copies


def gathers_of(links, layer_at, square, down, small, all_square, all_down, all_small):
    def of_square(start, order):
        blocks = slice(start, start + 2)
        return Gather(
            links,
            square.at[layer_at, blocks],
            lambda *place: all_square.at[(layer_at, blocks) + place],
            order,
        )

    def of_down(start, order):
        blocks = slice(start, start + 2)
        return Gather(
            links,
            down.at[layer_at, blocks],
            lambda *place: all_down.at[(layer_at,) + place + (blocks,)],
            order,
        )

    tiny = Gather(
        links, small.at[layer_at], lambda *place: all_small.at[(layer_at,) + place], (0, 3)
    )
    return [
        [tiny, of_square(0, (0, 3)), of_square(2, (3, 0))],
        [of_square(4, (0, 3)), of_square(6, (3, 0))],
        [of_down(0, (3, 0)), of_down(2, (3, 0))],
    ]


def bring_kernel(sizes, *refs):
    sent_x, square, down, small = refs[:4]
    got_x, all_square, all_down, all_small = refs[4:8]
    links = Links(sizes, *refs[8:])
    links.greet(links.partners())
    groups = []
    for layer_at in range(LAYERS):
        groups += gathers_of(
            links, layer_at, square, down, small, all_square, all_down, all_small
        )
    starts = deal_out(links, sent_x, got_x)
    share = -(-len(starts) // DEAL_TURNS)
    moved = []

    def run(step, at):
        if 0 <= at < len(groups):
            for item in groups[at]:
                getattr(item, step)()

    run("begin", 0)
    run("begin", 1)
    run("cross", 0)
    run("spread", 0)
    run("cross", 1)
    run("begin", 2)
    for at in range(len(groups) + 2):
        run("first", at)
        run("spread", at + 1)
        run("cross", at + 2)
        run("begin", at + 3)
        moved += [start() for start in starts[at * share : (at + 1) * share]]
        run("second", at - 1)
        run("third", at - 2)
    for group in groups:
        for item in group:
            item.end()
    for copy in moved:
        copy.wait()


def bring(sizes, sent_x, square, down, small):
    low = jnp.bfloat16
    batch, members, two, rows, width = sent_x.shape
    r = square.shape[2]
    got = jax.ShapeDtypeStruct((batch, two, members, rows, width), low)
    outs = [
        got,
        jax.ShapeDtypeStruct((LAYERS, square.shape[1]) + sizes + (r, width), low),
        jax.ShapeDtypeStruct((LAYERS,) + sizes + (down.shape[1], r, width), low),
        jax.ShapeDtypeStruct((LAYERS,) + sizes + (8, width), low),
    ]
    per_item = 3 + sum(n - 1 for n in sizes) + 4 + sizes[0] + sizes[3]
    count = 7 * LAYERS * per_item + members
    return pl.pallas_call(
        lambda *refs: bring_kernel(sizes, *refs),
        out_shape=outs,
        in_specs=[HBM] * 4,
        out_specs=[HBM] * 4,
        scratch_shapes=[pltpu.SemaphoreType.DMA((count,)), pltpu.SemaphoreType.DMA((count,))],
        compiler_params=pltpu.CompilerParams(collective_id=0, has_side_effects=True),
        name="bring",
    )(sent_x, square, down, small)


def each(dims, body):
    total = 1
    for n in dims:
        total *= n

    def step(flat, carry):
        at = []
        for n in reversed(dims):
            at.insert(0, flat % n)
            flat = flat // n
        body(tuple(at))
        return carry

    lax.fori_loop(0, total, step, 0)


def wide(ref, at):
    return ref[at].astype(jnp.float32)


class Sum:
    def __init__(self, links, source, order, lead, bufs, out_ref, leg="both"):
        self.links, self.order, self.lead, self.leg = links, order, lead, leg
        self.sent = []
        c = links.at[1]
        late = (2, 3) if order[0] == 0 else (0, 2)
        if leg == "late":
            self.half = bufs[0]
            self.opening = [links.plan_here(source, self.half)]
        else:
            self.mine, self.theirs, self.first, self.half = bufs[:4]
            there = self.send(source(1 - c), self.theirs, 1, 1)
            self.opening = [links.plan_here(source(c), self.mine), there]
            self.moving_first = self.spread(self.mine, (0, 2, 3), order[0], self.first)
        if leg == "early":
            self.out = self.half
            self.stages = [self.add_core, self.add_first, self.nothing, self.nothing]
        else:
            self.second, self.quarter, self.last, self.out = bufs[-4:]
            self.moving_second = self.spread(self.half, late, order[1], self.second)
            self.moving_last = self.spread(self.quarter, (2,), 2, self.last)
            self.late = late
            self.stages = [self.take_up, self.add_second, self.add_last, self.nothing]
            if leg == "both":
                self.stages = [self.add_core, self.add_first, self.add_second, self.add_last]
        if isinstance(out_ref, list):
            self.results = [links.plan_here(self.out.at[j], ref) for j, ref in enumerate(out_ref)]
        else:
            self.results = [links.plan_here(self.out, out_ref)]

    def send(self, source, target, axis, offset):
        copy = self.links.plan(source, target, self.links.along(axis, offset))
        self.sent.append(copy)
        return copy

    def begin(self):
        for copy in self.opening:
            copy.start()

    def at(self, *place):
        return (ALL,) * self.lead + place

    def spread(self, ref, axes, axis, into):
        size, me = self.links.sizes[axis], self.links.at[axis]
        found = []
        for k in range(1, size):
            place = [ALL] * len(axes)
            place[axes.index(axis)] = (me + k) % size
            found.append(self.send(ref.at[self.at(*place)], into.at[k - 1], axis, k))
        return found

    def fold(self, ref, axes, axis, arrived, into):
        size, me = self.links.sizes[axis], self.links.at[axis]
        spot = axes.index(axis) + self.lead

        def add(at):
            if size == 2 and into.dtype == LOW:
                into[at] = ref[at[:spot] + (me,) + at[spot:]] + arrived[(0,) + at]
                return
            total = wide(ref, at[:spot] + (me,) + at[spot:])
            for k in range(size - 1):
                total = total + wide(arrived, (k,) + at)
            into[at] = total.astype(into.dtype)

        each(into.shape[:-2], add)

    def nothing(self):
        pass

    def add_core(self):
        here, there = self.opening
        here.wait()
        there.wait_recv()

        def add(at):
            self.mine[at] = self.mine[at] + self.theirs[at]

        each(self.mine.shape[:-2], add)
        for copy in self.moving_first:
            copy.start()

    def add_first(self):
        for copy in self.moving_first:
            copy.wait_recv()
        self.fold(self.mine, (0, 2, 3), self.order[0], self.first, self.half)
        for copy in self.results if self.leg == "early" else self.moving_second:
            copy.start()

    def take_up(self):
        self.opening[0].wait()
        for copy in self.moving_second:
            copy.start()

    def add_second(self):
        for copy in self.moving_second:
            copy.wait_recv()
        self.fold(self.half, self.late, self.order[1], self.second, self.quarter)
        for copy in self.moving_last:
            copy.start()

    def add_last(self):
        for copy in self.moving_last:
            copy.wait_recv()
        self.fold(self.quarter, (2,), 2, self.last, self.out)
        for copy in self.results:
            copy.start()

    def end(self):
        for copy in self.results:
            copy.wait()
        for copy in self.sent:
            copy.wait_send()


class Whole:
    def __init__(self, links, source, bufs, out_ref):
        self.links, self.source, self.out_ref = links, source, out_ref
        self.held, self.arrived = bufs[:5], bufs[5:]
        self.sent = []
        self.stages = [self.stage_one, self.stage_two, self.stage_three, self.stage_four]

    def begin(self):
        self.here = self.links.start_here(self.source, self.held[0])

    def send(self, at, axis):
        self.moving = [
            self.links.start(
                self.held[at], self.arrived[at].at[k - 1], self.links.along(axis, k)
            )
            for k in range(1, self.links.sizes[axis])
        ]
        self.sent += self.moving

    def fold(self, at):
        for copy in self.moving:
            copy.wait_recv()
        total = self.held[at][...]
        for k in range(self.arrived[at].shape[0]):
            total = total + self.arrived[at][k]
        self.held[at + 1][...] = total

    def stage_one(self):
        self.here.wait()
        self.send(0, 1)

    def stage_two(self):
        self.fold(0)
        self.send(1, 0)

    def stage_three(self):
        self.fold(1)
        self.send(2, 3)

    def stage_four(self):
        self.fold(2)
        self.send(3, 2)

    def end(self):
        self.fold(3)
        result = self.links.start_here(self.held[4], self.out_ref)
        result.wait()
        for copy in self.sent:
            copy.wait_send()


def whole_buffers(sizes, shape):
    f32 = jnp.float32
    arrived = [pltpu.VMEM((sizes[axis] - 1,) + shape, f32) for axis in (1, 0, 3, 2)]
    return [pltpu.VMEM(shape, f32)] * 5 + arrived


Y_FIRST, X_FIRST = (3, 0), (0, 3)


def pair_of(kind, r, width):
    lead, tail = ((), (2, r, width)) if kind == "down" else ((2,), (r, width))
    return [(Y_FIRST, 0, lead, tail), (X_FIRST, 2, lead, tail)]


def half_shape(sizes, order, lead, tail):
    x, c, o, i = sizes
    return lead + ((x, o) if order[0] == 3 else (o, i)) + tail


def sum_buffers(sizes, order, lead, tail, leg="both"):
    x, c, o, i = sizes
    whole = lead + (x, o, i) + tail
    half = half_shape(sizes, order, lead, tail)
    quarter = lead + (o,) + tail
    early = [whole, whole, (sizes[order[0]] - 1,) + half]
    late = [(sizes[order[1]] - 1,) + quarter, quarter, (o - 1,) + lead + tail]
    shapes = (early if leg != "late" else []) + [half] + (late if leg != "early" else [])
    out = [pltpu.VMEM(lead + tail, jnp.float32)] if leg != "early" else []
    return [pltpu.VMEM(shape, LOW) for shape in shapes] + out


def sum_count(sizes):
    return 4 + sum(n - 1 for n in sizes)


def source_of_core(kind, array, start):
    blocks = slice(start, start + 2)
    if kind == "down":
        return lambda core: array.at[:, core, :, :, blocks]
    return lambda core: array.at[blocks, :, core]


class Rider:
    def __init__(self, sizes, r, width, legs, steps, number):
        self.sizes, self.legs, self.steps, self.number = sizes, legs, steps, number
        self.items = [(kind, leg, *item) for kind, leg in legs for item in pair_of(kind, r, width)]
        self.outs, self.scratch, self.inputs = [], [], 0
        for kind, leg in legs:
            self.inputs += 2 if leg == "late" else 1
            if leg == "late":
                self.outs.append(jax.ShapeDtypeStruct((4, r, width), jnp.float32))
            else:
                for order, start, lead, tail in pair_of(kind, r, width):
                    self.outs.append(
                        jax.ShapeDtypeStruct(half_shape(sizes, order, lead, tail), LOW)
                    )
        count = len(self.items) * sum_count(sizes)
        self.scratch = [pltpu.SemaphoreType.DMA((count,)), pltpu.SemaphoreType.DMA((count,))]
        for kind, leg, order, start, lead, tail in self.items:
            self.scratch += sum_buffers(sizes, order, lead, tail, leg)

    def board(self, ins, outs, scratch):
        self.links = Links(self.sizes, *scratch[:2])
        scratch = list(scratch[2:])
        ins, outs = list(ins), list(outs)
        self.sums = {"early": [], "late": []}
        for kind, leg in self.legs:
            if leg == "early":
                array = ins.pop(0)
            else:
                final = outs.pop(0)
            for order, start, lead, tail in pair_of(kind, *scratch[0].shape[-2:]):
                count = 4 if leg == "early" else 5
                bufs = scratch[:count]
                del scratch[:count]
                if leg == "early":
                    source, out = source_of_core(kind, array, start), outs.pop(0)
                else:
                    source, out = ins.pop(0), final.at[start : start + 2]
                item = Sum(self.links, source, order, len(lead), bufs, out, leg)
                self.sums[leg].append(item)

    def begin(self):
        self.links.greet(self.links.neighbours())
        for item in self.sums["late"] + self.sums["early"]:
            item.begin()

    def stage(self, leg, at):
        for item in self.sums[leg]:
            item.stages[at]()

    def end(self):
        for item in self.sums["late"] + self.sums["early"]:
            item.end()

    def step(self, name):
        if name == "begin":
            self.begin()
        elif name == "end":
            self.end()
        else:
            leg, at = name
            if self.sums[leg]:
                self.stage(leg, at)

    def params(self):
        return pltpu.CompilerParams(
            collective_id=self.number, has_side_effects=True, vmem_limit_bytes=VMEM_BYTES
        )


def home_kernel(sizes, legs, *refs):
    inputs, refs = refs[: len(legs) + 1], refs[len(legs) + 1 :]
    vec, sent, late_up, late_down, g_qkv, g_out, g_up, g_down, g_vec, back = refs[:10]
    links = Links(sizes, *refs[10:12])
    whole = Whole(links, vec, refs[12:21], g_vec)
    refs = list(refs[21:])
    width = vec.shape[-1]

    def place(layer_at, kind, j):
        if kind == "down":
            return g_down.at[layer_at, j]
        if kind == "attn" and j == 3:
            return g_out.at[layer_at]
        return (g_qkv if kind == "attn" else g_up).at[layer_at, :, j * width : (j + 1) * width]

    links.greet(links.partners())
    inputs = list(inputs)
    groups = []
    for kind, leg in legs:
        if leg == "both":
            array = inputs.pop(0)
        group = []
        for order, start, lead, tail in pair_of(kind, *refs[0].shape[-2:]):
            count = 5 if leg == "late" else 8
            bufs = refs[:count]
            del refs[:count]
            source = inputs.pop(0) if leg == "late" else source_of_core(kind, array, start)
            out = [place(int(leg == "late"), kind, j) for j in (start, start + 1)]
            group.append(Sum(links, source, order, len(lead), bufs, out, leg))
        groups.append(group)
    groups[0].append(whole)
    sums = [item for group in groups for item in group]
    for item in sums:
        item.begin()
    moved = deal_back(links, sent, back)
    for j in range(4):
        moved.append(links.start_here(late_up.at[j], place(1, "up", j)))
        moved.append(links.start_here(late_down.at[j], place(1, "down", j)))
    for turn in range(len(groups) + 3):
        for depth in range(4):
            if 0 <= turn - depth < len(groups):
                for item in groups[turn - depth]:
                    item.stages[depth]()
    for item in sums:
        item.end()
    for copy in moved:
        copy.wait()


def take_home(sizes, halves, grads, vec, sent, late):
    dws, dwu, dwd = grads
    r, width = dws.shape[-2:]
    legs = [("attn", "late"), ("down", "both"), ("up", "both"), ("attn", "both")]
    members = sizes[2] * sizes[3]
    f32 = jnp.float32
    batch, two, count, rows = sent.shape[:4]
    outs = [
        jax.ShapeDtypeStruct((LAYERS, r, 3 * width), f32),
        jax.ShapeDtypeStruct((LAYERS, r, width), f32),
        jax.ShapeDtypeStruct((LAYERS, r, 4 * width), f32),
        jax.ShapeDtypeStruct((LAYERS, 4, r, width), f32),
        jax.ShapeDtypeStruct(vec.shape, f32),
        jax.ShapeDtypeStruct((batch, count, two, rows, width), LOW),
    ]
    args = [*halves, dwd, dwu, dws, vec, sent, *late]
    scratch = whole_buffers(sizes, vec.shape)
    for kind, leg in legs:
        for order, start, lead, tail in pair_of(kind, r, width):
            scratch += sum_buffers(sizes, order, lead, tail, leg)
    count = (2 * len(legs) + 1) * sum_count(sizes) + members + 8
    sems = [pltpu.SemaphoreType.DMA((count,)), pltpu.SemaphoreType.DMA((count,))]
    return pl.pallas_call(
        lambda *refs: home_kernel(sizes, legs, *refs),
        out_shape=outs,
        in_specs=[HBM] * len(args),
        out_specs=[HBM] * len(outs),
        scratch_shapes=sems + scratch,
        compiler_params=pltpu.CompilerParams(
            collective_id=1, has_side_effects=True, vmem_limit_bytes=VMEM_BYTES
        ),
        name="take_home",
    )(*args)


def bin_mask(first_blocks, second_blocks, random_pair):
    block_ids = jnp.arange(NBLK)
    later_seg = block_ids >= first_blocks
    rel_block = jnp.where(later_seg, block_ids - first_blocks, block_ids)
    seg_len = jnp.where(later_seg, second_blocks, first_blocks)
    live_block = block_ids < first_blocks + second_blocks
    rand_rows = jnp.where(
        later_seg[:, None],
        jnp.take(random_pair[1], rel_block, axis=0),
        jnp.take(random_pair[0], rel_block, axis=0),
    )
    picked = jnp.remainder(rand_rows, seg_len[:, None])
    row_rel = rel_block[:, None]
    col_rel = rel_block[None, :]
    row_len = seg_len[:, None]
    nearby = jnp.abs(row_rel - col_rel) <= 1
    global_hit = (
        (col_rel == 0) | (col_rel == row_len - 1) | (row_rel == 0) | (row_rel == row_len - 1)
    )
    random_hit = jnp.any(picked[:, :, None] == rel_block[None, None, :], axis=1)
    same_seg = (
        (later_seg[:, None] == later_seg[None, :]) & live_block[:, None] & live_block[None, :]
    )
    allowed = (nearby | global_hit | random_hit) & same_seg
    return jnp.repeat(jnp.repeat(allowed, BLOCK, axis=0), BLOCK, axis=1)


def dot(left, right):
    return jnp.dot(left, right, preferred_element_type=jnp.float32)


def dot_back(left, right):
    return lax.dot_general(left, right, (((1,), (1,)), ((), ())), preferred_element_type=jnp.float32)


def dot_weight(left, right):
    return lax.dot_general(left, right, (((0,), (0,)), ((), ())), preferred_element_type=jnp.float32)


LOW = jnp.bfloat16
LANES = 128
BQ, BV, BO, GA, BA, BD, GF, BF, BU = range(9)


def layer_norm(residual):
    center = residual - jnp.mean(residual, axis=-1, keepdims=True)
    inv_std = lax.rsqrt(jnp.mean(center * center, axis=-1, keepdims=True) + epsilon)
    return (center * inv_std, inv_std)


def norm_back(grad_out, normed, inv_std, gain):
    scaled = grad_out * gain
    return inv_std * (
        scaled
        - jnp.mean(scaled, axis=-1, keepdims=True)
        - normed * jnp.mean(scaled * normed, axis=-1, keepdims=True)
    )


def gelu_parts(u):
    root = 0.7978845608028654
    t = jnp.tanh(root * (u + 0.044715 * (u * u * u)))
    half = 0.5 * (1.0 + t)
    slope = half + 0.5 * u * (1.0 - t * t) * (root * (1.0 + 3 * 0.044715 * (u * u)))
    return (u * half, slope)


def lanes_of(pair, head):
    return pair[:, head * HEAD_DIM : (head + 1) * HEAD_DIM]


def pair_at(pair, offset=0):
    return pl.ds(pl.multiple_of(offset + pair * 2 * HEAD_DIM, 2 * HEAD_DIM), 2 * HEAD_DIM)


def lane_ids(rows):
    return lax.broadcasted_iota(jnp.int32, (rows, LANES), 1)


def attn_fwd_kernel(x_ref, w_ref, v_ref, mask_ref, qkv_ref, ctx_ref, stat_ref, normed_ref):
    rows, width = x_ref.shape
    act = x_ref[...].astype(LOW)
    for j, bias in enumerate((BQ, None, BV)):
        out = dot(act, w_ref[0, j])
        if bias is not None:
            out = out + v_ref[0, bias : bias + 1, :]
        qkv_ref[:, j * width : (j + 1) * width] = out.astype(LOW)
    scale = HEAD_DIM ** (-0.5)
    lanes = lane_ids(rows)
    stat_ref[...] = jnp.zeros_like(stat_ref)

    def pair_step(pair, carry):
        q = qkv_ref[:, pair_at(pair)]
        k = qkv_ref[:, pair_at(pair, width)]
        v = qkv_ref[:, pair_at(pair, 2 * width)]
        mixed = []
        for head in range(2):
            s = dot_back(lanes_of(q, head), lanes_of(k, head)) * scale
            s = jnp.where(mask_ref[0] > 0, s, NEG)
            top = jnp.max(s, axis=-1, keepdims=True)
            e = jnp.exp(s - top)
            total = jnp.sum(e, axis=-1, keepdims=True)
            mixed.append(dot(e.astype(LOW), lanes_of(v, head)) / total)
            log_total = top + jnp.log(total)
            stat_ref[...] = jnp.where(lanes == 2 * pair + head, log_total, stat_ref[...])
        ctx_ref[:, pair_at(pair)] = jnp.concatenate(mixed, axis=1).astype(LOW)
        return carry

    lax.fori_loop(0, HEADS // 2, pair_step, 0)
    resid = x_ref[...].astype(jnp.float32) + dot(ctx_ref[...], w_ref[0, 3])
    normed, inv = layer_norm(resid + v_ref[0, BO : BO + 1, :])
    normed_ref[...] = normed
    stat_ref[...] = jnp.where(lanes == HEADS, inv, stat_ref[...])


def attn_fwd(x, square, vectors, mask, layer_at):
    rows, width = x.shape
    bins, block = mask.shape[:2]
    row = lambda n: pl.BlockSpec((block, n), lambda b: (b, 0))
    f32 = jnp.float32
    return pl.pallas_call(
        attn_fwd_kernel,
        grid=(bins,),
        in_specs=[
            row(width),
            pl.BlockSpec((1, 4, width, width), lambda b: (layer_at, 0, 0, 0)),
            pl.BlockSpec((1,) + vectors.shape[1:], lambda b: (layer_at, 0, 0)),
            pl.BlockSpec((1, block, block), lambda b: (b, 0, 0)),
        ],
        out_specs=[row(3 * width), row(width), row(LANES), row(width)],
        out_shape=[
            jax.ShapeDtypeStruct((rows, 3 * width), LOW),
            jax.ShapeDtypeStruct((rows, width), LOW),
            jax.ShapeDtypeStruct((rows, LANES), f32),
            jax.ShapeDtypeStruct((rows, width), f32),
        ],
        name="attn_fwd",
    )(x, square, vectors, mask)


def middle_of(normed_ref, v_ref):
    return normed_ref[...] * v_ref[0, GA : GA + 1, :] + v_ref[0, BA : BA + 1, :]


def bias_up_of(v_ref, at, count):
    picked = v_ref[0, BU : BU + 1, :]
    for j in range(1, count):
        picked = jnp.where(at == j, v_ref[0, BU + j : BU + j + 1, :], picked)
    return picked


def mlp_fwd_kernel(
    count, normed_ref, wu_ref, wd_ref, v_ref, up_ref, out_ref, low_ref, fnorm_ref, stat_ref, mid, acc
):
    at = pl.program_id(0)

    @pl.when(at == 0)
    def _():
        mid[...] = middle_of(normed_ref, v_ref).astype(LOW)
        acc[...] = jnp.zeros_like(acc)

    up = dot(mid[...], wu_ref[0, 0]) + bias_up_of(v_ref, at, count)
    up_ref[...] = up
    acc[...] += dot(gelu_parts(up)[0].astype(LOW), wd_ref[0])

    @pl.when(at == count - 1)
    def _():
        resid = middle_of(normed_ref, v_ref) + acc[...] + v_ref[0, BD : BD + 1, :]
        normed, inv = layer_norm(resid)
        fnorm_ref[...] = normed
        stat_ref[...] = jnp.broadcast_to(inv, stat_ref.shape)
        out = normed * v_ref[0, GF : GF + 1, :] + v_ref[0, BF : BF + 1, :]
        out_ref[...] = out
        low_ref[...] = out.astype(LOW)


def mlp_fwd(normed, square, down, vectors, layer_at):
    rows, width = normed.shape
    count = down.shape[1] // width
    whole = lambda n: pl.BlockSpec((rows, n), lambda j: (0, 0))
    f32 = jnp.float32
    return pl.pallas_call(
        lambda *refs: mlp_fwd_kernel(count, *refs),
        grid=(count,),
        in_specs=[
            whole(width),
            pl.BlockSpec((1, 1, width, width), lambda j: (layer_at, 4 + j, 0, 0)),
            pl.BlockSpec((1, width, width), lambda j: (layer_at, j, 0)),
            pl.BlockSpec((1,) + vectors.shape[1:], lambda j: (layer_at, 0, 0)),
        ],
        out_specs=[
            pl.BlockSpec((rows, width), lambda j: (0, j)),
            whole(width),
            whole(width),
            whole(width),
            whole(LANES),
        ],
        out_shape=[
            jax.ShapeDtypeStruct((rows, count * width), f32),
            jax.ShapeDtypeStruct((rows, width), f32),
            jax.ShapeDtypeStruct((rows, width), LOW),
            jax.ShapeDtypeStruct((rows, width), f32),
            jax.ShapeDtypeStruct((rows, LANES), f32),
        ],
        scratch_shapes=[pltpu.VMEM((rows, width), LOW), pltpu.VMEM((rows, width), f32)],
        name="mlp_fwd",
    )(normed, square, down, vectors)


def sum_rows(values):
    return jnp.sum(values, axis=0, keepdims=True)


def aboard(refs, rider, ins, outs):
    if rider is None:
        return refs, lambda here, part: None
    rest = refs[ins + rider.inputs :]
    middle, last = len(rider.outs), len(rider.scratch)
    own = refs[:ins] + rest[:outs] + rest[outs + middle : len(rest) - last]
    rider.board(refs[ins : ins + rider.inputs], rest[outs : outs + middle], rest[len(rest) - last :])

    def ride(here, part):
        for grid_at, due, name in rider.steps:
            if due == part:

                @pl.when(here(grid_at))
                def _(name=name):
                    rider.step(name)

    return own, ride


def carried(rider, in_specs, out_specs, out_shape, scratch):
    if rider is not None:
        in_specs = in_specs + [HBM] * rider.inputs
        out_specs = out_specs + [HBM] * len(rider.outs)
        out_shape = out_shape + rider.outs
        scratch = scratch + rider.scratch
    found = dict(
        in_specs=in_specs, out_specs=out_specs, out_shape=out_shape, scratch_shapes=scratch
    )
    if rider is not None:
        found["compiler_params"] = rider.params()
    return found


MLP_STEPS = [
    (0, 0, "begin"),
    (0, 1, ("late", 0)),
    (0, 2, ("early", 0)),
    (1, 1, ("late", 1)),
    (3, 1, ("early", 1)),
    (3, 2, ("late", 2)),
    (3, 3, "end"),
]
ATTN_STEPS = [
    (0, 0, "begin"),
    (0, 2, ("late", 0)),
    (0, 3, ("early", 0)),
    (0, 6, ("late", 1)),
    (1, 4, ("early", 1)),
    (1, 7, ("late", 2)),
    (1, 7, "end"),
]


def mlp_bwd_kernel(count, rider, *refs):
    own, ride = aboard(refs, rider, 9, 4)
    grad_ref, fnorm_ref, fstat_ref, normed_ref, stat_ref, up_ref, wu_ref, wd_ref, v_ref = own[:9]
    dwu_ref, dwd_ref, grad_a_ref, vec_ref, mid, grad_f, low_f, acc = own[9:]
    at = pl.program_id(0)
    here = lambda step: at == step
    ride(here, 0)

    @pl.when(at == 0)
    def _():
        grad_out, normed = grad_ref[...].astype(jnp.float32), fnorm_ref[...]
        vec_ref[...] = jnp.zeros_like(vec_ref)
        vec_ref[GF : GF + 1, :] = sum_rows(grad_out * normed)
        vec_ref[BF : BF + 1, :] = sum_rows(grad_out)
        grad = norm_back(grad_out, normed, fstat_ref[:, :1], v_ref[0, GF : GF + 1, :])
        vec_ref[BD : BD + 1, :] = sum_rows(grad)
        grad_f[...] = grad
        low_f[...] = grad.astype(LOW)
        mid[...] = middle_of(normed_ref, v_ref).astype(LOW)
        acc[...] = jnp.zeros_like(acc)

    act, slope = gelu_parts(up_ref[...])
    dwd_ref[...] = dot_weight(act.astype(LOW), low_f[...]).astype(LOW)
    ride(here, 1)
    grad_up = dot_back(low_f[...], wd_ref[0]) * slope
    vec_ref[pl.ds(BU + at, 1), :] = sum_rows(grad_up)
    low_up = grad_up.astype(LOW)
    dwu_ref[0] = dot_weight(mid[...], low_up).astype(LOW)
    acc[...] += dot_back(low_up, wu_ref[0, 0])
    ride(here, 2)

    @pl.when(at == count - 1)
    def _():
        grad_mid, normed = grad_f[...] + acc[...], normed_ref[...]
        vec_ref[GA : GA + 1, :] = sum_rows(grad_mid * normed)
        vec_ref[BA : BA + 1, :] = sum_rows(grad_mid)
        inv = stat_ref[:, HEADS : HEADS + 1]
        grad = norm_back(grad_mid, normed, inv, v_ref[0, GA : GA + 1, :])
        vec_ref[BO : BO + 1, :] = sum_rows(grad)
        grad_a_ref[...] = grad

    ride(here, 3)


def mlp_bwd(
    grad, fnorm, fstat, normed, stat, up, square, down, vectors, layer_at, rider=None, load=()
):
    rows, width = normed.shape
    count = down.shape[1] // width
    whole = lambda n: pl.BlockSpec((rows, n), lambda j: (0, 0))
    f32 = jnp.float32
    vec_rows = vectors.shape[1]
    in_specs = [
        whole(width),
        whole(width),
        whole(LANES),
        whole(width),
        whole(LANES),
        pl.BlockSpec((rows, width), lambda j: (0, j)),
        pl.BlockSpec((1, 1, width, width), lambda j: (layer_at, 4 + j, 0, 0)),
        pl.BlockSpec((1, width, width), lambda j: (layer_at, j, 0)),
        pl.BlockSpec((1, vec_rows, width), lambda j: (layer_at, 0, 0)),
    ]
    out_specs = [
        pl.BlockSpec((1, width, width), lambda j: (j, 0, 0)),
        pl.BlockSpec((width, width), lambda j: (j, 0)),
        whole(width),
        pl.BlockSpec((vec_rows, width), lambda j: (0, 0)),
    ]
    out_shape = [
        jax.ShapeDtypeStruct((count, width, width), LOW),
        jax.ShapeDtypeStruct((count * width, width), LOW),
        jax.ShapeDtypeStruct((rows, width), f32),
        jax.ShapeDtypeStruct((vec_rows, width), f32),
    ]
    scratch = [
        pltpu.VMEM((rows, width), LOW),
        pltpu.VMEM((rows, width), f32),
        pltpu.VMEM((rows, width), LOW),
        pltpu.VMEM((rows, width), f32),
    ]
    return pl.pallas_call(
        lambda *refs: mlp_bwd_kernel(count, rider, *refs),
        grid=(count,),
        name="mlp_bwd" if rider is None else "mlp_bwd_sums",
        **carried(rider, in_specs, out_specs, out_shape, scratch),
    )(grad, fnorm, fstat, normed, stat, up, square, down, vectors, *load)


def attn_bwd_kernel(rider, *refs):
    own, ride = aboard(refs, rider, 6, 4)
    grad_ref, qkv_ref, stat_ref, mask_ref, w_ref, vec_in = own[:6]
    dqkv_ref, grad_in_ref, low_ref, vec_ref, gctx = own[6:]
    rows, width = grad_ref.shape
    bin_at = pl.program_id(0)
    ride(lambda step: bin_at == step, 0)

    @pl.when(pl.program_id(0) == 0)
    def _():
        vec_ref[...] = vec_in[...]

    low_ref[...] = grad_ref[...].astype(LOW)
    gctx[...] = dot_back(low_ref[...], w_ref[0, 3]).astype(LOW)
    scale = HEAD_DIM ** (-0.5)
    lanes = lane_ids(rows)

    def pair_step(pair, carry):
        for part in range(HEADS // 2):
            ride(lambda step: (bin_at == step) & (pair == part), 1 + part)
        q = qkv_ref[:, pair_at(pair)]
        k = qkv_ref[:, pair_at(pair, width)]
        v = qkv_ref[:, pair_at(pair, 2 * width)]
        g = gctx[:, pair_at(pair)]
        grads = [[], [], []]
        for head in range(2):
            qh, kh, vh, gh = (lanes_of(t, head) for t in (q, k, v, g))
            log_total = jnp.sum(
                jnp.where(lanes == 2 * pair + head, stat_ref[...], 0.0), axis=-1, keepdims=True
            )
            s = dot_back(qh, kh) * scale
            s = jnp.where(mask_ref[0] > 0, s, NEG)
            p = jnp.exp(s - log_total)
            grad_p = dot_back(gh, vh)
            inner = jnp.sum(grad_p * p, axis=-1, keepdims=True)
            low_s = (p * (grad_p - inner)).astype(LOW)
            grads[0].append(dot(low_s, kh) * scale)
            grads[1].append(dot_weight(low_s, qh) * scale)
            grads[2].append(dot_weight(p.astype(LOW), gh))
        for j, row in ((0, BQ), (1, None), (2, BV)):
            both = jnp.concatenate(grads[j], axis=1)
            dqkv_ref[:, pair_at(pair, j * width)] = both.astype(LOW)
            if row is not None:
                vec_ref[row : row + 1, pair_at(pair)] += sum_rows(both)
        return carry

    lax.fori_loop(0, HEADS // 2, pair_step, 0)
    total = grad_ref[...]
    for j in range(3):
        total = total + dot_back(dqkv_ref[:, j * width : (j + 1) * width], w_ref[0, j])
    grad_in_ref[...] = total
    ride(lambda step: bin_at == step, 1 + HEADS // 2)


def attn_bwd(grad_a, qkv, stat, mask, square, vec, layer_at, rider=None, load=()):
    rows, width = grad_a.shape
    bins, block = mask.shape[:2]
    row = lambda n: pl.BlockSpec((block, n), lambda b: (b, 0))
    fixed = pl.BlockSpec(vec.shape, lambda b: (0, 0))
    f32 = jnp.float32
    in_specs = [
        row(width),
        row(3 * width),
        row(LANES),
        pl.BlockSpec((1, block, block), lambda b: (b, 0, 0)),
        pl.BlockSpec((1, 4, width, width), lambda b: (layer_at, 0, 0, 0)),
        fixed,
    ]
    out_shape = [
        jax.ShapeDtypeStruct((rows, 3 * width), LOW),
        jax.ShapeDtypeStruct((rows, width), f32),
        jax.ShapeDtypeStruct((rows, width), LOW),
        jax.ShapeDtypeStruct(vec.shape, f32),
    ]
    out_specs = [row(3 * width), row(width), row(width), fixed]
    scratch = [pltpu.VMEM((block, width), LOW)]
    return pl.pallas_call(
        lambda *refs: attn_bwd_kernel(rider, *refs),
        grid=(bins,),
        name=f"attn_bwd_sums{rider.number}",
        **carried(rider, in_specs, out_specs, out_shape, scratch),
    )(grad_a, qkv, stat, mask, square, vec, *load)


def attn_dw_kernel(act_ref, dqkv_ref, ctx_ref, low_ref, out_ref):
    at = pl.program_id(0)

    @pl.when(at < 3)
    def _():
        out_ref[0] = dot_weight(act_ref[...].astype(LOW), dqkv_ref[...]).astype(LOW)

    @pl.when(at == 3)
    def _():
        out_ref[0] = dot_weight(ctx_ref[...], low_ref[...]).astype(LOW)


def attn_dw(act, dqkv, ctx, low):
    rows, width = act.shape
    whole = pl.BlockSpec((rows, width), lambda j: (0, 0))
    return pl.pallas_call(
        attn_dw_kernel,
        grid=(4,),
        in_specs=[
            whole,
            pl.BlockSpec((rows, width), lambda j: (0, jnp.minimum(j, 2))),
            whole,
            whole,
        ],
        out_specs=pl.BlockSpec((1, width, width), lambda j: (j, 0, 0)),
        out_shape=jax.ShapeDtypeStruct((4, width, width), LOW),
        name="attn_dw",
    )(act, dqkv, ctx, low)


SMALL = ("bq", "bv", "bo", "ga", "ba", "bd", "gf", "bf", "bu")


def small_rows(p, layer_at, width):
    small = jnp.concatenate([p[name][layer_at] for name in SMALL])
    return jnp.pad(small, (0, 8 * width - small.shape[0])).reshape(8, width)


def vectors_of(all_small, rows):
    layers, width = all_small.shape[0], all_small.shape[-1]
    flat = all_small.reshape(layers, -1, 8 * width).astype(jnp.float32)
    even = flat[:, :, : 8 * rows].reshape(layers, -1, 8, rows).transpose(0, 2, 1, 3)
    up = flat[:, :, 8 * rows : 12 * rows]
    return jnp.concatenate([even.reshape(layers, 8, width), up.reshape(layers, 4, width)], axis=1)


def forward(hidden, act_in, w, mask, layer_at):
    square, down, vectors = w
    qkv, ctx, stat, normed = attn_fwd(hidden, square, vectors, mask, layer_at)
    up, out, out_low, fnorm, fstat = mlp_fwd(normed, square, down, vectors, layer_at)
    return out, out_low, (act_in, qkv, ctx, stat, normed, up, fnorm, fstat)


def backward_layers(grad, back, kept, w, mask, sizes, rows):
    square, down, vectors = w
    width = square.shape[-1]

    def of_mlp(grad, layer_at, *more):
        act_in, qkv, ctx, stat, normed, up, fnorm, fstat = kept[layer_at]
        return mlp_bwd(
            grad, fnorm, fstat, normed, stat, up, square, down, vectors, layer_at, *more
        )

    def of_attn(grad_a, vec, layer_at, *more):
        act_in, qkv, ctx, stat, *unused = kept[layer_at]
        dqkv, grad_in, low_a, vec, *sums = attn_bwd(
            grad_a, qkv, stat, mask, square, vec, layer_at, *more
        )
        return grad_in, attn_dw(act_in, dqkv, ctx, low_a), vec, sums

    blocks_out = lambda t: t.reshape((4,) + sizes + (rows, width))
    rows_out = lambda t: t.reshape(sizes + (4, rows, width))
    dwu, dwd, grad_a, vec = of_mlp(grad, 1)
    rider = Rider(sizes, rows, width, [("down", "early")], ATTN_STEPS, 2)
    grad, dws, vec_late, halves = of_attn(grad_a, vec, 1, rider, [rows_out(dwd)])
    grad, back = lax.optimization_barrier((grad, back))
    rider = Rider(sizes, rows, width, [("down", "late"), ("up", "early")], MLP_STEPS, 3)
    dwu, dwd, grad_a, vec, g_down, *halves = of_mlp(grad, 0, rider, [*halves, blocks_out(dwu)])
    rider = Rider(sizes, rows, width, [("up", "late"), ("attn", "early")], ATTN_STEPS, 4)
    grad, dws, vec, (g_up, *halves) = of_attn(grad_a, vec, 0, rider, [*halves, blocks_out(dws)])
    left = (blocks_out(dws), blocks_out(dwu), rows_out(dwd))
    return grad, back, (g_up, g_down), (halves, left, jnp.stack([vec, vec_late]))


def shift_down(rows, amount):
    doubled = jnp.concatenate([jnp.zeros_like(rows), rows], axis=0)
    return lax.dynamic_slice_in_dim(doubled, rows.shape[0] - amount, rows.shape[0], 0)


def shift_up(rows, amount):
    doubled = jnp.concatenate([rows, jnp.zeros_like(rows)], axis=0)
    return lax.dynamic_slice_in_dim(doubled, amount, rows.shape[0], 0)


def pack_bin(slots, first_len, second_len):
    positions = jnp.arange(slots.shape[1])[:, None]
    later = shift_down(jnp.where(positions < second_len, slots[1], 0), first_len)
    return jnp.where(positions < first_len, slots[0], later)


def unpack_bin(rows, first_len, second_len):
    positions = jnp.arange(rows.shape[0])[:, None]
    first = jnp.where(positions < first_len, rows, 0)
    second = jnp.where(positions < second_len, shift_up(rows, first_len), 0)
    return jnp.stack([first, second])


def per_device(tokens_in, cotangent, lengths, bin_deal, random_blocks, *weights):
    names = ("wqkv", "bq", "bv", "wo", "bo", "ga", "ba", "wu", "bu", "wd", "bd", "gf", "bf")
    p = dict(zip(names, weights))
    rows = p["wo"].shape[1]
    members = lax.axis_size("fsdp")
    member = lax.axis_index("fsdp")
    group_at = lax.axis_index("dp")
    grid = Grid(lax.axis_size("dp"), members)
    slot_count = 2 * members
    slot_ids = jnp.arange(slot_count)
    deal_here = lax.dynamic_index_in_dim(bin_deal, group_at, 1, keepdims=False)
    slot_hits = (deal_here[:, :, None] == slot_ids[None, None, :]).astype(jnp.int32)
    source_of = jnp.sum(slot_hits * slot_ids[None, :, None], axis=1)
    lengths_here = lax.dynamic_slice_in_dim(lengths, group_at * slot_count, slot_count, 1)
    bin_lengths = jnp.take_along_axis(lengths_here, source_of, axis=1)
    random_here = lax.dynamic_slice_in_dim(random_blocks, group_at * slot_count, slot_count, 1)
    batch_count, unused_slots, rows_dev, width = tokens_in.shape
    bin_len = rows_dev * members
    order_index = source_of[:, :, None, None]

    def dealt(array):
        sent = jnp.take_along_axis(array, order_index, axis=1)
        return sent.reshape(batch_count, members, 2, rows_dev, width)

    blocks = lambda w: w.reshape(LAYERS, rows, -1, width).transpose(0, 2, 1, 3)
    square = jnp.concatenate([blocks(p["wqkv"]), blocks(p["wo"]), blocks(p["wu"])], axis=1)
    down = p["wd"].reshape(LAYERS, -1, rows, width)
    small = jnp.stack([small_rows(p, layer_at, width) for layer_at in range(LAYERS)])
    sent_grad = dealt(cotangent)
    got_x, *gathered = bring(grid.sizes, dealt(tokens_in), square, down, small)
    got_x, sent_grad = lax.optimization_barrier((got_x, sent_grad))
    arrived_x = got_x.reshape(batch_count, 2, bin_len, width)
    arrived_grad = lax.all_to_all(
        sent_grad, "fsdp", split_axis=1, concat_axis=3, tiled=True
    )[:, 0]
    square, down, small = gathered
    side = rows * grid.count
    w = (
        square.reshape(LAYERS, -1, side, width),
        down.reshape(LAYERS, -1, width),
        vectors_of(small, rows),
    )
    slot_pair = lax.dynamic_slice_in_dim(bin_lengths, 2 * member, 2, 1)
    random_pair = lax.dynamic_slice_in_dim(random_here, 2 * member, 2, 1)
    allowed = jax.vmap(bin_mask)(slot_pair[:, 0], slot_pair[:, 1], random_pair)
    first_len = slot_pair[:, 0] * BLOCK
    second_len = slot_pair[:, 1] * BLOCK

    def packed(slots):
        bins = [pack_bin(slots[m], first_len[m], second_len[m]) for m in range(batch_count)]
        return jnp.concatenate(bins, axis=0)

    def to_slots(bins):
        bins = bins.reshape(batch_count, bin_len, width)
        slots = [unpack_bin(bins[m], first_len[m], second_len[m]) for m in range(batch_count)]
        return jnp.stack(slots)

    def in_order(back):
        back = back.reshape(batch_count, slot_count, rows_dev, width)
        return jnp.take_along_axis(back, deal_here[:, :, None, None], axis=1)

    mask = allowed.astype(jnp.float32)
    hidden = act_in = packed(arrived_x)
    kept = []
    for layer_at in range(LAYERS):
        hidden, act_in, stored = forward(hidden, act_in, w, mask, layer_at)
        kept.append(stored)
    sent = to_slots(act_in)[:, None]
    back = lax.all_to_all(sent, "fsdp", split_axis=3, concat_axis=1, tiled=True)
    arrived_grad, act_in = lax.optimization_barrier((arrived_grad, act_in))
    grad = packed(arrived_grad)
    grad, back, (g_up, g_down_late), left = backward_layers(grad, back, kept, w, mask, grid.sizes, rows)
    output = in_order(back)
    sent = to_slots(grad.astype(LOW)).reshape(batch_count, 2, members, rows_dev, width)
    g_qkv, g_out, g_up, g_down, g_vec, back = take_home(
        grid.sizes, *left, sent, (g_up, g_down_late)
    )
    input_grad = in_order(back)
    out = {
        "wqkv": g_qkv,
        "wo": g_out,
        "wu": g_up,
        "wd": g_down.reshape(LAYERS, -1, width),
    }
    place = group_at * members + member
    even = lax.dynamic_slice(g_vec, (0, 0, place * rows), (LAYERS, BU, rows))
    for at, name in enumerate(SMALL[:BU]):
        out[name] = even[:, at]
    parts = g_vec[:, BU:].reshape(LAYERS, -1)
    count = parts.shape[1] // grid.count
    out["bu"] = lax.dynamic_slice_in_dim(parts, place * count, count, 1)
    return (output, input_grad) + tuple(out[name] for name in names)


def solution(mesh):
    tokens = P(None, "dp", "fsdp", None)
    matrix = P(None, AXES, None)
    vector = P(None, AXES)
    weights = (matrix, vector, vector, matrix, vector, vector, vector)
    weights += (matrix, vector, matrix, vector, vector, vector)
    return jax.shard_map(
        per_device,
        mesh=mesh,
        in_specs=(tokens, tokens, P(), P(), P()) + weights,
        out_specs=(tokens, tokens) + weights,
        check_vma=False,
    )
```
